32 devices in a mesh: dp: 8 (over z, x), tensor: 4 (over y, core).
Axes of the slice: x: 2, y: 2, z: 4, core: 2. Of those that a mesh axis runs over, the one named last changes fastest.
Arguments:
- tokens: bfloat16 [2, 8192, 768], P(None, ('dp', 'tensor')), may hold values from -6 to 6
- qkv_weight: bfloat16 [768, 3, 768], P(None, None, 'tensor'), may hold values from -0.21875 to 0.21875
- qv_bias: bfloat16 [2, 768], P(None, 'tensor'), may hold values from -2 to 2
- out_weight: bfloat16 [768, 768], P('tensor'), may hold values from -1.75 to 1.75
- out_bias: bfloat16 [768], replicated, may hold values from -2 to 2
- ln1_gain: bfloat16 [768], replicated, may hold values from 0.5 to 1.5
- ln1_shift: bfloat16 [768], replicated, may hold values from -2 to 2
- fc_weight: bfloat16 [768, 3072], P(None, 'tensor'), may hold values from -0.21875 to 0.21875
- fc_bias: bfloat16 [3072], P('tensor'), may hold values from -2 to 2
- proj_weight: bfloat16 [3072, 768], P('tensor'), may hold values from -0.109375 to 0.109375
- proj_bias: bfloat16 [768], replicated, may hold values from -2 to 2
- ln2_gain: bfloat16 [768], replicated, may hold values from 0.5 to 1.5
- ln2_shift: bfloat16 [768], replicated, may hold values from -2 to 2
- seq_lengths: int32 [2, 8], P(None, 'dp'), may hold values from 512 to 1024, as said below
- out_grad: bfloat16 [2, 8192, 768], P(None, ('dp', 'tensor')), may hold values from -6 to 6
Outputs:
- layer_out: bfloat16 [2, 8192, 768], P(None, ('dp', 'tensor'))
- input_grad: float32 [2, 8192, 768], P(None, ('dp', 'tensor'))
- qkv_weight_grad: float32 [768, 3, 768], P(None, None, 'tensor')
- qv_bias_grad: float32 [2, 768], P(None, 'tensor')
- out_weight_grad: float32 [768, 768], P('tensor')
- out_bias_grad: float32 [768], replicated
- ln1_gain_grad: float32 [768], replicated
- ln1_shift_grad: float32 [768], replicated
- fc_weight_grad: float32 [768, 3072], P(None, 'tensor')
- fc_bias_grad: float32 [3072], P('tensor')
- proj_weight_grad: float32 [3072, 768], P('tensor')
- proj_bias_grad: float32 [768], replicated
- ln2_gain_grad: float32 [768], replicated
- ln2_shift_grad: float32 [768], replicated
The draws below stay inside these ranges and needn't reach their ends.
Inputs may be any that keep to these rules, and one draw needn't show every extreme that they name: `seq_lengths`: each slot's sequence has 512 to 1024 positions; in every draw some slot is exactly 1024 long and some exactly 512.
All inputs are finite; a program needn't handle non-finite values.
Results may differ from the reference program's by a relative error of at most 0.014.
Values may be sent and summed in bfloat16 or wider, within the bound.
No kernel may reach another device: no remote copies, remote signals or barrier semaphores. Data moves between devices by JAX's collectives and lax.ppermute only.
A program may use at most 128 MiB of HBM per device.

```python
import jax
import jax.numpy as jnp
from jax import lax

D = 768
HEADS = 12
HD = 64
FF = 3072
SLOT = 1024
MB = 2
SEQ_ROWS = 8192
SLOTS = 16
N_DP = 8


def draw_seq_lengths(key, part):
    base = jax.random.randint(jax.random.fold_in(key, 11), (SLOTS,), SLOT // 2, SLOT + 1)
    order = jax.random.permutation(jax.random.fold_in(key, 12), SLOTS)
    places = jnp.arange(SLOTS)
    base = jnp.where(places == order[0], SLOT, base)
    base = jnp.where(places == order[1], SLOT // 2, base)
    return base.reshape(MB, SLOTS // MB).astype(jnp.int32)


def block_levels(key, extent, split, smallest, top_value):
    loudness = 1.0
    for axis_at, blocks in split:
        steps = jax.random.uniform(jax.random.fold_in(jax.random.fold_in(key, 6), axis_at), (blocks,), jnp.float32, smallest / len(split), top_value / len(split))
        loudness = loudness * jnp.repeat(jnp.exp(steps), extent[axis_at] // blocks).reshape((-1,) + (1,) * (len(extent) - 1 - axis_at))
    return loudness


def normal_values(stream_key, extent, scale, limit, shards=(), dtype=jnp.bfloat16):
    values = jax.random.normal(stream_key, extent, jnp.float32) * scale
    if len(shards) > 0:
        values = block_levels(stream_key, extent, shards, -0.22, 0.18) * values
    return jnp.clip(values, min=-limit, max=limit).astype(dtype)


def setup_inputs(seed: int = 0) -> dict:
    key_list = jax.random.split(jax.random.key(seed), 16)
    tokens = normal_values(key_list[0], (MB, SEQ_ROWS, D), 1.0, 6.0, ((1, 32),))
    qkv_weight = normal_values(key_list[1], (D, 3, D), D ** -0.5, 0.21875, ((2, 4),))
    qv_bias = normal_values(key_list[2], (2, D), 0.3, 2.0, ((1, 4),))
    out_weight = normal_values(key_list[3], (D, D), (D * 16 // SLOT) ** -0.5, 1.75, ((0, 4),))
    out_bias = normal_values(key_list[4], (D,), 0.3, 2.0)
    ln1_gain = jnp.clip(1.0 + 0.1 * jax.random.normal(key_list[5], (D,), jnp.float32), 0.5, 1.5).astype(jnp.bfloat16)
    ln1_shift = normal_values(key_list[6], (D,), 0.3, 2.0)
    fc_weight = normal_values(key_list[7], (D, FF), D ** -0.5, 0.21875, ((1, 4),))
    fc_bias = normal_values(key_list[8], (FF,), 0.3, 2.0, ((0, 4),))
    proj_weight = normal_values(key_list[9], (FF, D), FF ** -0.5, 0.109375, ((0, 4),))
    proj_bias = normal_values(key_list[10], (D,), 0.3, 2.0)
    ln2_gain = jnp.clip(1.0 + 0.1 * jax.random.normal(key_list[11], (D,), jnp.float32), 0.5, 1.5).astype(jnp.bfloat16)
    ln2_shift = normal_values(key_list[12], (D,), 0.3, 2.0)
    seq_lengths = draw_seq_lengths(jax.random.fold_in(key_list[15], 71), 0)
    out_grad = normal_values(key_list[14], (MB, SEQ_ROWS, D), 1.0, 6.0, ((1, 32),))
    return {"tokens": tokens, "qkv_weight": qkv_weight, "qv_bias": qv_bias, "out_weight": out_weight, "out_bias": out_bias, "ln1_gain": ln1_gain, "ln1_shift": ln1_shift, "fc_weight": fc_weight, "fc_bias": fc_bias, "proj_weight": proj_weight, "proj_bias": proj_bias, "ln2_gain": ln2_gain, "ln2_shift": ln2_shift, "seq_lengths": seq_lengths, "out_grad": out_grad}


@jax.custom_vjp
def low(v):
    return lax.optimization_barrier(v.astype(jnp.bfloat16)).astype(jnp.float32)

@jax.custom_vjp
def low_back(v):
    return v

def low_keep(v):
    return (low(v), None)

def low_pass(kept, grad):
    return (grad,)

def back_keep(v):
    return (v, None)

def back_low(kept, grad):
    return (low(grad),)
low.defvjp(low_keep, low_pass)
low_back.defvjp(back_keep, back_low)

def layer_norm(values, gain, shift):
    average = lax.optimization_barrier(jnp.mean(values, axis=-1, keepdims=True))
    centered = values - average
    variance = lax.optimization_barrier(jnp.mean(centered * centered, axis=-1, keepdims=True))
    return centered * lax.rsqrt(variance + 1e-05) * gain + shift

def matmul(left, right):
    return jnp.dot(left, right, precision=lax.Precision.HIGHEST)

def slot_attention(packed, length):
    queries = packed[:, 0]
    key_rows = packed[:, 1]
    value_rows = packed[:, 2]
    scores = jnp.einsum('qhd,khd->hqk', queries, key_rows, precision=lax.Precision.HIGHEST) * HD ** (-0.5)
    scores = low_back(scores)
    position = jnp.arange(SLOT)
    key_valid = position < length
    scores = jnp.where(key_valid[None, None, :], scores, -1e+30)
    row_max = lax.optimization_barrier(jnp.max(scores, axis=-1, keepdims=True))
    expanded = jnp.exp(scores - row_max)
    weights = expanded / lax.optimization_barrier(jnp.sum(expanded, axis=-1, keepdims=True))
    mixed = jnp.einsum('hqk,khd->qhd', low(weights), value_rows, precision=lax.Precision.HIGHEST)
    mixed = jnp.where(key_valid[:, None, None], mixed, 0.0)
    return mixed.reshape(SLOT, D)

def attend_slot(packed_pair):
    return jax.checkpoint(slot_attention)(packed_pair[0], packed_pair[1])

def forward(params, seq_lengths):
    tokens, qkv_weight, qv_bias, out_weight, out_bias, ln1_gain, ln1_shift, fc_weight, fc_bias, proj_weight, proj_bias, ln2_gain, ln2_shift = params
    inputs = tokens.reshape(MB * SEQ_ROWS, D)
    normed = low(layer_norm(inputs, ln1_gain, ln1_shift))
    bias_full = jnp.concatenate([qv_bias[0], jnp.zeros_like(qv_bias[0]), qv_bias[1]])
    packed = low(low_back(matmul(normed, qkv_weight.reshape(D, 3 * D)) + bias_full))
    slots = packed.reshape(MB * N_DP, SLOT, 3, HEADS, HD)
    mixed = lax.map(attend_slot, (slots, seq_lengths.reshape(MB * N_DP)))
    mixed = low(low_back(mixed.reshape(MB * SEQ_ROWS, D)))
    hidden = inputs + low_back(matmul(mixed, out_weight) + out_bias)
    normed_two = low(layer_norm(hidden, ln2_gain, ln2_shift))
    gate = low_back(matmul(normed_two, fc_weight) + fc_bias)
    active = low(gate * jax.nn.sigmoid(1.702 * gate))
    result = hidden + low_back(matmul(active, proj_weight) + proj_bias)
    return result.reshape(MB, SEQ_ROWS, D)

def reference(tokens, qkv_weight, qv_bias, out_weight, out_bias, ln1_gain, ln1_shift, fc_weight, fc_bias, proj_weight, proj_bias, ln2_gain, ln2_shift, seq_lengths, out_grad):
    floats = tuple((entry_array.astype(jnp.float32) for entry_array in (tokens, qkv_weight, qv_bias, out_weight, out_bias, ln1_gain, ln1_shift, fc_weight, fc_bias, proj_weight, proj_bias, ln2_gain, ln2_shift)))
    layer_value, pullback = jax.vjp(lambda params: forward(params, seq_lengths), floats)
    grads = pullback(out_grad.astype(jnp.float32))[0]
    return (layer_value.astype(jnp.bfloat16), grads[0], grads[1], grads[2], grads[3], grads[4], grads[5], grads[6], grads[7], grads[8], grads[9], grads[10], grads[11], grads[12])
```

```python
import math

import jax
import jax.numpy as jnp
from jax import lax
from jax.experimental import pallas as pl
from jax.experimental.pallas import tpu as pltpu
from jax.sharding import PartitionSpec as P

HD = 64
LANES = 128
LOG2E = 1.4426950408889634
NEG = -1e30
EPS = 1e-05
BF = jnp.bfloat16
F32 = jnp.float32
VM = pl.BlockSpec(memory_space=pltpu.VMEM)
SM = pl.BlockSpec(memory_space=pltpu.SMEM)
HB = pl.BlockSpec(memory_space=pltpu.HBM)


def dg(a, b, ca, cb):
    return lax.dot_general(a, b, (((ca,), (cb,)), ((), ())), preferred_element_type=F32)


def sds(shape, dtype):
    return jax.ShapeDtypeStruct(tuple(shape), dtype)


class Line:
    def __init__(self):
        self.last = None

    def __call__(self, kernel, name, args, outs, n_smem=0, scratch=(), limit=24, far=0, needs=()):
        args = list(args)
        after = list(needs)
        if self.last is not None:
            after.append(self.last)
        if after:
            args[-1] = lax.optimization_barrier(tuple([args[-1]] + after))[0]
        for i in range(n_smem, n_smem + far):
            args[i] = pltpu.with_memory_space_constraint(args[i], pltpu.HBM)
        fetched = args[n_smem : n_smem + far]
        total = len(args)

        def run(*refs):
            if not far:
                return kernel(*refs)
            body_refs = refs[: len(refs) - far - 1]
            bufs = refs[len(refs) - far - 1 : -1]
            sems = refs[-1]
            copies = [
                pltpu.make_async_copy(refs[n_smem + i], bufs[i], sems.at[i]) for i in range(far)
            ]
            for cp in copies:
                cp.start()
            for cp in copies:
                cp.wait()
            return kernel(*body_refs[:n_smem], *bufs, *body_refs[n_smem + far :])

        extra = []
        if far:
            extra = [pltpu.VMEM(v.shape, v.dtype) for v in fetched] + [pltpu.SemaphoreType.DMA((far,))]
        res = pl.pallas_call(
            run,
            in_specs=[SM] * n_smem + [HB] * far + [VM] * (total - n_smem - far),
            out_specs=[VM] * len(outs),
            out_shape=outs,
            scratch_shapes=list(scratch) + extra,
            compiler_params=pltpu.CompilerParams(vmem_limit_bytes=limit << 20),
            cost_estimate=pl.CostEstimate(flops=1, transcendentals=0, bytes_accessed=1),
            name=name,
        )(*args)
        self.last = res[-1]
        return res


def normalize(x):
    d = x.shape[-1]
    xc = x - jnp.sum(x, axis=-1, keepdims=True) * (1.0 / d)
    var = jnp.sum(xc * xc, axis=-1, keepdims=True) * (1.0 / d)
    r = lax.rsqrt(var + EPS)
    return xc * r, r


def norm_back(grad, z, r, gain):
    d = z.shape[-1]
    e = grad * gain
    me = jnp.sum(e, axis=-1, keepdims=True) * (1.0 / d)
    mez = jnp.sum(e * z, axis=-1, keepdims=True) * (1.0 / d)
    return (e - me - z * mez) * r


def col_sum(x):
    return jnp.sum(x.astype(F32), axis=0, keepdims=True)


def ln1_kernel(*refs):
    vecs = refs[:6]
    fb_ref, qb_ref, tok_ref = refs[6:9]
    outs = refs[9:-2]
    small_ref, vec_ref = refs[-2:]
    vec_ref[...] = jnp.zeros(vec_ref.shape, F32)
    for i, v in enumerate(vecs):
        vec_ref[i : i + 1, :] = v[...].astype(F32).reshape(1, -1)
    for m, o_ref in enumerate(outs):
        z, _ = normalize(tok_ref[m].astype(F32))
        o_ref[...] = (z * vec_ref[1:2] + vec_ref[2:3]).astype(BF)
    small_ref[...] = jnp.zeros(small_ref.shape, F32)
    small_ref[0:1, : fb_ref.shape[0]] = fb_ref[...].astype(F32).reshape(1, -1)
    small_ref[1:3, : qb_ref.shape[1]] = qb_ref[...].astype(F32)


def weights_kernel(woo_ref, wqo_ref, so_ref, sx_ref, wox_ref, wqx_ref, qb_ref, fb_ref, wo_ref, wq_ref):
    c = lax.axis_index("tensor") & 1
    hc = woo_ref.shape[0]
    units = fb_ref.shape[1]
    fb_ref[0:1, :] = so_ref[0:1, :units]
    fb_ref[1:2, :] = sx_ref[0:1, :units]
    qb_ref[...] = jnp.zeros(qb_ref.shape, F32)

    def place(at_o, at_x):
        for at, b, o, q in ((at_o, so_ref, woo_ref, wqo_ref), (at_x, sx_ref, wox_ref, wqx_ref)):
            qb_ref[0:1, at : at + hc] = b[1:2, :hc]
            qb_ref[2:3, at : at + hc] = b[2:3, :hc]
            wo_ref[at : at + hc, :] = o[...]
            wq_ref[:, at : at + hc, :] = q[...]

    @pl.when(c == 0)
    def _():
        place(0, hc)

    @pl.when(c != 0)
    def _():
        place(hc, 0)


def qkv_kernel(b_ref, w_ref, no_ref, np_ref, qo_ref, qp_ref, kv_ref):
    rows, wide = qo_ref.shape
    for i, (n_ref, q_ref) in enumerate(((no_ref, qo_ref), (np_ref, qp_ref))):
        n = n_ref[...]
        for s in range(3):
            v = (dg(n, w_ref[s], 1, 1) + b_ref[s : s + 1]).astype(BF)
            if s == 0:
                q_ref[...] = v
            else:
                kv_ref[i * rows : (i + 1) * rows, wide * (s - 1) : wide * s] = v


def row_starts(rows):
    t = lax.axis_index("tensor")
    return [rows * t, rows * (t ^ 2), rows * (t ^ 1), rows * (t ^ 3)]


def key_bias(starts, length, rows):
    out = []
    for b in range(4):
        at = lax.broadcasted_iota(jnp.int32, (rows, LANES), 0) + starts[b]
        out.append(jnp.where(at < length, 0.0, NEG).astype(BF))
    return jnp.concatenate(out, axis=0)


def attend_kernel(m, part, len_ref, ka_ref, kb_ref, w_ref, q_ref, mixed_ref, lse_ref, term_ref):
    rows, wide = q_ref.shape
    length = len_ref[m, 0]
    starts = row_starts(rows)
    c = LOG2E / math.sqrt(HD)
    bias = key_bias(starts, length, rows)
    lane = lax.broadcasted_iota(jnp.int32, (4 * rows, LANES), 1)
    laneq = lax.broadcasted_iota(jnp.int32, (rows, LANES), 1)
    valid = lax.broadcasted_iota(jnp.int32, (rows, LANES), 0) + starts[part] < length
    kvs = (ka_ref, kb_ref)

    def pair(p, carry):
        cs = pl.ds(pl.multiple_of(LANES * p, LANES), LANES)
        vs = pl.ds(pl.multiple_of(wide + LANES * p, LANES), LANES)
        kp = jnp.concatenate([r[:, cs] for r in kvs], axis=0)
        vp = jnp.concatenate([r[:, vs] for r in kvs], axis=0)
        qp = q_ref[:, cs]
        os = []
        ls = []
        for h in range(2):
            inh = (laneq < HD) if h == 0 else (laneq >= HD)
            mark = HD * (1 - h)
            one = jnp.where(laneq == mark, 1.0, 0.0).astype(BF)
            s = dg(jnp.where(inh, qp, one), jnp.where(lane == mark, bias, kp), 1, 1)
            top = jnp.max(s, axis=1, keepdims=True)
            e = jnp.exp2((s - top) * c)
            l = jnp.sum(e, axis=1, keepdims=True)
            os.append(dg(e.astype(BF), vp, 1, 0) * (1.0 / l))
            ls.append(top * c + jnp.log2(l))
        ob = jnp.where(laneq < HD, os[0], os[1])
        lt = jnp.where(laneq < HD, ls[0], ls[1]).T
        lse_ref[pl.ds(8 * p, 1), :] = lt[0:1]
        lse_ref[pl.ds(8 * p + 1, 1), :] = lt[HD : HD + 1]
        mixed_ref[:, cs] = jnp.where(valid, ob, 0.0).astype(BF)
        return carry

    lax.fori_loop(0, wide // LANES, pair, 0)
    term_ref[...] = dg(mixed_ref[...], w_ref[...], 1, 0).astype(term_ref.dtype)


def mid_kernel(m, own_ref, rcv_ref, vec_ref, tok_ref, hid_ref, n_ref):
    h = tok_ref[m].astype(F32) + (own_ref[...] + rcv_ref[...].astype(F32)) + vec_ref[0:1]
    hid_ref[...] = h
    z, _ = normalize(h)
    n_ref[...] = (z * vec_ref[4:5] + vec_ref[5:6]).astype(BF)


def mlp_kernel(m, g_ref, fo_ref, fx_ref, bias_ref, po_ref, px_ref, n_ref, ao_ref, ax_ref, ggo_ref, ggx_ref, sum_ref, term_ref):
    n = n_ref[...]
    g = g_ref[m]
    back = None
    for j, (f_ref, p_ref, a_ref, gg_ref) in enumerate(
        ((fo_ref, po_ref, ao_ref, ggo_ref), (fx_ref, px_ref, ax_ref, ggx_ref))
    ):
        f = f_ref[...]
        gate = dg(n, f, 1, 0) + bias_ref[j : j + 1]
        q = 0.5 * jnp.tanh(0.851 * gate) + 0.5
        a_ref[...] = (gate * q).astype(BF)
        slope = q + 1.702 * gate * q * (1.0 - q)
        gg = (dg(g, p_ref[...], 1, 1) * slope).astype(BF)
        gg_ref[...] = gg
        term = dg(gg, f, 1, 1)
        back = term if back is None else back + term
        sum_ref[j : j + 1] = col_sum(gg)
    term_ref[...] = back.astype(term_ref.dtype)


def proj_kernel(count, po_ref, px_ref, *refs):
    out_ref = refs[-1]
    for m in range(count):
        out_ref[m] = (dg(refs[2 * m][...], po_ref[...], 1, 0) + dg(refs[2 * m + 1][...], px_ref[...], 1, 0)).astype(
            out_ref.dtype
        )


def ln2_back_kernel(m, hid_ref, own_ref, rcv_ref, vec_ref, grad_ref, hg_ref, st_ref, br_ref):
    z, r = normalize(hid_ref[...])
    ng = own_ref[...] + rcv_ref[...].astype(F32)
    g = grad_ref[m].astype(F32)
    hg = g + norm_back(ng, z, r, vec_ref[4:5])
    hg_ref[...] = hg
    br = hg.astype(BF)
    br_ref[...] = br
    st_ref[...] = jnp.zeros(st_ref.shape, F32)
    st_ref[2:3] = col_sum(ng * z)
    st_ref[3:4] = col_sum(ng)
    st_ref[4:5] = col_sum(br)
    st_ref[5:6] = col_sum(g)


def attend_back_kernel(m, part, *refs):
    len_ref, ka_ref, kb_ref, w_ref, mixed_ref, lse_ref, b_ref = refs[:7]
    refs = refs[7:]
    if part:
        (acc_in, q_ref, dq_ref, out_ref, send_ref, do_ref) = refs
    else:
        (q_ref, dq_ref, acc_ref, do_ref) = refs
    rows, wide = q_ref.shape
    length = len_ref[m, 0]
    starts = row_starts(rows)
    c = LOG2E / math.sqrt(HD)
    sc = 1.0 / math.sqrt(HD)
    at = lax.broadcasted_iota(jnp.int32, (rows, wide), 0) + starts[part]
    do_ref[...] = jnp.where(at < length, dg(b_ref[...], w_ref[...], 1, 1), 0.0).astype(BF)
    bias = key_bias(starts, length, rows)
    lane = lax.broadcasted_iota(jnp.int32, (4 * rows, LANES), 1)
    laneq = lax.broadcasted_iota(jnp.int32, (rows, LANES), 1)
    zero = jnp.zeros((), BF)
    kvs = (ka_ref, kb_ref)

    def pair(p, carry):
        cs = pl.ds(pl.multiple_of(LANES * p, LANES), LANES)
        vs = pl.ds(pl.multiple_of(wide + LANES * p, LANES), LANES)
        kp = jnp.concatenate([r[:, cs] for r in kvs], axis=0)
        vp = jnp.concatenate([r[:, vs] for r in kvs], axis=0)
        kt = kp.T
        qp = q_ref[:, cs]
        dop = do_ref[:, cs]
        prod = (dop.astype(F32) * mixed_ref[:, cs].astype(F32)).T
        dqt = []
        dk = None
        dv = None
        for h in range(2):
            inh = (laneq < HD) if h == 0 else (laneq >= HD)
            mark = HD * (1 - h)
            qz = jnp.where(inh, qp, zero)
            qh = jnp.where(laneq == mark, jnp.ones((), BF), qz)
            doh = jnp.where(inh, dop, zero)
            st = dg(jnp.where(lane == mark, bias, kp), qh, 1, 1)
            pt = jnp.exp2(st * c - lse_ref[pl.ds(8 * p + h, 1), :])
            dpt = dg(vp, doh, 1, 1)
            row = jnp.sum(prod[HD * h : HD * (h + 1)], axis=0, keepdims=True)
            ds = (pt * (dpt - row)).astype(BF)
            dvh = dg(pt.astype(BF), doh, 1, 0)
            dkh = dg(ds, qz, 1, 0)
            dqt.append(dg(kt[HD * h : HD * (h + 1)], ds, 1, 0))
            dv = dvh if dv is None else dv + dvh
            dk = dkh if dk is None else dk + dkh
        dq_ref[:, cs] = (jnp.concatenate(dqt, axis=0).T * sc).astype(BF)
        dk = dk * sc
        if part:
            dk = dk + acc_in[:, cs]
            dv = dv + acc_in[:, vs]
            out_ref[:, cs] = dk[: 2 * rows]
            out_ref[:, vs] = dv[: 2 * rows]
            send_ref[:, cs] = dk[2 * rows :].astype(BF)
            send_ref[:, vs] = dv[2 * rows :].astype(BF)
        else:
            acc_ref[:, cs] = dk
            acc_ref[:, vs] = dv
        return carry

    lax.fori_loop(0, wide // LANES, pair, 0)


def qkv_back_kernel(dqo_ref, dqp_ref, own_ref, w_ref, rcv_ref, dkv_ref, ngo_ref, sum_ref, ngr_ref):
    rows = ngo_ref.shape[0]
    wide = dqo_ref.shape[1]
    sq = None
    sv = None
    for i, dq_ref, o_ref in ((1, dqp_ref, ngr_ref), (0, dqo_ref, ngo_ref)):
        at = slice(i * rows, (i + 1) * rows)
        dkv = (own_ref[at, :] + rcv_ref[at, :].astype(F32)).astype(BF)
        dkv_ref[at, :] = dkv
        dq = dq_ref[...]
        ng = dg(dq, w_ref[0], 1, 0) + dg(dkv[:, :wide], w_ref[1], 1, 0) + dg(dkv[:, wide:], w_ref[2], 1, 0)
        o_ref[...] = ng.astype(o_ref.dtype)
        cq = col_sum(dq)
        cv = col_sum(dkv[:, wide:])
        sq = cq if sq is None else sq + cq
        sv = cv if sv is None else sv + cv
    sum_ref[0:1] = sq
    sum_ref[1:2] = sv


def ln1_back_kernel(count, *refs):
    tok_ref = refs[0]
    vec_ref = refs[1]
    hgs = refs[2 : 2 + count]
    owns = refs[2 + count : 2 + 2 * count]
    rcvs = refs[2 + 2 * count : 2 + 3 * count]
    ig_ref, st_ref = refs[2 + 3 * count :]
    g = None
    s = None
    for m in range(count):
        z, r = normalize(tok_ref[m].astype(F32))
        ng = owns[m][...] + rcvs[m][...].astype(F32)
        ig_ref[m] = hgs[m][...] + norm_back(ng, z, r, vec_ref[1:2])
        gm = col_sum(ng * z)
        sm = col_sum(ng)
        g = gm if g is None else g + gm
        s = sm if s is None else s + sm
    st_ref[...] = jnp.zeros(st_ref.shape, F32)
    st_ref[0:1] = g
    st_ref[1:2] = s


def out_kernel(count, vec_ref, *refs):
    hids = refs[:count]
    own_ref, rcv_ref, o_ref = refs[count:]
    for m in range(count):
        o_ref[m] = (hids[m][...] + (own_ref[m] + rcv_ref[m].astype(F32)) + vec_ref[3:4]).astype(BF)


def rows_product(pairs):
    acc = None
    for a, b in pairs:
        t = dg(a, b, 0, 0)
        acc = t if acc is None else acc + t
    return acc


def mlp_weights_kernel(count, *refs):
    n = 2 * count
    acts = refs[:n]
    gates = refs[n : 2 * n]
    norms = refs[2 * n : 3 * n]
    go_ref, gp_ref, pj_ref, fc_ref = refs[3 * n :]
    gs = []
    for m in range(count):
        gs += [go_ref[m], gp_ref[m]]
    pj_ref[...] = rows_product([(a[...], g) for a, g in zip(acts, gs)]).astype(pj_ref.dtype)
    fc_ref[...] = rows_product([(a[...], b[...]) for a, b in zip(norms, gates)]).astype(fc_ref.dtype)


def attend_weights_kernel(count, *refs):
    n = 2 * count
    dqs = refs[:n]
    norms = refs[n : 2 * n]
    mixes = refs[2 * n : 3 * n]
    brs = refs[3 * n : 4 * n]
    dkvs = refs[4 * n : 4 * n + count]
    outs = refs[4 * n + count :]
    c = lax.axis_index("tensor") & 1
    rows, wide = dqs[0].shape
    hc = wide // 2
    ns = [r[...] for r in norms]
    full = [jnp.concatenate(ns[2 * m : 2 * m + 2], axis=0) for m in range(count)]
    pieces = [
        rows_product([(a[...], b) for a, b in zip(dqs, ns)]),
        rows_product([(a[:, :wide], b) for a, b in zip(dkvs, full)]),
        rows_product([(a[:, wide:], b) for a, b in zip(dkvs, full)]),
        rows_product([(a[...], b[...]) for a, b in zip(mixes, brs)]),
    ]
    for i, p in enumerate(pieces):
        own_ref, send_ref = outs[2 * (i // 2) : 2 * (i // 2) + 2]
        at = slice((i % 2) * hc, (i % 2 + 1) * hc)
        low = p[:hc]
        high = p[hc:]
        own_ref[at, :] = jnp.where(c == 0, low, high)
        send_ref[at, :] = jnp.where(c == 0, high, low).astype(BF)


def add_kernel(rcv_ref, own_ref, out_ref):
    out_ref[...] = (own_ref[...].astype(F32) + rcv_ref[...].astype(F32)).astype(out_ref.dtype)


def halve_kernel(bit, rcv_ref, own_ref, keep_ref, send_ref):
    r = keep_ref.shape[0]
    b = (lax.axis_index("dp") >> bit) & 1
    mine = pl.ds(pl.multiple_of(b * r, r), r)
    other = pl.ds(pl.multiple_of((1 - b) * r, r), r)
    send_ref[...] = (own_ref[other, :].astype(F32) + rcv_ref[other, :].astype(F32)).astype(BF)
    keep_ref[...] = own_ref[mine, :].astype(F32) + rcv_ref[mine, :].astype(F32)


def join_kernel(bit, rcv_ref, own_ref, out_ref):
    r = own_ref.shape[0]
    b = (lax.axis_index("dp") >> bit) & 1
    out_ref[pl.ds(pl.multiple_of(b * r, r), r), :] = own_ref[...].astype(out_ref.dtype)
    out_ref[pl.ds(pl.multiple_of((1 - b) * r, r), r), :] = rcv_ref[...].astype(out_ref.dtype)


def stats_kernel(count, *refs):
    lst2 = refs[:count]
    fsums = refs[count : 3 * count]
    qsums = refs[3 * count : 4 * count]
    lst1_ref, own_ref, send_ref = refs[4 * count :]
    c = lax.axis_index("tensor") & 1
    common = lst1_ref[...]
    for r in lst2:
        common = common + r[...]
    f = fsums[0][...]
    for r in fsums[1:]:
        f = f + r[...]
    q = qsums[0][...]
    for r in qsums[1:]:
        q = q + r[...]
    wide = own_ref.shape[1]
    hc = q.shape[1] // 2
    qpad = jnp.zeros((1, wide - 2 * hc), F32)
    low = jnp.concatenate([q[0:1, :hc], q[1:2, :hc], qpad], axis=1)
    high = jnp.concatenate([q[0:1, hc:], q[1:2, hc:], qpad], axis=1)
    own_ref[...] = common
    send_ref[...] = common
    own_ref[6:7] = jnp.where(c == 0, low, high)
    send_ref[6:7] = jnp.where(c == 0, high, low)
    own_ref[7:8] = f[0:1]
    send_ref[7:8] = f[1:2]


def across_kernel(rcv_ref, own_ref, out_ref):
    at = lax.broadcasted_iota(jnp.int32, own_ref.shape, 0)
    out_ref[...] = own_ref[...] + jnp.where(at < 6, rcv_ref[...], 0.0)


def body(
    tokens, qkv_weight, qv_bias, out_weight, out_bias, ln1_gain, ln1_shift, fc_weight, fc_bias,
    proj_weight, proj_bias, ln2_gain, ln2_shift, seq_lengths, out_grad,
):
    batches, rows, width = tokens.shape
    hc = out_weight.shape[0]
    wide = 2 * hc
    units = fc_weight.shape[1]
    tsize = lax.axis_size("tensor")
    dsize = lax.axis_size("dp")
    bits = dsize.bit_length() - 1
    cpairs = [(i, i ^ 1) for i in range(tsize)]
    ypairs = [(i, i ^ 2) for i in range(tsize)]
    mb = range(batches)
    line = Line()

    def core(v):
        return lax.ppermute(v, "tensor", cpairs)

    def across(v):
        return lax.ppermute(v, "tensor", ypairs)

    def swap(v, b):
        return lax.ppermute(v, "dp", [(i, i ^ (1 << b)) for i in range(dsize)])

    def after(v, *deps):
        return lax.optimization_barrier((v,) + deps)[0]

    def kernel_of(f, *static):
        def kernel(*refs):
            f(*static, *refs)

        return kernel

    def halve(own, rcv, b, name, **kw):
        size = own.shape[0] // 2
        if size % 16:
            both = own.astype(F32) + rcv.astype(F32)
            both = both.reshape((2, size) + own.shape[1:])
            bit = (lax.axis_index("dp") >> b) & 1
            keep = lax.dynamic_index_in_dim(both, bit, 0, keepdims=False)
            return keep, lax.dynamic_index_in_dim(both, 1 - bit, 0, keepdims=False).astype(BF)
        shape = (size,) + own.shape[1:]
        return line(kernel_of(halve_kernel, b), "halve" + name, [rcv, own], [sds(shape, F32), sds(shape, BF)], **kw)

    def join(piece, rcv, b, dtype, name):
        size = piece.shape[0]
        if size % 16:
            low = ((lax.axis_index("dp") >> b) & 1) == 0
            return jnp.concatenate([jnp.where(low, piece, rcv), jnp.where(low, rcv, piece)], axis=0).astype(dtype)
        shape = (2 * size,) + piece.shape[1:]
        return line(kernel_of(join_kernel, b), "join" + name, [rcv, piece], [sds(shape, dtype)])[0]

    class Sum:
        def __init__(self, own, rcv, name, turn=0):
            self.own, self.rcv, self.name, self.at = own, rcv, name, 0
            self.order = [(b + turn) % bits for b in range(bits)]

        def go(self, **kw):
            k = self.at
            self.at += 1
            if k > 2 * bits:
                return
            if k < bits:
                self.own, send = halve(self.own, self.rcv, self.order[k], self.name, **kw)
            elif k == bits:
                send = line(add_kernel, "last" + self.name, [self.rcv, self.own], [sds(self.own.shape, BF)], **kw)[0]
                self.own = send
            else:
                b = self.order[2 * bits - k]
                send = join(self.own, self.rcv, b, F32 if k == 2 * bits else BF, self.name)
                self.own = send
            if k < 2 * bits:
                self.rcv = swap(send, self.order[k if k < bits else 2 * bits - 1 - k])

        def finish(self):
            while self.at <= 2 * bits:
                self.go()
            return self.own

    wq_o = jnp.transpose(qkv_weight, (1, 2, 0))
    wq_x = core(wq_o)
    wo_x = core(out_weight)

    packed = (8, max(units, width))
    *normed, small, vec = line(
        ln1_kernel, "ln1",
        [out_bias, ln1_gain, ln1_shift, proj_bias, ln2_gain, ln2_shift, fc_bias, qv_bias, tokens],
        [sds((rows, width), BF)] * batches + [sds(packed, F32), sds((8, width), F32)], far=9,
    )
    normed_p = [across(v) for v in normed]
    qb, fb, wo, wq = line(
        weights_kernel, "weights", [out_weight, wq_o, small, core(small), wo_x, wq_x],
        [sds((3, wide), F32), sds((2, units), F32), sds((wide, width), BF), sds((3, wide, width), BF)], far=2,
    )

    q = [[None, None] for _ in mb]
    kv = [[None, None] for _ in mb]

    def qkv(m, **kw):
        q[m][0], q[m][1], kv[m][0] = line(
            qkv_kernel, "qkv", [qb, wq, normed[m], normed_p[m]],
            [sds((rows, wide), BF)] * 2 + [sds((2 * rows, 2 * wide), BF)], **kw,
        )
        kv[m][1] = core(kv[m][0])

    mixed = [[None, None] for _ in mb]
    lse = [[None, None] for _ in mb]
    own = [None for _ in mb]
    rcv = [None for _ in mb]
    lse_rows = 8 * (wide // LANES)

    def attend(m, part, **kw):
        mixed[m][part], lse[m][part], term = line(
            kernel_of(attend_kernel, m, part), "attend", [seq_lengths] + kv[m] + [wo, q[m][part]],
            [sds((rows, wide), BF), sds((lse_rows, rows), F32), sds((rows, width), BF if part else F32)],
            n_smem=1, **kw,
        )
        if part:
            rcv[m] = across(term)
        else:
            own[m] = term

    hid = [None for _ in mb]
    n2 = [[None, None] for _ in mb]

    def mid(m, **kw):
        hid[m], n2[m][0] = line(
            kernel_of(mid_kernel, m), "mid", [own[m], rcv[m], vec, tokens],
            [sds((rows, width), F32), sds((rows, width), BF)], **kw,
        )
        n2[m][1] = across(n2[m][0])

    acts = [[None, None] for _ in mb]
    gates = [[None, None] for _ in mb]
    fsum = [[None, None] for _ in mb]
    nown = [None for _ in mb]
    nrcv = [None for _ in mb]

    def mlp(m, part, **kw):
        a_o, a_x, g_o, g_x, fsum[m][part], term = line(
            kernel_of(mlp_kernel, m), "mlp",
            [grads_p if part else out_grad, fc_weight, fc_x, fb, proj_weight, pj_x, n2[m][part]],
            [sds((rows, units), BF)] * 4 + [sds((2, units), F32), sds((rows, width), BF if part else F32)], **kw,
        )
        acts[m][part] = (a_o, a_x)
        gates[m][part] = (g_o, g_x)
        if part:
            nrcv[m] = across(term)
        else:
            nown[m] = term

    flat = [(m, part) for m in mb for part in range(2)]

    def mlp_weights(k, dtype, name, **kw):
        return line(
            kernel_of(mlp_weights_kernel, batches), name,
            [acts[m][i][k] for m, i in flat] + [gates[m][i][k] for m, i in flat] + [n2[m][i] for m, i in flat]
            + [out_grad, grads_p],
            [sds((units, width), dtype), sds((width, units), dtype)], **kw,
        )

    hg = [None for _ in mb]
    st2 = [None for _ in mb]
    br = [[None, None] for _ in mb]

    def ln2_back(m, **kw):
        hg[m], st2[m], br[m][0] = line(
            kernel_of(ln2_back_kernel, m), "ln2b", [hid[m], nown[m], nrcv[m], vec, out_grad],
            [sds((rows, width), F32), sds((8, width), F32), sds((rows, width), BF)], **kw,
        )
        br[m][1] = across(br[m][0])

    def proj(part, **kw):
        return line(
            kernel_of(proj_kernel, batches), "proj",
            [proj_weight, pj_x] + [acts[m][part][k] for m in mb for k in range(2)],
            [sds((batches, rows, width), BF if part else F32)], **kw,
        )[0]

    dq = [[None, None] for _ in mb]
    acc = [None for _ in mb]
    dkvo = [None for _ in mb]
    dkvr = [None for _ in mb]
    dkvs = [None for _ in mb]

    def attend_back(m, part, **kw):
        args = [seq_lengths] + kv[m] + [wo, mixed[m][part], lse[m][part], br[m][part]]
        scratch = [pltpu.VMEM((rows, wide), BF)]
        if part:
            dq[m][1], dkvo[m], send = line(
                kernel_of(attend_back_kernel, m, 1), "attendb", args + [acc[m], q[m][1]],
                [sds((rows, wide), BF), sds((2 * rows, 2 * wide), F32), sds((2 * rows, 2 * wide), BF)],
                n_smem=1, scratch=scratch, **kw,
            )
            dkvs[m] = send
        else:
            dq[m][0], acc[m] = line(
                kernel_of(attend_back_kernel, m, 0), "attendb", args + [q[m][0]],
                [sds((rows, wide), BF), sds((4 * rows, 2 * wide), F32)],
                n_smem=1, scratch=scratch, **kw,
            )

    dkv = [None for _ in mb]
    ngo = [None for _ in mb]
    ngr = [None for _ in mb]
    ngs = [None for _ in mb]
    qsum = [None for _ in mb]

    def qkv_back(m, **kw):
        dkv[m], ngo[m], qsum[m], rem = line(
            qkv_back_kernel, "qkvb", [dq[m][0], dq[m][1], dkvo[m], wq, dkvr[m]],
            [sds((2 * rows, 2 * wide), BF), sds((rows, width), F32), sds((2, wide), F32), sds((rows, width), BF)],
            **kw,
        )
        ngs[m] = rem

    last = batches - 1
    qkv(0)
    fc_x = core(after(fc_weight, q[0][0]))
    pj_x = core(after(proj_weight, q[0][0]))
    for m in mb[1:]:
        qkv(m)
    grads_p = across(after(out_grad, q[last][0]))
    attend(0, 1)
    attend(1, 1)
    attend(0, 0)
    attend(1, 0, needs=[grads_p])
    mid(0)
    mid(1)
    mlp(0, 0)
    mlp(1, 0)
    mlp(0, 1)
    mlp(1, 1)
    pj_send, fc_send = mlp_weights(1, BF, "mlpwx")
    pj_own, fc_own = mlp_weights(0, F32, "mlpwo")
    ln2_back(0)
    ln2_back(1)
    pj_back = core(after(pj_send, st2[last]))
    fc_back = core(after(fc_send, st2[last]))
    pown = proj(0)
    p_sum = Sum(pj_own, pj_back, "p")
    f_sum = Sum(fc_own, fc_back, "f")
    p_sum.go()
    attend_back(0, 0)
    attend_back(1, 0)
    p_sum.go(needs=[br[m][1] for m in mb])
    f_sum.go()
    attend_back(0, 1)
    p_sum.go()
    attend_back(1, 1)
    p_sum.go()
    f_sum.go()
    for m in mb:
        dkvr[m] = core(after(dkvs[m], f_sum.own))
    psend = proj(1)
    qkv_back(0)
    qkv_back(1)
    p_sum.go()
    f_sum.go()

    both = [normed, normed_p]
    a1_own, a1_send, a2_own, a2_send = line(
        kernel_of(attend_weights_kernel, batches), "attw",
        [dq[m][i] for m, i in flat] + [both[i][m] for m, i in flat] + [mixed[m][i] for m, i in flat]
        + [br[m][i] for m, i in flat] + dkv,
        [sds((2 * hc, width), F32), sds((2 * hc, width), BF)] * 2,
        limit=32,
    )
    ngr = [across(after(ngs[m], a2_send)) for m in mb]
    a_sum = Sum(a1_own, core(a1_send), "a")
    b_sum = Sum(a2_own, core(a2_send), "b", turn=1)
    a_sum.go()
    b_sum.go()
    prcv = across(after(psend, b_sum.own))
    p_sum.go()
    f_sum.go()
    a_sum.go()
    b_sum.go()
    ig, st1 = line(
        kernel_of(ln1_back_kernel, batches), "ln1b", [tokens, vec] + hg + ngo + ngr,
        [sds((batches, rows, width), F32), sds((8, width), F32)],
    )
    s_own, s_send = line(
        kernel_of(stats_kernel, batches), "stats",
        st2 + [fsum[m][i] for m, i in flat] + qsum + [st1],
        [sds((8, width), F32), sds((8, width), F32)],
    )
    s_rcv = core(s_send)
    f_sum.go()
    a_sum.go()
    b_sum.go()
    stats = line(add_kernel, "stat", [s_rcv, s_own], [sds((8, width), F32)])[0]
    s_rcv = across(stats)
    a_sum.go()
    b_sum.go()
    f_sum.go()
    stats = line(across_kernel, "staty", [s_rcv, stats], [sds((8, width), F32)])[0]
    for b in range(bits):
        s_rcv = swap(stats, b)
        a_sum.go()
        b_sum.go()
        stats = line(add_kernel, "stat", [s_rcv, stats], [sds((8, width), F32)])[0]
        if b == 0:
            layer_out = line(
                kernel_of(out_kernel, batches), "out", [vec] + hid + [pown, prcv],
                [sds((batches, rows, width), BF)],
            )[0]
    pj_grad = p_sum.finish()
    fc_grad = f_sum.finish()
    qk_grad = a_sum.finish()
    vo_grad = b_sum.finish()
    qk_grad = qk_grad.reshape(2, hc, width)
    qkv_grad = jnp.concatenate([qk_grad, vo_grad[None, :hc]], axis=0)

    return (
        layer_out,
        ig,
        jnp.transpose(qkv_grad, (2, 0, 1)),
        stats[6, :wide].reshape(2, hc),
        vo_grad[hc:],
        stats[4],
        stats[0],
        stats[1],
        fc_grad,
        stats[7],
        pj_grad,
        stats[5],
        stats[2],
        stats[3],
    )


def solution(mesh):
    placed = (
        P(None, ("dp", "tensor"), None),
        P(None, None, "tensor"),
        P(None, "tensor"),
        P("tensor", None),
        P(),
        P(),
        P(),
        P(None, "tensor"),
        P("tensor"),
        P("tensor", None),
        P(),
        P(),
        P(),
        P(None, "dp"),
        P(None, ("dp", "tensor"), None),
    )
    return jax.shard_map(
        body,
        mesh=mesh,
        in_specs=placed,
        out_specs=(
            P(None, ("dp", "tensor"), None),
            P(None, ("dp", "tensor"), None),
            P(None, None, "tensor"),
            P(None, "tensor"),
            P("tensor", None),
            P(),
            P(),
            P(),
            P(None, "tensor"),
            P("tensor"),
            P("tensor", None),
            P(),
            P(),
            P(),
        ),
        check_vma=False,
    )
```

```python
import math

import jax
import jax.numpy as jnp
from jax import lax
from jax.experimental import pallas as pl
from jax.experimental.pallas import tpu as pltpu
from jax.sharding import PartitionSpec as P

HD = 64
LANES = 128
LOG2E = 1.4426950408889634
NEG = -1e30
EPS = 1e-05
BF = jnp.bfloat16
F32 = jnp.float32
VM = pl.BlockSpec(memory_space=pltpu.VMEM)
SM = pl.BlockSpec(memory_space=pltpu.SMEM)
HB = pl.BlockSpec(memory_space=pltpu.HBM)


def dg(a, b, ca, cb):
    return lax.dot_general(a, b, (((ca,), (cb,)), ((), ())), preferred_element_type=F32)


def sds(shape, dtype):
    return jax.ShapeDtypeStruct(tuple(shape), dtype)


TIMES = dict(
    ln1=2.0, weights=1.4, qkv=2.3, attend=5.2, mid=0.4, mlp=4.0, mlpwx=4.0, mlpwo=4.0, ln2b=1.8, proj=1.4,
    attendb=7.0, qkvb=2.8, attw=2.7, ln1b=2.4, out=1.1, halve=10.0, last=10.0, join=10.0,
)
SCALE = 0.3


class Line:
    def __init__(self):
        self.last = None

    def __call__(self, kernel, name, args, outs, n_smem=0, scratch=(), limit=24, far=0, needs=()):
        args = list(args)
        after = list(needs)
        if self.last is not None:
            after.append(self.last)
        if after:
            args[-1] = lax.optimization_barrier(tuple([args[-1]] + after))[0]
        for i in range(n_smem, n_smem + far):
            args[i] = pltpu.with_memory_space_constraint(args[i], pltpu.HBM)
        fetched = args[n_smem : n_smem + far]
        total = len(args)

        def run(*refs):
            if not far:
                return kernel(*refs)
            body_refs = refs[: len(refs) - far - 1]
            bufs = refs[len(refs) - far - 1 : -1]
            sems = refs[-1]
            copies = [
                pltpu.make_async_copy(refs[n_smem + i], bufs[i], sems.at[i]) for i in range(far)
            ]
            for cp in copies:
                cp.start()
            for cp in copies:
                cp.wait()
            return kernel(*body_refs[:n_smem], *bufs, *body_refs[n_smem + far :])

        extra = []
        if far:
            extra = [pltpu.VMEM(v.shape, v.dtype) for v in fetched] + [pltpu.SemaphoreType.DMA((far,))]
        res = pl.pallas_call(
            run,
            in_specs=[SM] * n_smem + [HB] * far + [VM] * (total - n_smem - far),
            out_specs=[VM] * len(outs),
            out_shape=outs,
            scratch_shapes=list(scratch) + extra,
            compiler_params=pltpu.CompilerParams(vmem_limit_bytes=limit << 20),
            cost_estimate=pl.CostEstimate(
                flops=int(SCALE * 1.1e9 * TIMES.get(name.split("_")[0], 0.2)), transcendentals=0, bytes_accessed=1
            ),
            name=name,
        )(*args)
        self.last = res[-1]
        return res


def normalize(x):
    d = x.shape[-1]
    xc = x - jnp.sum(x, axis=-1, keepdims=True) * (1.0 / d)
    var = jnp.sum(xc * xc, axis=-1, keepdims=True) * (1.0 / d)
    r = lax.rsqrt(var + EPS)
    return xc * r, r


def norm_back(grad, z, r, gain):
    d = z.shape[-1]
    e = grad * gain
    me = jnp.sum(e, axis=-1, keepdims=True) * (1.0 / d)
    mez = jnp.sum(e * z, axis=-1, keepdims=True) * (1.0 / d)
    return (e - me - z * mez) * r


def col_sum(x):
    return jnp.sum(x.astype(F32), axis=0, keepdims=True)


def ln1_kernel(*refs):
    vecs = refs[:6]
    fb_ref, qb_ref, tok_ref = refs[6:9]
    outs = refs[9:-2]
    small_ref, vec_ref = refs[-2:]
    vec_ref[...] = jnp.zeros(vec_ref.shape, F32)
    for i, v in enumerate(vecs):
        vec_ref[i : i + 1, :] = v[...].astype(F32).reshape(1, -1)
    for m, o_ref in enumerate(outs):
        z, _ = normalize(tok_ref[m].astype(F32))
        o_ref[...] = (z * vec_ref[1:2] + vec_ref[2:3]).astype(BF)
    small_ref[...] = jnp.zeros(small_ref.shape, F32)
    small_ref[0:1, : fb_ref.shape[0]] = fb_ref[...].astype(F32).reshape(1, -1)
    small_ref[1:3, : qb_ref.shape[1]] = qb_ref[...].astype(F32)


def weights_kernel(woo_ref, wqo_ref, so_ref, sx_ref, wox_ref, wqx_ref, qb_ref, fb_ref, wo_ref, wq_ref):
    c = lax.axis_index("tensor") & 1
    hc = woo_ref.shape[0]
    units = fb_ref.shape[1]
    fb_ref[0:1, :] = so_ref[0:1, :units]
    fb_ref[1:2, :] = sx_ref[0:1, :units]
    qb_ref[...] = jnp.zeros(qb_ref.shape, F32)

    def place(at_o, at_x):
        for at, b, o, q in ((at_o, so_ref, woo_ref, wqo_ref), (at_x, sx_ref, wox_ref, wqx_ref)):
            qb_ref[0:1, at : at + hc] = b[1:2, :hc]
            qb_ref[2:3, at : at + hc] = b[2:3, :hc]
            wo_ref[at : at + hc, :] = o[...]
            wq_ref[:, at : at + hc, :] = q[...]

    @pl.when(c == 0)
    def _():
        place(0, hc)

    @pl.when(c != 0)
    def _():
        place(hc, 0)


def qkv_kernel(b_ref, w_ref, no_ref, np_ref, qo_ref, qp_ref, kv_ref):
    rows, wide = qo_ref.shape
    for i, (n_ref, q_ref) in enumerate(((no_ref, qo_ref), (np_ref, qp_ref))):
        n = n_ref[...]
        for s in range(3):
            v = (dg(n, w_ref[s], 1, 1) + b_ref[s : s + 1]).astype(BF)
            if s == 0:
                q_ref[...] = v
            else:
                kv_ref[i * rows : (i + 1) * rows, wide * (s - 1) : wide * s] = v


def row_starts(rows):
    t = lax.axis_index("tensor")
    return [rows * t, rows * (t ^ 2), rows * (t ^ 1), rows * (t ^ 3)]


def key_bias(starts, length, rows):
    out = []
    for b in range(4):
        at = lax.broadcasted_iota(jnp.int32, (rows, LANES), 0) + starts[b]
        out.append(jnp.where(at < length, 0.0, NEG).astype(BF))
    return jnp.concatenate(out, axis=0)


def attend_kernel(m, part, len_ref, ka_ref, kb_ref, w_ref, q_ref, mixed_ref, lse_ref, term_ref):
    rows, wide = q_ref.shape
    length = len_ref[m, 0]
    starts = row_starts(rows)
    c = LOG2E / math.sqrt(HD)
    bias = key_bias(starts, length, rows)
    lane = lax.broadcasted_iota(jnp.int32, (4 * rows, LANES), 1)
    laneq = lax.broadcasted_iota(jnp.int32, (rows, LANES), 1)
    valid = lax.broadcasted_iota(jnp.int32, (rows, LANES), 0) + starts[part] < length
    kvs = (ka_ref, kb_ref)

    def pair(p, carry):
        cs = pl.ds(pl.multiple_of(LANES * p, LANES), LANES)
        vs = pl.ds(pl.multiple_of(wide + LANES * p, LANES), LANES)
        kp = jnp.concatenate([r[:, cs] for r in kvs], axis=0)
        vp = jnp.concatenate([r[:, vs] for r in kvs], axis=0)
        qp = q_ref[:, cs]
        os = []
        ls = []
        for h in range(2):
            inh = (laneq < HD) if h == 0 else (laneq >= HD)
            mark = HD * (1 - h)
            one = jnp.where(laneq == mark, 1.0, 0.0).astype(BF)
            s = dg(jnp.where(inh, qp, one), jnp.where(lane == mark, bias, kp), 1, 1)
            top = jnp.max(s, axis=1, keepdims=True)
            e = jnp.exp2((s - top) * c)
            l = jnp.sum(e, axis=1, keepdims=True)
            os.append(dg(e.astype(BF), vp, 1, 0) * (1.0 / l))
            ls.append(top * c + jnp.log2(l))
        ob = jnp.where(laneq < HD, os[0], os[1])
        lt = jnp.where(laneq < HD, ls[0], ls[1]).T
        lse_ref[pl.ds(8 * p, 1), :] = lt[0:1]
        lse_ref[pl.ds(8 * p + 1, 1), :] = lt[HD : HD + 1]
        mixed_ref[:, cs] = jnp.where(valid, ob, 0.0).astype(BF)
        return carry

    lax.fori_loop(0, wide // LANES, pair, 0)
    term_ref[...] = dg(mixed_ref[...], w_ref[...], 1, 0).astype(term_ref.dtype)


def mid_kernel(m, own_ref, rcv_ref, vec_ref, tok_ref, hid_ref, n_ref):
    h = tok_ref[m].astype(F32) + (own_ref[...] + rcv_ref[...].astype(F32)) + vec_ref[0:1]
    hid_ref[...] = h
    z, _ = normalize(h)
    n_ref[...] = (z * vec_ref[4:5] + vec_ref[5:6]).astype(BF)


def mlp_kernel(m, g_ref, fo_ref, fx_ref, bias_ref, po_ref, px_ref, n_ref, ao_ref, ax_ref, ggo_ref, ggx_ref, sum_ref, term_ref):
    n = n_ref[...]
    g = g_ref[m]
    back = None
    for j, (f_ref, p_ref, a_ref, gg_ref) in enumerate(
        ((fo_ref, po_ref, ao_ref, ggo_ref), (fx_ref, px_ref, ax_ref, ggx_ref))
    ):
        f = f_ref[...]
        gate = dg(n, f, 1, 0) + bias_ref[j : j + 1]
        q = 0.5 * jnp.tanh(0.851 * gate) + 0.5
        a_ref[...] = (gate * q).astype(BF)
        slope = q + 1.702 * gate * q * (1.0 - q)
        gg = (dg(g, p_ref[...], 1, 1) * slope).astype(BF)
        gg_ref[...] = gg
        term = dg(gg, f, 1, 1)
        back = term if back is None else back + term
        sum_ref[j : j + 1] = col_sum(gg)
    term_ref[...] = back.astype(term_ref.dtype)


def proj_kernel(count, po_ref, px_ref, *refs):
    out_ref = refs[-1]
    for m in range(count):
        out_ref[m] = (dg(refs[2 * m][...], po_ref[...], 1, 0) + dg(refs[2 * m + 1][...], px_ref[...], 1, 0)).astype(
            out_ref.dtype
        )


def ln2_back_kernel(m, hid_ref, own_ref, rcv_ref, vec_ref, grad_ref, hg_ref, st_ref, br_ref):
    z, r = normalize(hid_ref[...])
    ng = own_ref[...] + rcv_ref[...].astype(F32)
    g = grad_ref[m].astype(F32)
    hg = g + norm_back(ng, z, r, vec_ref[4:5])
    hg_ref[...] = hg
    br = hg.astype(BF)
    br_ref[...] = br
    st_ref[...] = jnp.zeros(st_ref.shape, F32)
    st_ref[2:3] = col_sum(ng * z)
    st_ref[3:4] = col_sum(ng)
    st_ref[4:5] = col_sum(br)
    st_ref[5:6] = col_sum(g)


def attend_back_kernel(m, part, *refs):
    len_ref, ka_ref, kb_ref, w_ref, mixed_ref, lse_ref, b_ref = refs[:7]
    refs = refs[7:]
    if part:
        (acc_in, q_ref, dq_ref, out_ref, send_ref, do_ref) = refs
    else:
        (q_ref, dq_ref, acc_ref, do_ref) = refs
    rows, wide = q_ref.shape
    length = len_ref[m, 0]
    starts = row_starts(rows)
    c = LOG2E / math.sqrt(HD)
    sc = 1.0 / math.sqrt(HD)
    at = lax.broadcasted_iota(jnp.int32, (rows, wide), 0) + starts[part]
    do_ref[...] = jnp.where(at < length, dg(b_ref[...], w_ref[...], 1, 1), 0.0).astype(BF)
    bias = key_bias(starts, length, rows)
    lane = lax.broadcasted_iota(jnp.int32, (4 * rows, LANES), 1)
    laneq = lax.broadcasted_iota(jnp.int32, (rows, LANES), 1)
    zero = jnp.zeros((), BF)
    kvs = (ka_ref, kb_ref)

    def pair(p, carry):
        cs = pl.ds(pl.multiple_of(LANES * p, LANES), LANES)
        vs = pl.ds(pl.multiple_of(wide + LANES * p, LANES), LANES)
        kp = jnp.concatenate([r[:, cs] for r in kvs], axis=0)
        vp = jnp.concatenate([r[:, vs] for r in kvs], axis=0)
        kt = kp.T
        qp = q_ref[:, cs]
        dop = do_ref[:, cs]
        prod = (dop.astype(F32) * mixed_ref[:, cs].astype(F32)).T
        dqt = []
        dk = None
        dv = None
        for h in range(2):
            inh = (laneq < HD) if h == 0 else (laneq >= HD)
            mark = HD * (1 - h)
            qz = jnp.where(inh, qp, zero)
            qh = jnp.where(laneq == mark, jnp.ones((), BF), qz)
            doh = jnp.where(inh, dop, zero)
            st = dg(jnp.where(lane == mark, bias, kp), qh, 1, 1)
            pt = jnp.exp2(st * c - lse_ref[pl.ds(8 * p + h, 1), :])
            dpt = dg(vp, doh, 1, 1)
            row = jnp.sum(prod[HD * h : HD * (h + 1)], axis=0, keepdims=True)
            ds = (pt * (dpt - row)).astype(BF)
            dvh = dg(pt.astype(BF), doh, 1, 0)
            dkh = dg(ds, qz, 1, 0)
            dqt.append(dg(kt[HD * h : HD * (h + 1)], ds, 1, 0))
            dv = dvh if dv is None else dv + dvh
            dk = dkh if dk is None else dk + dkh
        dq_ref[:, cs] = (jnp.concatenate(dqt, axis=0).T * sc).astype(BF)
        dk = dk * sc
        if part:
            dk = dk + acc_in[:, cs]
            dv = dv + acc_in[:, vs]
            out_ref[:, cs] = dk[: 2 * rows]
            out_ref[:, vs] = dv[: 2 * rows]
            send_ref[:, cs] = dk[2 * rows :].astype(BF)
            send_ref[:, vs] = dv[2 * rows :].astype(BF)
        else:
            acc_ref[:, cs] = dk
            acc_ref[:, vs] = dv
        return carry

    lax.fori_loop(0, wide // LANES, pair, 0)


def qkv_back_kernel(count, *refs):
    w_ref = refs[0]
    ins = refs[1 : 1 + 4 * count]
    outs = refs[1 + 4 * count :]
    ngr_ref = outs[-1]
    sum_ref = outs[-2]
    rows = ngr_ref.shape[1]
    sq = None
    sv = None
    for m in range(count):
        dqo_ref, dqp_ref, own_ref, rcv_ref = ins[4 * m : 4 * m + 4]
        dkv_ref, ngo_ref = outs[2 * m : 2 * m + 2]
        wide = dqo_ref.shape[1]
        for i, dq_ref in ((1, dqp_ref), (0, dqo_ref)):
            at = slice(i * rows, (i + 1) * rows)
            dkv = (own_ref[at, :] + rcv_ref[at, :].astype(F32)).astype(BF)
            dkv_ref[at, :] = dkv
            dq = dq_ref[...]
            ng = dg(dq, w_ref[0], 1, 0) + dg(dkv[:, :wide], w_ref[1], 1, 0) + dg(dkv[:, wide:], w_ref[2], 1, 0)
            if i:
                ngr_ref[m] = ng.astype(BF)
            else:
                ngo_ref[...] = ng
            cq = col_sum(dq)
            cv = col_sum(dkv[:, wide:])
            sq = cq if sq is None else sq + cq
            sv = cv if sv is None else sv + cv
    sum_ref[0:1] = sq
    sum_ref[1:2] = sv


def ln1_back_kernel(count, *refs):
    tok_ref = refs[0]
    vec_ref = refs[1]
    hgs = refs[2 : 2 + count]
    owns = refs[2 + count : 2 + 2 * count]
    rcv_ref, ig_ref, st_ref = refs[2 + 2 * count :]
    g = None
    s = None
    for m in range(count):
        z, r = normalize(tok_ref[m].astype(F32))
        ng = owns[m][...] + rcv_ref[m].astype(F32)
        ig_ref[m] = hgs[m][...] + norm_back(ng, z, r, vec_ref[1:2])
        gm = col_sum(ng * z)
        sm = col_sum(ng)
        g = gm if g is None else g + gm
        s = sm if s is None else s + sm
    st_ref[...] = jnp.zeros(st_ref.shape, F32)
    st_ref[0:1] = g
    st_ref[1:2] = s


def out_kernel(count, vec_ref, *refs):
    hids = refs[:count]
    own_ref, rcv_ref, o_ref = refs[count:]
    for m in range(count):
        o_ref[m] = (hids[m][...] + (own_ref[m] + rcv_ref[m].astype(F32)) + vec_ref[3:4]).astype(BF)


def rows_product(pairs):
    acc = None
    for a, b in pairs:
        t = dg(a, b, 0, 0)
        acc = t if acc is None else acc + t
    return acc


def mlp_weights_kernel(count, *refs):
    n = 2 * count
    acts = refs[:n]
    gates = refs[n : 2 * n]
    norms = refs[2 * n : 3 * n]
    go_ref, gp_ref, pj_ref, fc_ref = refs[3 * n :]
    gs = []
    for m in range(count):
        gs += [go_ref[m], gp_ref[m]]
    pj_ref[...] = rows_product([(a[...], g) for a, g in zip(acts, gs)]).astype(pj_ref.dtype)
    fc_ref[...] = rows_product([(a[...], b[...]) for a, b in zip(norms, gates)]).astype(fc_ref.dtype)


def attend_weights_kernel(count, *refs):
    n = 2 * count
    dqs = refs[:n]
    norms = refs[n : 2 * n]
    mixes = refs[2 * n : 3 * n]
    brs = refs[3 * n : 4 * n]
    dkvs = refs[4 * n : 4 * n + count]
    outs = refs[4 * n + count :]
    c = lax.axis_index("tensor") & 1
    rows, wide = dqs[0].shape
    hc = wide // 2
    ns = [r[...] for r in norms]
    full = [jnp.concatenate(ns[2 * m : 2 * m + 2], axis=0) for m in range(count)]
    pieces = [
        rows_product([(a[...], b) for a, b in zip(dqs, ns)]),
        rows_product([(a[:, :wide], b) for a, b in zip(dkvs, full)]),
        rows_product([(a[:, wide:], b) for a, b in zip(dkvs, full)]),
        rows_product([(a[...], b[...]) for a, b in zip(mixes, brs)]),
    ]
    for i, p in enumerate(pieces):
        own_ref, send_ref = outs[2 * (i // 2) : 2 * (i // 2) + 2]
        at = slice((i % 2) * hc, (i % 2 + 1) * hc)
        low = p[:hc]
        high = p[hc:]
        own_ref[at, :] = jnp.where(c == 0, low, high)
        send_ref[at, :] = jnp.where(c == 0, high, low).astype(BF)


def add_kernel(rcv_ref, own_ref, out_ref):
    out_ref[...] = (own_ref[...].astype(F32) + rcv_ref[...].astype(F32)).astype(out_ref.dtype)


def halve_kernel(bit, rcv_ref, own_ref, keep_ref, send_ref):
    r = keep_ref.shape[0]
    b = (lax.axis_index("dp") >> bit) & 1
    mine = pl.ds(pl.multiple_of(b * r, r), r)
    other = pl.ds(pl.multiple_of((1 - b) * r, r), r)
    send_ref[...] = (own_ref[other, :].astype(F32) + rcv_ref[other, :].astype(F32)).astype(BF)
    keep_ref[...] = own_ref[mine, :].astype(F32) + rcv_ref[mine, :].astype(F32)


def join_kernel(bit, rcv_ref, own_ref, out_ref):
    r = own_ref.shape[0]
    b = (lax.axis_index("dp") >> bit) & 1
    out_ref[pl.ds(pl.multiple_of(b * r, r), r), :] = own_ref[...].astype(out_ref.dtype)
    out_ref[pl.ds(pl.multiple_of((1 - b) * r, r), r), :] = rcv_ref[...].astype(out_ref.dtype)


def join_both_kernel(bit, rcv_a, own_a, rcv_b, own_b, qkv_ref, out_ref):
    r = own_a.shape[0]
    b = (lax.axis_index("dp") >> bit) & 1
    qkv_ref[pl.ds(pl.multiple_of(b * r, r), r), :] = own_a[...].astype(F32)
    qkv_ref[pl.ds(pl.multiple_of((1 - b) * r, r), r), :] = rcv_a[...].astype(F32)

    @pl.when(b == 0)
    def _():
        qkv_ref[2 * r :, :] = own_b[...].astype(F32)
        out_ref[...] = rcv_b[...].astype(F32)

    @pl.when(b != 0)
    def _():
        qkv_ref[2 * r :, :] = rcv_b[...].astype(F32)
        out_ref[...] = own_b[...].astype(F32)


def stats_kernel(count, *refs):
    lst2 = refs[:count]
    fsums = refs[count : 3 * count]
    q_ref, lst1_ref, own_ref, send_ref = refs[3 * count :]
    c = lax.axis_index("tensor") & 1
    common = lst1_ref[...]
    for r in lst2:
        common = common + r[...]
    f = fsums[0][...]
    for r in fsums[1:]:
        f = f + r[...]
    q = q_ref[...]
    wide = own_ref.shape[1]
    hc = q.shape[1] // 2
    qpad = jnp.zeros((1, wide - 2 * hc), F32)
    low = jnp.concatenate([q[0:1, :hc], q[1:2, :hc], qpad], axis=1)
    high = jnp.concatenate([q[0:1, hc:], q[1:2, hc:], qpad], axis=1)
    own_ref[...] = common
    send_ref[...] = common
    own_ref[6:7] = jnp.where(c == 0, low, high)
    send_ref[6:7] = jnp.where(c == 0, high, low)
    own_ref[7:8] = f[0:1]
    send_ref[7:8] = f[1:2]


def spread_kernel(rcv_ref, own_ref, fb_ref, qb_ref, *outs):
    total = own_ref[...] + rcv_ref[...]
    for i, o_ref in enumerate(outs):
        o_ref[...] = total[i : i + 1].reshape(o_ref.shape)
    hc = qb_ref.shape[1]
    qb_ref[0:1, :] = total[6:7, :hc]
    qb_ref[1:2, :] = total[6:7, hc : 2 * hc]
    fb_ref[...] = total[7:8, : fb_ref.shape[0]].reshape(fb_ref.shape)


def across_kernel(rcv_ref, own_ref, out_ref):
    at = lax.broadcasted_iota(jnp.int32, own_ref.shape, 0)
    out_ref[...] = own_ref[...] + jnp.where(at < 6, rcv_ref[...], 0.0)


def body(
    tokens, qkv_weight, qv_bias, out_weight, out_bias, ln1_gain, ln1_shift, fc_weight, fc_bias,
    proj_weight, proj_bias, ln2_gain, ln2_shift, seq_lengths, out_grad,
):
    batches, rows, width = tokens.shape
    hc = out_weight.shape[0]
    wide = 2 * hc
    units = fc_weight.shape[1]
    tsize = lax.axis_size("tensor")
    dsize = lax.axis_size("dp")
    bits = dsize.bit_length() - 1
    cpairs = [(i, i ^ 1) for i in range(tsize)]
    ypairs = [(i, i ^ 2) for i in range(tsize)]
    mb = range(batches)
    line = Line()

    def core(v):
        return lax.ppermute(v, "tensor", cpairs)

    def across(v):
        return lax.ppermute(v, "tensor", ypairs)

    def swap(v, b):
        return lax.ppermute(v, "dp", [(i, i ^ (1 << b)) for i in range(dsize)])

    def after(v, *deps):
        return lax.optimization_barrier((v,) + deps)[0]

    def kernel_of(f, *static):
        def kernel(*refs):
            f(*static, *refs)

        return kernel

    def halve(own, rcv, b, name, **kw):
        size = own.shape[0] // 2
        if size % 16:
            both = own.astype(F32) + rcv.astype(F32)
            both = both.reshape((2, size) + own.shape[1:])
            bit = (lax.axis_index("dp") >> b) & 1
            keep = lax.dynamic_index_in_dim(both, bit, 0, keepdims=False)
            return keep, lax.dynamic_index_in_dim(both, 1 - bit, 0, keepdims=False).astype(BF)
        shape = (size,) + own.shape[1:]
        return line(kernel_of(halve_kernel, b), "halve_" + name, [rcv, own], [sds(shape, F32), sds(shape, BF)], **kw)

    def join(piece, rcv, b, dtype, name):
        size = piece.shape[0]
        if size % 16:
            low = ((lax.axis_index("dp") >> b) & 1) == 0
            return jnp.concatenate([jnp.where(low, piece, rcv), jnp.where(low, rcv, piece)], axis=0).astype(dtype)
        shape = (2 * size,) + piece.shape[1:]
        return line(kernel_of(join_kernel, b), "join_" + name, [rcv, piece], [sds(shape, dtype)])[0]

    class Sum:
        def __init__(self, own, rcv, name, turn=0):
            self.own, self.rcv, self.name, self.at = own, rcv, name, 0
            self.order = [(b + turn) % bits for b in range(bits)]

        def go(self, **kw):
            k = self.at
            self.at += 1
            if k > 2 * bits:
                return
            if k < bits:
                self.own, send = halve(self.own, self.rcv, self.order[k], self.name, **kw)
            elif k == bits:
                send = line(add_kernel, "last_" + self.name, [self.rcv, self.own], [sds(self.own.shape, BF)], **kw)[0]
                self.own = send
            else:
                b = self.order[2 * bits - k]
                send = join(self.own, self.rcv, b, F32 if k == 2 * bits else BF, self.name)
                self.own = send
            if k < 2 * bits:
                self.rcv = swap(send, self.order[k if k < bits else 2 * bits - 1 - k])

        def finish(self):
            while self.at <= 2 * bits:
                self.go()
            return self.own

    wq_o = jnp.transpose(qkv_weight, (1, 2, 0))
    wq_x = core(wq_o)
    wo_x = core(out_weight)

    packed = (8, max(units, width))
    *normed, small, vec = line(
        ln1_kernel, "ln1",
        [out_bias, ln1_gain, ln1_shift, proj_bias, ln2_gain, ln2_shift, fc_bias, qv_bias, tokens],
        [sds((rows, width), BF)] * batches + [sds(packed, F32), sds((8, width), F32)], far=9,
    )
    normed_p = [across(v) for v in normed]
    qb, fb, wo, wq = line(
        weights_kernel, "weights", [out_weight, wq_o, small, core(small), wo_x, wq_x],
        [sds((3, wide), F32), sds((2, units), F32), sds((wide, width), BF), sds((3, wide, width), BF)], far=2,
    )

    q = [[None, None] for _ in mb]
    kv = [[None, None] for _ in mb]

    def qkv(m, **kw):
        q[m][0], q[m][1], kv[m][0] = line(
            qkv_kernel, "qkv", [qb, wq, normed[m], normed_p[m]],
            [sds((rows, wide), BF)] * 2 + [sds((2 * rows, 2 * wide), BF)], **kw,
        )
        kv[m][1] = core(kv[m][0])

    mixed = [[None, None] for _ in mb]
    lse = [[None, None] for _ in mb]
    own = [None for _ in mb]
    rcv = [None for _ in mb]
    lse_rows = 8 * (wide // LANES)

    def attend(m, part, **kw):
        mixed[m][part], lse[m][part], term = line(
            kernel_of(attend_kernel, m, part), "attend", [seq_lengths] + kv[m] + [wo, q[m][part]],
            [sds((rows, wide), BF), sds((lse_rows, rows), F32), sds((rows, width), BF if part else F32)],
            n_smem=1, **kw,
        )
        if part:
            rcv[m] = across(term)
        else:
            own[m] = term

    hid = [None for _ in mb]
    n2 = [[None, None] for _ in mb]

    def mid(m, **kw):
        hid[m], n2[m][0] = line(
            kernel_of(mid_kernel, m), "mid", [own[m], rcv[m], vec, tokens],
            [sds((rows, width), F32), sds((rows, width), BF)], **kw,
        )
        n2[m][1] = across(n2[m][0])

    acts = [[None, None] for _ in mb]
    gates = [[None, None] for _ in mb]
    fsum = [[None, None] for _ in mb]
    nown = [None for _ in mb]
    nrcv = [None for _ in mb]

    def mlp(m, part, **kw):
        a_o, a_x, g_o, g_x, fsum[m][part], term = line(
            kernel_of(mlp_kernel, m), "mlp",
            [grads_p if part else out_grad, fc_weight, fc_x, fb, proj_weight, pj_x, n2[m][part]],
            [sds((rows, units), BF)] * 4 + [sds((2, units), F32), sds((rows, width), BF if part else F32)], **kw,
        )
        acts[m][part] = (a_o, a_x)
        gates[m][part] = (g_o, g_x)
        if part:
            nrcv[m] = across(term)
        else:
            nown[m] = term

    flat = [(m, part) for m in mb for part in range(2)]

    def mlp_weights(k, dtype, name, **kw):
        return line(
            kernel_of(mlp_weights_kernel, batches), name,
            [acts[m][i][k] for m, i in flat] + [gates[m][i][k] for m, i in flat] + [n2[m][i] for m, i in flat]
            + [out_grad, grads_p],
            [sds((units, width), dtype), sds((width, units), dtype)], **kw,
        )

    hg = [None for _ in mb]
    st2 = [None for _ in mb]
    br = [[None, None] for _ in mb]

    def ln2_back(m, **kw):
        hg[m], st2[m], br[m][0] = line(
            kernel_of(ln2_back_kernel, m), "ln2b", [hid[m], nown[m], nrcv[m], vec, out_grad],
            [sds((rows, width), F32), sds((8, width), F32), sds((rows, width), BF)], **kw,
        )
        br[m][1] = across(br[m][0])

    def proj(part, **kw):
        return line(
            kernel_of(proj_kernel, batches), "proj",
            [proj_weight, pj_x] + [acts[m][part][k] for m in mb for k in range(2)],
            [sds((batches, rows, width), BF if part else F32)], **kw,
        )[0]

    dq = [[None, None] for _ in mb]
    acc = [None for _ in mb]
    dkvo = [None for _ in mb]
    dkvr = [None for _ in mb]
    dkvs = [None for _ in mb]

    def attend_back(m, part, **kw):
        args = [seq_lengths] + kv[m] + [wo, mixed[m][part], lse[m][part], br[m][part]]
        scratch = [pltpu.VMEM((rows, wide), BF)]
        if part:
            dq[m][1], dkvo[m], send = line(
                kernel_of(attend_back_kernel, m, 1), "attendb", args + [acc[m], q[m][1]],
                [sds((rows, wide), BF), sds((2 * rows, 2 * wide), F32), sds((2 * rows, 2 * wide), BF)],
                n_smem=1, scratch=scratch, **kw,
            )
            dkvs[m] = send
        else:
            dq[m][0], acc[m] = line(
                kernel_of(attend_back_kernel, m, 0), "attendb", args + [q[m][0]],
                [sds((rows, wide), BF), sds((4 * rows, 2 * wide), F32)],
                n_smem=1, scratch=scratch, **kw,
            )

    def qkv_back(**kw):
        args = [wq]
        for m in mb:
            args += [dq[m][0], dq[m][1], dkvo[m], dkvr[m]]
        *res, qsum, rem = line(
            kernel_of(qkv_back_kernel, batches), "qkvb", args,
            [sds((2 * rows, 2 * wide), BF), sds((rows, width), F32)] * batches
            + [sds((2, wide), F32), sds((batches, rows, width), BF)], **kw,
        )
        return res[0::2], res[1::2], qsum, rem

    last = batches - 1
    qkv(0)
    fc_x = core(after(fc_weight, q[0][0]))
    pj_x = core(after(proj_weight, q[0][0]))
    for m in mb[1:]:
        qkv(m)
    grads_p = across(after(out_grad, q[last][0]))
    attend(0, 1)
    attend(1, 1)
    attend(0, 0)
    attend(1, 0, needs=[grads_p])
    mid(0)
    mid(1)
    mlp(0, 0)
    mlp(1, 0)
    mlp(0, 1)
    mlp(1, 1)
    pj_send, fc_send = mlp_weights(1, BF, "mlpwx")
    pj_own, fc_own = mlp_weights(0, F32, "mlpwo")
    ln2_back(0)
    ln2_back(1)
    pj_back = core(after(pj_send, st2[last]))
    fc_back = core(after(fc_send, st2[last]))
    pown = proj(0)
    p_sum = Sum(pj_own, pj_back, "p")
    f_sum = Sum(fc_own, fc_back, "f")
    p_sum.go()
    psend = proj(1)
    attend_back(0, 0)
    attend_back(1, 0)
    f_sum.go(needs=[br[m][1] for m in mb])
    p_sum.go()
    prcv = across(after(psend, p_sum.own))
    attend_back(0, 1)
    p_sum.go()
    attend_back(1, 1)
    p_sum.go(needs=[prcv])
    f_sum.go()
    for m in mb:
        dkvr[m] = core(after(dkvs[m], f_sum.own))
    dkv, ngo, qsum, ngs = qkv_back()

    both = [normed, normed_p]
    a1_own, a1_send, a2_own, a2_send = line(
        kernel_of(attend_weights_kernel, batches), "attw",
        [dq[m][i] for m, i in flat] + [both[i][m] for m, i in flat] + [mixed[m][i] for m, i in flat]
        + [br[m][i] for m, i in flat] + dkv,
        [sds((2 * hc, width), F32), sds((2 * hc, width), BF)] * 2,
        limit=32,
    )
    ngr = across(after(ngs, a2_send))
    a_sum = Sum(a1_own, core(a1_send), "a")
    b_sum = Sum(a2_own, core(a2_send), "b")
    p_sum.go()
    f_sum.go()
    a_sum.go()
    b_sum.go()
    layer_out = line(
        kernel_of(out_kernel, batches), "out", [vec] + hid + [pown, prcv], [sds((batches, rows, width), BF)],
    )[0]
    p_sum.go()
    f_sum.go()
    a_sum.go()
    b_sum.go()
    a_sum.go()
    f_sum.go()
    ig, st1 = line(
        kernel_of(ln1_back_kernel, batches), "ln1b", [tokens, vec] + hg + ngo + [ngr],
        [sds((batches, rows, width), F32), sds((8, width), F32)],
    )
    b_sum.go()
    s_own, s_send = line(
        kernel_of(stats_kernel, batches), "stats",
        st2 + [fsum[m][i] for m, i in flat] + [qsum, st1],
        [sds((8, width), F32), sds((8, width), F32)],
    )
    s_rcv = core(s_send)
    a_sum.go()
    f_sum.go()
    stats = line(add_kernel, "stat", [s_rcv, s_own], [sds((8, width), F32)])[0]
    s_rcv = across(stats)
    p_sum.finish()
    b_sum.go()
    a_sum.go()
    stats = line(across_kernel, "staty", [s_rcv, stats], [sds((8, width), F32)])[0]
    for b in range(bits):
        s_rcv = swap(stats, b)
        for chain in (b_sum, a_sum):
            if chain.at < 2 * bits:
                chain.go()
        if b == 1:
            f_sum.finish()
        if b < bits - 1:
            stats = line(add_kernel, "stat", [s_rcv, stats], [sds((8, width), F32)])[0]
    for chain in (a_sum, b_sum):
        while chain.at < 2 * bits:
            chain.go()
    vector = sds((width,), F32)
    fb_grad, qb_grad, *vectors = line(
        spread_kernel, "spread", [s_rcv, stats],
        [sds((units,), F32), sds((2, hc), F32)] + [vector] * 6,
    )
    qkv_grad, out_grad_w = line(
        kernel_of(join_both_kernel, a_sum.order[0]), "join_ab", [a_sum.rcv, a_sum.own, b_sum.rcv, b_sum.own],
        [sds((3 * hc, width), F32), sds((hc, width), F32)],
    )
    fc_grad = f_sum.finish()
    pj_grad = p_sum.own

    return (
        layer_out,
        ig,
        jnp.transpose(qkv_grad.reshape(3, hc, width), (2, 0, 1)),
        qb_grad,
        out_grad_w,
        vectors[4],
        vectors[0],
        vectors[1],
        fc_grad,
        fb_grad,
        pj_grad,
        vectors[5],
        vectors[2],
        vectors[3],
    )


def solution(mesh):
    placed = (
        P(None, ("dp", "tensor"), None),
        P(None, None, "tensor"),
        P(None, "tensor"),
        P("tensor", None),
        P(),
        P(),
        P(),
        P(None, "tensor"),
        P("tensor"),
        P("tensor", None),
        P(),
        P(),
        P(),
        P(None, "dp"),
        P(None, ("dp", "tensor"), None),
    )
    return jax.shard_map(
        body,
        mesh=mesh,
        in_specs=placed,
        out_specs=(
            P(None, ("dp", "tensor"), None),
            P(None, ("dp", "tensor"), None),
            P(None, None, "tensor"),
            P(None, "tensor"),
            P("tensor", None),
            P(),
            P(),
            P(),
            P(None, "tensor"),
            P("tensor"),
            P("tensor", None),
            P(),
            P(),
            P(),
        ),
        check_vma=False,
    )
```

```python
import math

import jax
import jax.numpy as jnp
from jax import lax
from jax.experimental import pallas as pl
from jax.experimental.pallas import tpu as pltpu
from jax.sharding import PartitionSpec as P

HD = 64
LANES = 128
LOG2E = 1.4426950408889634
NEG = -1e30
EPS = 1e-05
BF = jnp.bfloat16
F32 = jnp.float32
VM = pl.BlockSpec(memory_space=pltpu.VMEM)
SM = pl.BlockSpec(memory_space=pltpu.SMEM)
HB = pl.BlockSpec(memory_space=pltpu.HBM)


def dg(a, b, ca, cb):
    return lax.dot_general(a, b, (((ca,), (cb,)), ((), ())), preferred_element_type=F32)


def sds(shape, dtype):
    return jax.ShapeDtypeStruct(tuple(shape), dtype)


TIMES = dict(
    ln1=2.0, weights=1.4, qkv=2.3, attend=5.2, mid=0.4, mlp=4.0, mlpwx=4.0, mlpwo=4.0, ln2b=27.0, proj=1.4,
    attendb=7.0, qkvb=2.8, attw=2.7, ln1b=2.4, out=1.1, halve=10.0, last=10.0, join=10.0,
)
SCALE = 0.3


class Line:
    def __init__(self):
        self.last = None

    def __call__(self, kernel, name, args, outs, n_smem=0, scratch=(), limit=24, far=0, needs=()):
        args = list(args)
        after = list(needs)
        if self.last is not None:
            after.append(self.last)
        if after:
            args[-1] = lax.optimization_barrier(tuple([args[-1]] + after))[0]
        for i in range(n_smem, n_smem + far):
            args[i] = pltpu.with_memory_space_constraint(args[i], pltpu.HBM)
        fetched = args[n_smem : n_smem + far]
        total = len(args)

        def run(*refs):
            if not far:
                return kernel(*refs)
            body_refs = refs[: len(refs) - far - 1]
            bufs = refs[len(refs) - far - 1 : -1]
            sems = refs[-1]
            copies = [
                pltpu.make_async_copy(refs[n_smem + i], bufs[i], sems.at[i]) for i in range(far)
            ]
            for cp in copies:
                cp.start()
            for cp in copies:
                cp.wait()
            return kernel(*body_refs[:n_smem], *bufs, *body_refs[n_smem + far :])

        extra = []
        if far:
            extra = [pltpu.VMEM(v.shape, v.dtype) for v in fetched] + [pltpu.SemaphoreType.DMA((far,))]
        res = pl.pallas_call(
            run,
            in_specs=[SM] * n_smem + [HB] * far + [VM] * (total - n_smem - far),
            out_specs=[VM] * len(outs),
            out_shape=outs,
            scratch_shapes=list(scratch) + extra,
            compiler_params=pltpu.CompilerParams(vmem_limit_bytes=limit << 20),
            cost_estimate=pl.CostEstimate(
                flops=int(SCALE * 1.1e9 * TIMES.get(name.split("_")[0], 0.2)), transcendentals=0, bytes_accessed=1
            ),
            name=name,
        )(*args)
        self.last = res[-1]
        return res


def normalize(x):
    d = x.shape[-1]
    xc = x - jnp.sum(x, axis=-1, keepdims=True) * (1.0 / d)
    var = jnp.sum(xc * xc, axis=-1, keepdims=True) * (1.0 / d)
    r = lax.rsqrt(var + EPS)
    return xc * r, r


def norm_back(grad, z, r, gain):
    d = z.shape[-1]
    e = grad * gain
    me = jnp.sum(e, axis=-1, keepdims=True) * (1.0 / d)
    mez = jnp.sum(e * z, axis=-1, keepdims=True) * (1.0 / d)
    return (e - me - z * mez) * r


def chunked(total, size, body, carry=None):
    if total % size:
        return body(pl.ds(0, total), carry)
    return lax.fori_loop(0, total // size, lambda i, c: body(pl.ds(pl.multiple_of(i * size, size), size), c), carry)


def col_sum(x):
    return jnp.sum(x.astype(F32), axis=0, keepdims=True)


def ln1_kernel(*refs):
    vecs = refs[:6]
    fb_ref, qb_ref, tok_ref = refs[6:9]
    outs = refs[9:-2]
    small_ref, vec_ref = refs[-2:]
    vec_ref[...] = jnp.zeros(vec_ref.shape, F32)
    for i, v in enumerate(vecs):
        vec_ref[i : i + 1, :] = v[...].astype(F32).reshape(1, -1)
    for m, o_ref in enumerate(outs):
        z, _ = normalize(tok_ref[m].astype(F32))
        o_ref[...] = (z * vec_ref[1:2] + vec_ref[2:3]).astype(BF)
    small_ref[...] = jnp.zeros(small_ref.shape, F32)
    small_ref[0:1, : fb_ref.shape[0]] = fb_ref[...].astype(F32).reshape(1, -1)
    small_ref[1:3, : qb_ref.shape[1]] = qb_ref[...].astype(F32)


def weights_kernel(woo_ref, wqo_ref, so_ref, sx_ref, wox_ref, wqx_ref, qb_ref, fb_ref, wo_ref, wq_ref):
    c = lax.axis_index("tensor") & 1
    hc = woo_ref.shape[0]
    units = fb_ref.shape[1]
    fb_ref[0:1, :] = so_ref[0:1, :units]
    fb_ref[1:2, :] = sx_ref[0:1, :units]
    qb_ref[...] = jnp.zeros(qb_ref.shape, F32)

    def place(at_o, at_x):
        for at, b, o, q in ((at_o, so_ref, woo_ref, wqo_ref), (at_x, sx_ref, wox_ref, wqx_ref)):
            qb_ref[0:1, at : at + hc] = b[1:2, :hc]
            qb_ref[2:3, at : at + hc] = b[2:3, :hc]
            wo_ref[at : at + hc, :] = o[...]
            wq_ref[:, at : at + hc, :] = q[...]

    @pl.when(c == 0)
    def _():
        place(0, hc)

    @pl.when(c != 0)
    def _():
        place(hc, 0)


def qkv_kernel(b_ref, w_ref, no_ref, np_ref, qo_ref, qp_ref, kv_ref):
    rows, wide = qo_ref.shape
    for i, (n_ref, q_ref) in enumerate(((no_ref, qo_ref), (np_ref, qp_ref))):
        n = n_ref[...]
        for s in range(3):
            v = (dg(n, w_ref[s], 1, 1) + b_ref[s : s + 1]).astype(BF)
            if s == 0:
                q_ref[...] = v
            else:
                kv_ref[i * rows : (i + 1) * rows, wide * (s - 1) : wide * s] = v


def row_starts(rows):
    t = lax.axis_index("tensor")
    return [rows * t, rows * (t ^ 2), rows * (t ^ 1), rows * (t ^ 3)]


def key_bias(starts, length, rows):
    out = []
    for b in range(4):
        at = lax.broadcasted_iota(jnp.int32, (rows, LANES), 0) + starts[b]
        out.append(jnp.where(at < length, 0.0, NEG).astype(BF))
    return jnp.concatenate(out, axis=0)


def attend_kernel(m, part, len_ref, ka_ref, kb_ref, w_ref, q_ref, mixed_ref, lse_ref, term_ref):
    rows, wide = q_ref.shape
    length = len_ref[m, 0]
    starts = row_starts(rows)
    c = LOG2E / math.sqrt(HD)
    bias = key_bias(starts, length, rows)
    lane = lax.broadcasted_iota(jnp.int32, (4 * rows, LANES), 1)
    laneq = lax.broadcasted_iota(jnp.int32, (rows, LANES), 1)
    valid = lax.broadcasted_iota(jnp.int32, (rows, LANES), 0) + starts[part] < length
    kvs = (ka_ref, kb_ref)

    def pair(p, carry):
        cs = pl.ds(pl.multiple_of(LANES * p, LANES), LANES)
        vs = pl.ds(pl.multiple_of(wide + LANES * p, LANES), LANES)
        kp = jnp.concatenate([r[:, cs] for r in kvs], axis=0)
        vp = jnp.concatenate([r[:, vs] for r in kvs], axis=0)
        qp = q_ref[:, cs]
        os = []
        ls = []
        for h in range(2):
            inh = (laneq < HD) if h == 0 else (laneq >= HD)
            mark = HD * (1 - h)
            one = jnp.where(laneq == mark, 1.0, 0.0).astype(BF)
            s = dg(jnp.where(inh, qp, one), jnp.where(lane == mark, bias, kp), 1, 1)
            top = jnp.max(s, axis=1, keepdims=True)
            e = jnp.exp2((s - top) * c)
            l = jnp.sum(e, axis=1, keepdims=True)
            os.append(dg(e.astype(BF), vp, 1, 0) * (1.0 / l))
            ls.append(top * c + jnp.log2(l))
        ob = jnp.where(laneq < HD, os[0], os[1])
        lt = jnp.where(laneq < HD, ls[0], ls[1]).T
        lse_ref[pl.ds(8 * p, 1), :] = lt[0:1]
        lse_ref[pl.ds(8 * p + 1, 1), :] = lt[HD : HD + 1]
        mixed_ref[:, cs] = jnp.where(valid, ob, 0.0).astype(BF)
        return carry

    lax.fori_loop(0, wide // LANES, pair, 0)
    term_ref[...] = dg(mixed_ref[...], w_ref[...], 1, 0).astype(term_ref.dtype)


def mid_kernel(m, own_ref, rcv_ref, vec_ref, tok_ref, hid_ref, n_ref):
    h = tok_ref[m].astype(F32) + (own_ref[...] + rcv_ref[...].astype(F32)) + vec_ref[0:1]
    hid_ref[...] = h
    z, _ = normalize(h)
    n_ref[...] = (z * vec_ref[4:5] + vec_ref[5:6]).astype(BF)


def mlp_kernel(m, g_ref, fo_ref, fx_ref, bias_ref, po_ref, px_ref, n_ref, ao_ref, ax_ref, ggo_ref, ggx_ref, sum_ref, term_ref):
    n = n_ref[...]
    g = g_ref[m]
    back = None
    for j, (f_ref, p_ref, a_ref, gg_ref) in enumerate(
        ((fo_ref, po_ref, ao_ref, ggo_ref), (fx_ref, px_ref, ax_ref, ggx_ref))
    ):
        f = f_ref[...]
        gate = dg(n, f, 1, 0) + bias_ref[j : j + 1]
        q = 0.5 * jnp.tanh(0.851 * gate) + 0.5
        a_ref[...] = (gate * q).astype(BF)
        slope = q + 1.702 * gate * q * (1.0 - q)
        gg = (dg(g, p_ref[...], 1, 1) * slope).astype(BF)
        gg_ref[...] = gg
        term = dg(gg, f, 1, 1)
        back = term if back is None else back + term
        sum_ref[j : j + 1] = col_sum(gg)
    term_ref[...] = back.astype(term_ref.dtype)


def proj_kernel(count, po_ref, px_ref, *refs):
    out_ref = refs[-1]
    for m in range(count):
        out_ref[m] = (dg(refs[2 * m][...], po_ref[...], 1, 0) + dg(refs[2 * m + 1][...], px_ref[...], 1, 0)).astype(
            out_ref.dtype
        )


def ln2_back_kernel(m, hid_ref, own_ref, rcv_ref, vec_ref, grad_ref, hg_ref, st_ref, br_ref):
    st_ref[...] = jnp.zeros(st_ref.shape, F32)

    def some(at, carry):
        z, r = normalize(hid_ref[at, :])
        ng = own_ref[at, :] + rcv_ref[at, :].astype(F32)
        g = grad_ref[m, at, :].astype(F32)
        hg = g + norm_back(ng, z, r, vec_ref[4:5])
        hg_ref[at, :] = hg
        br = hg.astype(BF)
        br_ref[at, :] = br
        for i, v in enumerate((ng * z, ng, br, g)):
            st_ref[2 + i : 3 + i] = st_ref[2 + i : 3 + i] + col_sum(v)
        return carry

    chunked(br_ref.shape[0], 128, some, 0)


def attend_back_kernel(m, part, *refs):
    len_ref, ka_ref, kb_ref, w_ref, mixed_ref, lse_ref, b_ref = refs[:7]
    refs = refs[7:]
    if part:
        (acc_in, q_ref, dq_ref, out_ref, send_ref, do_ref) = refs
    else:
        (q_ref, dq_ref, acc_ref, do_ref) = refs
    rows, wide = q_ref.shape
    length = len_ref[m, 0]
    starts = row_starts(rows)
    c = LOG2E / math.sqrt(HD)
    sc = 1.0 / math.sqrt(HD)
    at = lax.broadcasted_iota(jnp.int32, (rows, wide), 0) + starts[part]
    do_ref[...] = jnp.where(at < length, dg(b_ref[...], w_ref[...], 1, 1), 0.0).astype(BF)
    bias = key_bias(starts, length, rows)
    laneq = lax.broadcasted_iota(jnp.int32, (rows, LANES), 1)
    zero = jnp.zeros((), BF)
    kvs = (ka_ref, kb_ref)
    blocks = 2 if part else 1
    size = 4 * rows // blocks
    lane = lax.broadcasted_iota(jnp.int32, (size, LANES), 1)

    def pair(p, carry):
        cs = pl.ds(pl.multiple_of(LANES * p, LANES), LANES)
        vs = pl.ds(pl.multiple_of(wide + LANES * p, LANES), LANES)
        qp = q_ref[:, cs]
        dop = do_ref[:, cs]
        prod = (dop.astype(F32) * mixed_ref[:, cs].astype(F32)).T
        dqt = [None, None]
        for j in range(blocks):
            mine = kvs if blocks == 1 else kvs[j : j + 1]
            kp = jnp.concatenate([r[:, cs] for r in mine], axis=0)
            vp = jnp.concatenate([r[:, vs] for r in mine], axis=0)
            bj = bias[size * j : size * (j + 1)]
            kt = kp.T
            dk = None
            dv = None
            for h in range(2):
                inh = (laneq < HD) if h == 0 else (laneq >= HD)
                mark = HD * (1 - h)
                qz = jnp.where(inh, qp, zero)
                qh = jnp.where(laneq == mark, jnp.ones((), BF), qz)
                doh = jnp.where(inh, dop, zero)
                st = dg(jnp.where(lane == mark, bj, kp), qh, 1, 1)
                pt = jnp.exp2(st * c - lse_ref[pl.ds(8 * p + h, 1), :])
                dpt = dg(vp, doh, 1, 1)
                row = jnp.sum(prod[HD * h : HD * (h + 1)], axis=0, keepdims=True)
                ds = (pt * (dpt - row)).astype(BF)
                dvh = dg(pt.astype(BF), doh, 1, 0)
                dkh = dg(ds, qz, 1, 0)
                t = dg(kt[HD * h : HD * (h + 1)], ds, 1, 0)
                dqt[h] = t if dqt[h] is None else dqt[h] + t
                dv = dvh if dv is None else dv + dvh
                dk = dkh if dk is None else dk + dkh
            dk = dk * sc
            if part:
                at = slice(size * j, size * (j + 1))
                dk = dk + acc_in[at, cs]
                dv = dv + acc_in[at, vs]
                o_ref = send_ref if j else out_ref
                o_ref[:, cs] = dk.astype(o_ref.dtype)
                o_ref[:, vs] = dv.astype(o_ref.dtype)
            else:
                acc_ref[:, cs] = dk
                acc_ref[:, vs] = dv
        dq_ref[:, cs] = (jnp.concatenate(dqt, axis=0).T * sc).astype(BF)
        return carry

    lax.fori_loop(0, wide // LANES, pair, 0)


def qkv_back_kernel(count, *refs):
    w_ref = refs[0]
    ins = refs[1 : 1 + 4 * count]
    outs = refs[1 + 4 * count :]
    ngr_ref = outs[-1]
    sum_ref = outs[-2]
    rows = ngr_ref.shape[1]
    sq = None
    sv = None
    for m in range(count):
        dqo_ref, dqp_ref, own_ref, rcv_ref = ins[4 * m : 4 * m + 4]
        dkv_ref, ngo_ref = outs[2 * m : 2 * m + 2]
        wide = dqo_ref.shape[1]
        for i, dq_ref in ((1, dqp_ref), (0, dqo_ref)):
            at = slice(i * rows, (i + 1) * rows)
            dkv = (own_ref[at, :] + rcv_ref[at, :].astype(F32)).astype(BF)
            dkv_ref[at, :] = dkv
            dq = dq_ref[...]
            ng = dg(dq, w_ref[0], 1, 0) + dg(dkv[:, :wide], w_ref[1], 1, 0) + dg(dkv[:, wide:], w_ref[2], 1, 0)
            if i:
                ngr_ref[m] = ng.astype(BF)
            else:
                ngo_ref[...] = ng
            cq = col_sum(dq)
            cv = col_sum(dkv[:, wide:])
            sq = cq if sq is None else sq + cq
            sv = cv if sv is None else sv + cv
    sum_ref[0:1] = sq
    sum_ref[1:2] = sv


def ln1_back_kernel(count, *refs):
    tok_ref = refs[0]
    vec_ref = refs[1]
    hgs = refs[2 : 2 + count]
    owns = refs[2 + count : 2 + 2 * count]
    rcv_ref, ig_ref, st_ref = refs[2 + 2 * count :]
    st_ref[...] = jnp.zeros(st_ref.shape, F32)
    for m in range(count):

        def some(at, carry, m=m):
            z, r = normalize(tok_ref[m, at, :].astype(F32))
            ng = owns[m][at, :] + rcv_ref[m, at, :].astype(F32)
            ig_ref[m, at, :] = hgs[m][at, :] + norm_back(ng, z, r, vec_ref[1:2])
            for i, v in enumerate((ng * z, ng)):
                st_ref[i : i + 1] = st_ref[i : i + 1] + col_sum(v)
            return carry

        chunked(tok_ref.shape[1], 128, some, 0)


def out_kernel(count, vec_ref, *refs):
    hids = refs[:count]
    own_ref, rcv_ref, o_ref = refs[count:]
    for m in range(count):
        o_ref[m] = (hids[m][...] + (own_ref[m] + rcv_ref[m].astype(F32)) + vec_ref[3:4]).astype(BF)


def rows_product(pairs):
    acc = None
    for a, b in pairs:
        t = dg(a, b, 0, 0)
        acc = t if acc is None else acc + t
    return acc


def mlp_weights_kernel(count, *refs):
    n = 2 * count
    acts = refs[:n]
    gates = refs[n : 2 * n]
    norms = refs[2 * n : 3 * n]
    go_ref, gp_ref, pj_ref, fc_ref = refs[3 * n :]
    gs = []
    for m in range(count):
        gs += [go_ref[m], gp_ref[m]]
    pj_ref[...] = rows_product([(a[...], g) for a, g in zip(acts, gs)]).astype(pj_ref.dtype)
    fc_ref[...] = rows_product([(a[...], b[...]) for a, b in zip(norms, gates)]).astype(fc_ref.dtype)


def attend_weights_kernel(count, *refs):
    n = 2 * count
    dqs = refs[:n]
    norms = refs[n : 2 * n]
    mixes = refs[2 * n : 3 * n]
    brs = refs[3 * n : 4 * n]
    dkvs = refs[4 * n : 4 * n + count]
    outs = refs[4 * n + count :]
    c = lax.axis_index("tensor") & 1
    rows, wide = dqs[0].shape
    hc = wide // 2
    ns = [r[...] for r in norms]
    full = [jnp.concatenate(ns[2 * m : 2 * m + 2], axis=0) for m in range(count)]
    pieces = [
        rows_product([(a[...], b) for a, b in zip(dqs, ns)]),
        rows_product([(a[:, :wide], b) for a, b in zip(dkvs, full)]),
        rows_product([(a[:, wide:], b) for a, b in zip(dkvs, full)]),
        rows_product([(a[...], b[...]) for a, b in zip(mixes, brs)]),
    ]
    for i, p in enumerate(pieces):
        own_ref, send_ref = outs[2 * (i // 2) : 2 * (i // 2) + 2]
        at = slice((i % 2) * hc, (i % 2 + 1) * hc)
        low = p[:hc]
        high = p[hc:]
        own_ref[at, :] = jnp.where(c == 0, low, high)
        send_ref[at, :] = jnp.where(c == 0, high, low).astype(BF)


def add_kernel(rcv_ref, own_ref, out_ref):
    out_ref[...] = (own_ref[...].astype(F32) + rcv_ref[...].astype(F32)).astype(out_ref.dtype)


def halve_kernel(bit, rcv_ref, own_ref, keep_ref, send_ref):
    r = keep_ref.shape[0]
    b = (lax.axis_index("dp") >> bit) & 1
    mine = pl.ds(pl.multiple_of(b * r, r), r)
    other = pl.ds(pl.multiple_of((1 - b) * r, r), r)
    send_ref[...] = (own_ref[other, :].astype(F32) + rcv_ref[other, :].astype(F32)).astype(BF)
    keep_ref[...] = own_ref[mine, :].astype(F32) + rcv_ref[mine, :].astype(F32)


def join_kernel(bit, rcv_ref, own_ref, out_ref):
    r = own_ref.shape[0]
    b = (lax.axis_index("dp") >> bit) & 1
    out_ref[pl.ds(pl.multiple_of(b * r, r), r), :] = own_ref[...].astype(out_ref.dtype)
    out_ref[pl.ds(pl.multiple_of((1 - b) * r, r), r), :] = rcv_ref[...].astype(out_ref.dtype)


def join_both_kernel(bit, rcv_a, own_a, rcv_b, own_b, qkv_ref, out_ref):
    r = own_a.shape[0]
    b = (lax.axis_index("dp") >> bit) & 1
    qkv_ref[pl.ds(pl.multiple_of(b * r, r), r), :] = own_a[...].astype(F32)
    qkv_ref[pl.ds(pl.multiple_of((1 - b) * r, r), r), :] = rcv_a[...].astype(F32)

    @pl.when(b == 0)
    def _():
        qkv_ref[2 * r :, :] = own_b[...].astype(F32)
        out_ref[...] = rcv_b[...].astype(F32)

    @pl.when(b != 0)
    def _():
        qkv_ref[2 * r :, :] = rcv_b[...].astype(F32)
        out_ref[...] = own_b[...].astype(F32)


def stats_kernel(count, *refs):
    lst2 = refs[:count]
    fsums = refs[count : 3 * count]
    q_ref, lst1_ref, own_ref, send_ref = refs[3 * count :]
    c = lax.axis_index("tensor") & 1
    common = lst1_ref[...]
    for r in lst2:
        common = common + r[...]
    f = fsums[0][...]
    for r in fsums[1:]:
        f = f + r[...]
    q = q_ref[...]
    wide = own_ref.shape[1]
    hc = q.shape[1] // 2
    qpad = jnp.zeros((1, wide - 2 * hc), F32)
    low = jnp.concatenate([q[0:1, :hc], q[1:2, :hc], qpad], axis=1)
    high = jnp.concatenate([q[0:1, hc:], q[1:2, hc:], qpad], axis=1)
    own_ref[...] = common
    send_ref[...] = common
    own_ref[6:7] = jnp.where(c == 0, low, high)
    send_ref[6:7] = jnp.where(c == 0, high, low)
    own_ref[7:8] = f[0:1]
    send_ref[7:8] = f[1:2]


def spread_kernel(rcv_ref, own_ref, fb_ref, qb_ref, *outs):
    at = lax.broadcasted_iota(jnp.int32, own_ref.shape, 0)
    total = own_ref[...] + jnp.where(at < 6, rcv_ref[...], 0.0)
    for i, o_ref in enumerate(outs):
        o_ref[...] = total[i : i + 1].reshape(o_ref.shape)
    hc = qb_ref.shape[1]
    qb_ref[0:1, :] = total[6:7, :hc]
    qb_ref[1:2, :] = total[6:7, hc : 2 * hc]
    fb_ref[...] = total[7:8, : fb_ref.shape[0]].reshape(fb_ref.shape)


def body(
    tokens, qkv_weight, qv_bias, out_weight, out_bias, ln1_gain, ln1_shift, fc_weight, fc_bias,
    proj_weight, proj_bias, ln2_gain, ln2_shift, seq_lengths, out_grad,
):
    batches, rows, width = tokens.shape
    hc = out_weight.shape[0]
    wide = 2 * hc
    units = fc_weight.shape[1]
    tsize = lax.axis_size("tensor")
    dsize = lax.axis_size("dp")
    bits = dsize.bit_length() - 1
    cpairs = [(i, i ^ 1) for i in range(tsize)]
    ypairs = [(i, i ^ 2) for i in range(tsize)]
    mb = range(batches)
    line = Line()

    def core(v):
        return lax.ppermute(v, "tensor", cpairs)

    def across(v):
        return lax.ppermute(v, "tensor", ypairs)

    def swap(v, b):
        return lax.ppermute(v, "dp", [(i, i ^ (1 << b)) for i in range(dsize)])

    def after(v, *deps):
        return lax.optimization_barrier((v,) + deps)[0]

    def kernel_of(f, *static):
        def kernel(*refs):
            f(*static, *refs)

        return kernel

    def halve(own, rcv, b, name, **kw):
        size = own.shape[0] // 2
        if size % 16:
            both = own.astype(F32) + rcv.astype(F32)
            both = both.reshape((2, size) + own.shape[1:])
            bit = (lax.axis_index("dp") >> b) & 1
            keep = lax.dynamic_index_in_dim(both, bit, 0, keepdims=False)
            return keep, lax.dynamic_index_in_dim(both, 1 - bit, 0, keepdims=False).astype(BF)
        shape = (size,) + own.shape[1:]
        return line(kernel_of(halve_kernel, b), "halve_" + name, [rcv, own], [sds(shape, F32), sds(shape, BF)], **kw)

    def join(piece, rcv, b, dtype, name, kind="join_"):
        size = piece.shape[0]
        if size % 16:
            low = ((lax.axis_index("dp") >> b) & 1) == 0
            return jnp.concatenate([jnp.where(low, piece, rcv), jnp.where(low, rcv, piece)], axis=0).astype(dtype)
        shape = (2 * size,) + piece.shape[1:]
        return line(kernel_of(join_kernel, b), kind + name, [rcv, piece], [sds(shape, dtype)])[0]

    class Sum:
        def __init__(self, own, rcv, name, turn=0):
            self.own, self.rcv, self.name, self.at = own, rcv, name, 0
            self.order = [(b + turn) % bits for b in range(bits)]

        def go(self, **kw):
            k = self.at
            self.at += 1
            if k > 2 * bits:
                return
            if k < bits:
                self.own, send = halve(self.own, self.rcv, self.order[k], self.name, **kw)
            elif k == bits:
                send = line(add_kernel, "last_" + self.name, [self.rcv, self.own], [sds(self.own.shape, BF)], **kw)[0]
                self.own = send
            else:
                b = self.order[2 * bits - k]
                final = k == 2 * bits
                kind = "final_" if final and self.name == "f" else "join_"
                send = join(self.own, self.rcv, b, F32 if final else BF, self.name, kind)
                self.own = send
            if k < 2 * bits:
                self.rcv = swap(send, self.order[k if k < bits else 2 * bits - 1 - k])

        def finish(self):
            while self.at <= 2 * bits:
                self.go()
            return self.own

    wq_o = jnp.transpose(qkv_weight, (1, 2, 0))
    wq_x = core(wq_o)
    wo_x = core(out_weight)

    packed = (8, max(units, width))
    *normed, small, vec = line(
        ln1_kernel, "ln1",
        [out_bias, ln1_gain, ln1_shift, proj_bias, ln2_gain, ln2_shift, fc_bias, qv_bias, tokens],
        [sds((rows, width), BF)] * batches + [sds(packed, F32), sds((8, width), F32)], far=9,
    )
    normed_p = [across(v) for v in normed]
    qb, fb, wo, wq = line(
        weights_kernel, "weights", [out_weight, wq_o, small, core(small), wo_x, wq_x],
        [sds((3, wide), F32), sds((2, units), F32), sds((wide, width), BF), sds((3, wide, width), BF)], far=2,
    )

    q = [[None, None] for _ in mb]
    kv = [[None, None] for _ in mb]

    def qkv(m, **kw):
        q[m][0], q[m][1], kv[m][0] = line(
            qkv_kernel, "qkv", [qb, wq, normed[m], normed_p[m]],
            [sds((rows, wide), BF)] * 2 + [sds((2 * rows, 2 * wide), BF)], **kw,
        )
        kv[m][1] = core(kv[m][0])

    mixed = [[None, None] for _ in mb]
    lse = [[None, None] for _ in mb]
    own = [None for _ in mb]
    rcv = [None for _ in mb]
    lse_rows = 8 * (wide // LANES)

    def attend(m, part, **kw):
        mixed[m][part], lse[m][part], term = line(
            kernel_of(attend_kernel, m, part), "attend", [seq_lengths] + kv[m] + [wo, q[m][part]],
            [sds((rows, wide), BF), sds((lse_rows, rows), F32), sds((rows, width), BF if part else F32)],
            n_smem=1, **kw,
        )
        if part:
            rcv[m] = across(term)
        else:
            own[m] = term

    hid = [None for _ in mb]
    n2 = [[None, None] for _ in mb]

    def mid(m, **kw):
        hid[m], n2[m][0] = line(
            kernel_of(mid_kernel, m), "mid", [own[m], rcv[m], vec, tokens],
            [sds((rows, width), F32), sds((rows, width), BF)], **kw,
        )
        n2[m][1] = across(n2[m][0])

    acts = [[None, None] for _ in mb]
    gates = [[None, None] for _ in mb]
    fsum = [[None, None] for _ in mb]
    nown = [None for _ in mb]
    nrcv = [None for _ in mb]

    def mlp(m, part, **kw):
        a_o, a_x, g_o, g_x, fsum[m][part], term = line(
            kernel_of(mlp_kernel, m), "mlp",
            [grads_p if part else out_grad, fc_weight, fc_x, fb, proj_weight, pj_x, n2[m][part]],
            [sds((rows, units), BF)] * 4 + [sds((2, units), F32), sds((rows, width), BF if part else F32)], **kw,
        )
        acts[m][part] = (a_o, a_x)
        gates[m][part] = (g_o, g_x)
        if part:
            nrcv[m] = across(term)
        else:
            nown[m] = term

    flat = [(m, part) for m in mb for part in range(2)]

    def mlp_weights(k, dtype, name, **kw):
        return line(
            kernel_of(mlp_weights_kernel, batches), name,
            [acts[m][i][k] for m, i in flat] + [gates[m][i][k] for m, i in flat] + [n2[m][i] for m, i in flat]
            + [out_grad, grads_p],
            [sds((units, width), dtype), sds((width, units), dtype)], **kw,
        )

    hg = [None for _ in mb]
    st2 = [None for _ in mb]
    br = [[None, None] for _ in mb]

    def ln2_back(m, **kw):
        hg[m], st2[m], br[m][0] = line(
            kernel_of(ln2_back_kernel, m), "ln2b", [hid[m], nown[m], nrcv[m], vec, out_grad],
            [sds((rows, width), F32), sds((8, width), F32), sds((rows, width), BF)], **kw,
        )
        br[m][1] = across(br[m][0])

    def proj(part, **kw):
        return line(
            kernel_of(proj_kernel, batches), "proj",
            [proj_weight, pj_x] + [acts[m][part][k] for m in mb for k in range(2)],
            [sds((batches, rows, width), BF if part else F32)], **kw,
        )[0]

    dq = [[None, None] for _ in mb]
    acc = [None for _ in mb]
    dkvo = [None for _ in mb]
    dkvr = [None for _ in mb]
    dkvs = [None for _ in mb]

    def attend_back(m, part, **kw):
        args = [seq_lengths] + kv[m] + [wo, mixed[m][part], lse[m][part], br[m][part]]
        scratch = [pltpu.VMEM((rows, wide), BF)]
        if part:
            dq[m][1], dkvo[m], send = line(
                kernel_of(attend_back_kernel, m, 1), "attendb", args + [acc[m], q[m][1]],
                [sds((rows, wide), BF), sds((2 * rows, 2 * wide), F32), sds((2 * rows, 2 * wide), BF)],
                n_smem=1, scratch=scratch, **kw,
            )
            dkvs[m] = send
        else:
            dq[m][0], acc[m] = line(
                kernel_of(attend_back_kernel, m, 0), "attendb", args + [q[m][0]],
                [sds((rows, wide), BF), sds((4 * rows, 2 * wide), F32)],
                n_smem=1, scratch=scratch, **kw,
            )

    def qkv_back(**kw):
        args = [wq]
        for m in mb:
            args += [dq[m][0], dq[m][1], dkvo[m], dkvr[m]]
        *res, qsum, rem = line(
            kernel_of(qkv_back_kernel, batches), "qkvb", args,
            [sds((2 * rows, 2 * wide), BF), sds((rows, width), F32)] * batches
            + [sds((2, wide), F32), sds((batches, rows, width), BF)], **kw,
        )
        return res[0::2], res[1::2], qsum, rem

    last = batches - 1
    qkv(0)
    fc_x = core(after(fc_weight, q[0][0]))
    pj_x = core(after(proj_weight, q[0][0]))
    grads_p = across(after(out_grad, q[0][0]))
    for m in mb[1:]:
        qkv(m)
    attend(0, 1)
    attend(1, 1)
    attend(0, 0, needs=[grads_p])
    attend(1, 0)
    mid(0)
    mid(1)
    mlp(0, 0)
    mlp(1, 0)
    mlp(0, 1)
    mlp(1, 1)
    pj_send, fc_send = mlp_weights(1, BF, "mlpwx")
    pj_own, fc_own = mlp_weights(0, F32, "mlpwo")
    ln2_back(0)
    ln2_back(1)
    pj_back = core(pj_send)
    fc_back = core(fc_send)
    p_sum = Sum(pj_own, pj_back, "p")
    f_sum = Sum(fc_own, fc_back, "f")
    p_sum.go()
    pown = proj(0)
    psend = proj(1)
    attend_back(0, 0)
    attend_back(1, 0)
    f_sum.go(needs=[br[m][1] for m in mb])
    p_sum.go()
    prcv = across(after(psend, p_sum.own))
    attend_back(0, 1)
    p_sum.go()
    attend_back(1, 1)
    p_sum.go(needs=[prcv])
    f_sum.go()
    for m in mb:
        dkvr[m] = core(after(dkvs[m], f_sum.own))
    dkv, ngo, qsum, ngs = qkv_back()

    both = [normed, normed_p]
    a1_own, a1_send, a2_own, a2_send = line(
        kernel_of(attend_weights_kernel, batches), "attw",
        [dq[m][i] for m, i in flat] + [both[i][m] for m, i in flat] + [mixed[m][i] for m, i in flat]
        + [br[m][i] for m, i in flat] + dkv,
        [sds((2 * hc, width), F32), sds((2 * hc, width), BF)] * 2,
        limit=32,
    )
    ngr = across(after(ngs, a2_send))
    a_sum = Sum(a1_own, core(a1_send), "a")
    b_sum = Sum(a2_own, core(a2_send), "b")
    p_sum.go()
    f_sum.go()
    a_sum.go()
    b_sum.go()
    layer_out = line(
        kernel_of(out_kernel, batches), "out", [vec] + hid + [pown, prcv], [sds((batches, rows, width), BF)],
    )[0]
    p_sum.go()
    f_sum.go()
    a_sum.go()
    b_sum.go()
    a_sum.go()
    f_sum.go()
    ig, st1 = line(
        kernel_of(ln1_back_kernel, batches), "ln1b", [tokens, vec] + hg + ngo + [ngr],
        [sds((batches, rows, width), F32), sds((8, width), F32)],
    )
    b_sum.go()
    s_own, s_send = line(
        kernel_of(stats_kernel, batches), "stats",
        st2 + [fsum[m][i] for m, i in flat] + [qsum, st1],
        [sds((8, width), F32), sds((8, width), F32)],
    )
    s_rcv = core(s_send)
    a_sum.go()

    def stat():
        return line(add_kernel, "stat", [s_rcv, stats], [sds((8, width), F32)])[0]

    stats = s_own
    stats = stat()
    s_rcv = swap(stats, 0)
    f_sum.go()
    p_sum.finish()
    b_sum.go()
    a_sum.go()
    for b in range(1, bits):
        stats = stat()
        s_rcv = swap(stats, b)
        for chain in (b_sum, a_sum):
            if chain.at < 2 * bits:
                chain.go()
    stats = stat()
    s_rcv = across(stats)
    for chain in (a_sum, b_sum):
        while chain.at < 2 * bits:
            chain.go()
    f_sum.finish()
    vector = sds((width,), F32)
    fb_grad, qb_grad, *vectors = line(
        spread_kernel, "spread", [s_rcv, stats],
        [sds((units,), F32), sds((2, hc), F32)] + [vector] * 6,
    )
    qkv_grad, out_grad_w = line(
        kernel_of(join_both_kernel, a_sum.order[0]), "join_ab", [a_sum.rcv, a_sum.own, b_sum.rcv, b_sum.own],
        [sds((3 * hc, width), F32), sds((hc, width), F32)],
    )
    fc_grad = f_sum.own
    pj_grad = p_sum.own

    return (
        layer_out,
        ig,
        jnp.transpose(qkv_grad.reshape(3, hc, width), (2, 0, 1)),
        qb_grad,
        out_grad_w,
        vectors[4],
        vectors[0],
        vectors[1],
        fc_grad,
        fb_grad,
        pj_grad,
        vectors[5],
        vectors[2],
        vectors[3],
    )


def solution(mesh):
    placed = (
        P(None, ("dp", "tensor"), None),
        P(None, None, "tensor"),
        P(None, "tensor"),
        P("tensor", None),
        P(),
        P(),
        P(),
        P(None, "tensor"),
        P("tensor"),
        P("tensor", None),
        P(),
        P(),
        P(),
        P(None, "dp"),
        P(None, ("dp", "tensor"), None),
    )
    return jax.shard_map(
        body,
        mesh=mesh,
        in_specs=placed,
        out_specs=(
            P(None, ("dp", "tensor"), None),
            P(None, ("dp", "tensor"), None),
            P(None, None, "tensor"),
            P(None, "tensor"),
            P("tensor", None),
            P(),
            P(),
            P(),
            P(None, "tensor"),
            P("tensor"),
            P("tensor", None),
            P(),
            P(),
            P(),
        ),
        check_vma=False,
    )
```

```python
import math

import jax
import jax.numpy as jnp
from jax import lax
from jax.experimental import pallas as pl
from jax.experimental.pallas import tpu as pltpu
from jax.sharding import PartitionSpec as P

HD = 64
LANES = 128
LOG2E = 1.4426950408889634
NEG = -1e30
EPS = 1e-05
BF = jnp.bfloat16
F32 = jnp.float32
VM = pl.BlockSpec(memory_space=pltpu.VMEM)
SM = pl.BlockSpec(memory_space=pltpu.SMEM)
HB = pl.BlockSpec(memory_space=pltpu.HBM)


def dg(a, b, ca, cb):
    return lax.dot_general(a, b, (((ca,), (cb,)), ((), ())), preferred_element_type=F32)


def sds(shape, dtype):
    return jax.ShapeDtypeStruct(tuple(shape), dtype)


TIMES = dict(
    ln1=2.0, weights=1.4, qkv=2.3, attend=5.2, mid=0.4, mlp=4.0, mlpwx=4.0, mlpwo=4.0, ln2b=27.0, proj=1.4,
    attendb=7.0, qkvb=2.8, attw=2.7, ln1b=2.4, out=1.1, halve=10.0, last=10.0, join=10.0,
)
SCALE = 0.3


class Line:
    def __init__(self):
        self.last = None

    def __call__(self, kernel, name, args, outs, n_smem=0, scratch=(), limit=24, far=0, needs=()):
        args = list(args)
        after = list(needs)
        if self.last is not None:
            after.append(self.last)
        if after:
            args[-1] = lax.optimization_barrier(tuple([args[-1]] + after))[0]
        for i in range(n_smem, n_smem + far):
            args[i] = pltpu.with_memory_space_constraint(args[i], pltpu.HBM)
        fetched = args[n_smem : n_smem + far]
        total = len(args)

        def run(*refs):
            if not far:
                return kernel(*refs)
            body_refs = refs[: len(refs) - far - 1]
            bufs = refs[len(refs) - far - 1 : -1]
            sems = refs[-1]
            copies = [
                pltpu.make_async_copy(refs[n_smem + i], bufs[i], sems.at[i]) for i in range(far)
            ]
            for cp in copies:
                cp.start()
            for cp in copies:
                cp.wait()
            return kernel(*body_refs[:n_smem], *bufs, *body_refs[n_smem + far :])

        extra = []
        if far:
            extra = [pltpu.VMEM(v.shape, v.dtype) for v in fetched] + [pltpu.SemaphoreType.DMA((far,))]
        res = pl.pallas_call(
            run,
            in_specs=[SM] * n_smem + [HB] * far + [VM] * (total - n_smem - far),
            out_specs=[VM] * len(outs),
            out_shape=outs,
            scratch_shapes=list(scratch) + extra,
            compiler_params=pltpu.CompilerParams(vmem_limit_bytes=limit << 20),
            cost_estimate=pl.CostEstimate(
                flops=int(SCALE * 1.1e9 * TIMES.get(name.split("_")[0], 0.2)), transcendentals=0, bytes_accessed=1
            ),
            name=name,
        )(*args)
        self.last = res[-1]
        return res


def normalize(x):
    d = x.shape[-1]
    xc = x - jnp.sum(x, axis=-1, keepdims=True) * (1.0 / d)
    var = jnp.sum(xc * xc, axis=-1, keepdims=True) * (1.0 / d)
    r = lax.rsqrt(var + EPS)
    return xc * r, r


def norm_back(grad, z, r, gain):
    d = z.shape[-1]
    e = grad * gain
    me = jnp.sum(e, axis=-1, keepdims=True) * (1.0 / d)
    mez = jnp.sum(e * z, axis=-1, keepdims=True) * (1.0 / d)
    return (e - me - z * mez) * r


def chunked(total, size, body, carry=None):
    if total % size:
        return body(pl.ds(0, total), carry)
    return lax.fori_loop(0, total // size, lambda i, c: body(pl.ds(pl.multiple_of(i * size, size), size), c), carry)


def col_sum(x):
    return jnp.sum(x.astype(F32), axis=0, keepdims=True)


def ln1_kernel(*refs):
    vecs = refs[:6]
    fb_ref, qb_ref, tok_ref = refs[6:9]
    outs = refs[9:-2]
    small_ref, vec_ref = refs[-2:]
    vec_ref[...] = jnp.zeros(vec_ref.shape, F32)
    for i, v in enumerate(vecs):
        vec_ref[i : i + 1, :] = v[...].astype(F32).reshape(1, -1)
    for m, o_ref in enumerate(outs):
        z, _ = normalize(tok_ref[m].astype(F32))
        o_ref[...] = (z * vec_ref[1:2] + vec_ref[2:3]).astype(BF)
    small_ref[...] = jnp.zeros(small_ref.shape, F32)
    small_ref[0:1, : fb_ref.shape[0]] = fb_ref[...].astype(F32).reshape(1, -1)
    small_ref[1:3, : qb_ref.shape[1]] = qb_ref[...].astype(F32)


def weights_kernel(woo_ref, wqo_ref, so_ref, sx_ref, wox_ref, wqx_ref, qb_ref, fb_ref, wo_ref, wq_ref):
    c = lax.axis_index("tensor") & 1
    hc = woo_ref.shape[0]
    units = fb_ref.shape[1]
    fb_ref[0:1, :] = so_ref[0:1, :units]
    fb_ref[1:2, :] = sx_ref[0:1, :units]
    qb_ref[...] = jnp.zeros(qb_ref.shape, F32)

    def place(at_o, at_x):
        for at, b, o, q in ((at_o, so_ref, woo_ref, wqo_ref), (at_x, sx_ref, wox_ref, wqx_ref)):
            qb_ref[0:1, at : at + hc] = b[1:2, :hc]
            qb_ref[2:3, at : at + hc] = b[2:3, :hc]
            wo_ref[at : at + hc, :] = o[...]
            wq_ref[:, at : at + hc, :] = q[...]

    @pl.when(c == 0)
    def _():
        place(0, hc)

    @pl.when(c != 0)
    def _():
        place(hc, 0)


def qkv_kernel(b_ref, w_ref, no_ref, np_ref, qo_ref, qp_ref, kv_ref):
    rows, wide = qo_ref.shape
    for i, (n_ref, q_ref) in enumerate(((no_ref, qo_ref), (np_ref, qp_ref))):
        n = n_ref[...]
        for s in range(3):
            v = (dg(n, w_ref[s], 1, 1) + b_ref[s : s + 1]).astype(BF)
            if s == 0:
                q_ref[...] = v
            else:
                kv_ref[i * rows : (i + 1) * rows, wide * (s - 1) : wide * s] = v


def row_starts(rows):
    t = lax.axis_index("tensor")
    return [rows * t, rows * (t ^ 2), rows * (t ^ 1), rows * (t ^ 3)]


def key_bias(starts, length, rows):
    out = []
    for b in range(4):
        at = lax.broadcasted_iota(jnp.int32, (rows, LANES), 0) + starts[b]
        out.append(jnp.where(at < length, 0.0, NEG).astype(BF))
    return jnp.concatenate(out, axis=0)


def attend_kernel(m, part, len_ref, ka_ref, kb_ref, w_ref, q_ref, mixed_ref, lse_ref, term_ref):
    rows, wide = q_ref.shape
    length = len_ref[m, 0]
    starts = row_starts(rows)
    c = LOG2E / math.sqrt(HD)
    bias = key_bias(starts, length, rows)
    lane = lax.broadcasted_iota(jnp.int32, (4 * rows, LANES), 1)
    laneq = lax.broadcasted_iota(jnp.int32, (rows, LANES), 1)
    valid = lax.broadcasted_iota(jnp.int32, (rows, LANES), 0) + starts[part] < length
    kvs = (ka_ref, kb_ref)

    def head(at, carry):
        p = at >> 1
        h = at & 1
        cs = pl.ds(pl.multiple_of(LANES * p, LANES), LANES)
        vs = pl.ds(pl.multiple_of(wide + LANES * p, LANES), LANES)
        kp = jnp.concatenate([r[:, cs] for r in kvs], axis=0)
        vp = jnp.concatenate([r[:, vs] for r in kvs], axis=0)
        inh = (laneq // HD) == h
        mark = HD * (1 - h)
        one = jnp.where(laneq == mark, 1.0, 0.0).astype(BF)
        s = dg(jnp.where(inh, q_ref[:, cs], one), jnp.where(lane == mark, bias, kp), 1, 1)
        top = jnp.max(s, axis=1, keepdims=True)
        e = jnp.exp2((s - top) * c)
        l = jnp.sum(e, axis=1, keepdims=True)
        o = dg(e.astype(BF), vp, 1, 0) * (1.0 / l)
        lt = jnp.broadcast_to(top * c + jnp.log2(l), o.shape).T
        lse_ref[pl.ds(8 * p + h, 1), :] = lt[0:1]
        mixed_ref[:, cs] = jnp.where(inh, jnp.where(valid, o, 0.0).astype(BF), mixed_ref[:, cs])
        return carry

    lax.fori_loop(0, wide // HD, head, 0)
    term_ref[...] = dg(mixed_ref[...], w_ref[...], 1, 0).astype(term_ref.dtype)


def mid_kernel(m, own_ref, rcv_ref, vec_ref, tok_ref, hid_ref, n_ref):
    h = tok_ref[m].astype(F32) + (own_ref[...] + rcv_ref[...].astype(F32)) + vec_ref[0:1]
    hid_ref[...] = h
    z, _ = normalize(h)
    n_ref[...] = (z * vec_ref[4:5] + vec_ref[5:6]).astype(BF)


def mlp_kernel(m, g_ref, fo_ref, fx_ref, bias_ref, po_ref, px_ref, n_ref, ao_ref, ax_ref, ggo_ref, ggx_ref, sum_ref, term_ref):
    n = n_ref[...]
    g = g_ref[m]
    back = None
    for j, (f_ref, p_ref, a_ref, gg_ref) in enumerate(
        ((fo_ref, po_ref, ao_ref, ggo_ref), (fx_ref, px_ref, ax_ref, ggx_ref))
    ):
        f = f_ref[...]
        gate = dg(n, f, 1, 0) + bias_ref[j : j + 1]
        q = 0.5 * jnp.tanh(0.851 * gate) + 0.5
        a_ref[...] = (gate * q).astype(BF)
        slope = q + 1.702 * gate * q * (1.0 - q)
        gg = (dg(g, p_ref[...], 1, 1) * slope).astype(BF)
        gg_ref[...] = gg
        term = dg(gg, f, 1, 1)
        back = term if back is None else back + term
        sum_ref[j : j + 1] = col_sum(gg)
    term_ref[...] = back.astype(term_ref.dtype)


def proj_kernel(count, po_ref, px_ref, *refs):
    out_ref = refs[-1]
    for m in range(count):
        out_ref[m] = (dg(refs[2 * m][...], po_ref[...], 1, 0) + dg(refs[2 * m + 1][...], px_ref[...], 1, 0)).astype(
            out_ref.dtype
        )


def ln2_back_kernel(m, hid_ref, own_ref, rcv_ref, vec_ref, grad_ref, hg_ref, st_ref, br_ref):
    st_ref[...] = jnp.zeros(st_ref.shape, F32)

    def some(at, carry):
        z, r = normalize(hid_ref[at, :])
        ng = own_ref[at, :] + rcv_ref[at, :].astype(F32)
        g = grad_ref[m, at, :].astype(F32)
        hg = g + norm_back(ng, z, r, vec_ref[4:5])
        hg_ref[at, :] = hg
        br = hg.astype(BF)
        br_ref[at, :] = br
        for i, v in enumerate((ng * z, ng, br, g)):
            st_ref[2 + i : 3 + i] = st_ref[2 + i : 3 + i] + col_sum(v)
        return carry

    chunked(br_ref.shape[0], 128, some, 0)


def attend_back_kernel(m, part, *refs):
    len_ref, ka_ref, kb_ref, w_ref, mixed_ref, lse_ref, b_ref = refs[:7]
    refs = refs[7:]
    if part:
        (acc_in, q_ref, dq_ref, out_ref, send_ref, do_ref) = refs
    else:
        (q_ref, dq_ref, acc_ref, do_ref) = refs
    rows, wide = q_ref.shape
    length = len_ref[m, 0]
    starts = row_starts(rows)
    c = LOG2E / math.sqrt(HD)
    sc = 1.0 / math.sqrt(HD)
    at = lax.broadcasted_iota(jnp.int32, (rows, wide), 0) + starts[part]
    do_ref[...] = jnp.where(at < length, dg(b_ref[...], w_ref[...], 1, 1), 0.0).astype(BF)
    bias = key_bias(starts, length, rows)
    laneq = lax.broadcasted_iota(jnp.int32, (rows, LANES), 1)
    zero = jnp.zeros((), BF)
    kvs = (ka_ref, kb_ref)
    blocks = 2 if part else 1
    size = 4 * rows // blocks
    lane = lax.broadcasted_iota(jnp.int32, (size, LANES), 1)

    def pair(p, carry):
        cs = pl.ds(pl.multiple_of(LANES * p, LANES), LANES)
        vs = pl.ds(pl.multiple_of(wide + LANES * p, LANES), LANES)
        qp = q_ref[:, cs]
        dop = do_ref[:, cs]
        prod = (dop.astype(F32) * mixed_ref[:, cs].astype(F32)).T
        dqt = [None, None]
        for j in range(blocks):
            mine = kvs if blocks == 1 else kvs[j : j + 1]
            kp = jnp.concatenate([r[:, cs] for r in mine], axis=0)
            vp = jnp.concatenate([r[:, vs] for r in mine], axis=0)
            bj = bias[size * j : size * (j + 1)]
            kt = kp.T
            dk = None
            dv = None
            for h in range(2):
                inh = (laneq < HD) if h == 0 else (laneq >= HD)
                mark = HD * (1 - h)
                qz = jnp.where(inh, qp, zero)
                qh = jnp.where(laneq == mark, jnp.ones((), BF), qz)
                doh = jnp.where(inh, dop, zero)
                st = dg(jnp.where(lane == mark, bj, kp), qh, 1, 1)
                pt = jnp.exp2(st * c - lse_ref[pl.ds(8 * p + h, 1), :])
                dpt = dg(vp, doh, 1, 1)
                row = jnp.sum(prod[HD * h : HD * (h + 1)], axis=0, keepdims=True)
                ds = (pt * (dpt - row)).astype(BF)
                dvh = dg(pt.astype(BF), doh, 1, 0)
                dkh = dg(ds, qz, 1, 0)
                t = dg(kt[HD * h : HD * (h + 1)], ds, 1, 0)
                dqt[h] = t if dqt[h] is None else dqt[h] + t
                dv = dvh if dv is None else dv + dvh
                dk = dkh if dk is None else dk + dkh
            dk = dk * sc
            if part:
                at = slice(size * j, size * (j + 1))
                dk = dk + acc_in[at, cs]
                dv = dv + acc_in[at, vs]
                o_ref = send_ref if j else out_ref
                o_ref[:, cs] = dk.astype(o_ref.dtype)
                o_ref[:, vs] = dv.astype(o_ref.dtype)
            else:
                acc_ref[:, cs] = dk
                acc_ref[:, vs] = dv
        dq_ref[:, cs] = (jnp.concatenate(dqt, axis=0).T * sc).astype(BF)
        return carry

    lax.fori_loop(0, wide // LANES, pair, 0)


def qkv_back_kernel(count, *refs):
    w_ref = refs[0]
    ins = refs[1 : 1 + 4 * count]
    outs = refs[1 + 4 * count :]
    ngr_ref = outs[-1]
    sum_ref = outs[-2]
    rows = ngr_ref.shape[1]
    sq = None
    sv = None
    for m in range(count):
        dqo_ref, dqp_ref, own_ref, rcv_ref = ins[4 * m : 4 * m + 4]
        dkv_ref, ngo_ref = outs[2 * m : 2 * m + 2]
        wide = dqo_ref.shape[1]
        for i, dq_ref in ((1, dqp_ref), (0, dqo_ref)):
            at = slice(i * rows, (i + 1) * rows)
            dkv = (own_ref[at, :] + rcv_ref[at, :].astype(F32)).astype(BF)
            dkv_ref[at, :] = dkv
            dq = dq_ref[...]
            ng = dg(dq, w_ref[0], 1, 0) + dg(dkv[:, :wide], w_ref[1], 1, 0) + dg(dkv[:, wide:], w_ref[2], 1, 0)
            if i:
                ngr_ref[m] = ng.astype(BF)
            else:
                ngo_ref[...] = ng
            cq = col_sum(dq)
            cv = col_sum(dkv[:, wide:])
            sq = cq if sq is None else sq + cq
            sv = cv if sv is None else sv + cv
    sum_ref[0:1] = sq
    sum_ref[1:2] = sv


def ln1_back_kernel(count, *refs):
    tok_ref = refs[0]
    vec_ref = refs[1]
    hgs = refs[2 : 2 + count]
    owns = refs[2 + count : 2 + 2 * count]
    rcv_ref, ig_ref, st_ref = refs[2 + 2 * count :]
    st_ref[...] = jnp.zeros(st_ref.shape, F32)
    for m in range(count):

        def some(at, carry, m=m):
            z, r = normalize(tok_ref[m, at, :].astype(F32))
            ng = owns[m][at, :] + rcv_ref[m, at, :].astype(F32)
            ig_ref[m, at, :] = hgs[m][at, :] + norm_back(ng, z, r, vec_ref[1:2])
            for i, v in enumerate((ng * z, ng)):
                st_ref[i : i + 1] = st_ref[i : i + 1] + col_sum(v)
            return carry

        chunked(tok_ref.shape[1], 128, some, 0)


def out_kernel(count, vec_ref, *refs):
    hids = refs[:count]
    own_ref, rcv_ref, o_ref = refs[count:]
    for m in range(count):

        def some(i, size, m=m):
            at = pl.ds(i, size)
            o_ref[m, at, :] = (
                hids[m][at, :] + (own_ref[m, at, :] + rcv_ref[m, at, :].astype(F32)) + vec_ref[3:4]
            ).astype(BF)

        by_rows(o_ref.shape[1], some)


def rows_product(pairs):
    acc = None
    for a, b in pairs:
        t = dg(a, b, 0, 0)
        acc = t if acc is None else acc + t
    return acc


def mlp_weights_kernel(count, *refs):
    n = 2 * count
    acts = refs[:n]
    gates = refs[n : 2 * n]
    norms = refs[2 * n : 3 * n]
    go_ref, gp_ref, pj_ref, fc_ref = refs[3 * n :]
    gs = []
    for m in range(count):
        gs += [go_ref[m], gp_ref[m]]
    pj_ref[...] = rows_product([(a[...], g) for a, g in zip(acts, gs)]).astype(pj_ref.dtype)
    fc_ref[...] = rows_product([(a[...], b[...]) for a, b in zip(norms, gates)]).astype(fc_ref.dtype)


def attend_weights_kernel(count, *refs):
    n = 2 * count
    dqs = refs[:n]
    norms = refs[n : 2 * n]
    mixes = refs[2 * n : 3 * n]
    brs = refs[3 * n : 4 * n]
    dkvs = refs[4 * n : 4 * n + count]
    outs = refs[4 * n + count :]
    c = lax.axis_index("tensor") & 1
    rows, wide = dqs[0].shape
    hc = wide // 2
    ns = [r[...] for r in norms]
    full = [jnp.concatenate(ns[2 * m : 2 * m + 2], axis=0) for m in range(count)]
    pieces = [
        rows_product([(a[...], b) for a, b in zip(dqs, ns)]),
        rows_product([(a[:, :wide], b) for a, b in zip(dkvs, full)]),
        rows_product([(a[:, wide:], b) for a, b in zip(dkvs, full)]),
        rows_product([(a[...], b[...]) for a, b in zip(mixes, brs)]),
    ]
    for i, p in enumerate(pieces):
        own_ref, send_ref = outs[2 * (i // 2) : 2 * (i // 2) + 2]
        at = slice((i % 2) * hc, (i % 2 + 1) * hc)
        low = p[:hc]
        high = p[hc:]
        own_ref[at, :] = jnp.where(c == 0, low, high)
        send_ref[at, :] = jnp.where(c == 0, high, low).astype(BF)


def by_rows(total, body):
    size = 48 if total % 48 == 0 else 64 if total % 64 == 0 else total
    if size == total:
        body(0, total)
        return

    def some(i, carry):
        body(pl.multiple_of(i * size, 16), size)
        return carry

    lax.fori_loop(0, total // size, some, 0)


def add_kernel(rcv_ref, own_ref, out_ref):
    def some(i, size):
        at = pl.ds(i, size)
        out_ref[at, :] = (own_ref[at, :].astype(F32) + rcv_ref[at, :].astype(F32)).astype(out_ref.dtype)

    by_rows(out_ref.shape[0], some)


def halve_kernel(bit, rcv_ref, own_ref, keep_ref, send_ref):
    r = keep_ref.shape[0]
    b = (lax.axis_index("dp") >> bit) & 1

    def some(i, size):
        at = pl.ds(i, size)
        mine = pl.ds(pl.multiple_of(b * r + i, 16), size)
        other = pl.ds(pl.multiple_of((1 - b) * r + i, 16), size)
        send_ref[at, :] = (own_ref[other, :].astype(F32) + rcv_ref[other, :].astype(F32)).astype(BF)
        keep_ref[at, :] = own_ref[mine, :].astype(F32) + rcv_ref[mine, :].astype(F32)

    by_rows(r, some)


def join_kernel(bit, rcv_ref, own_ref, out_ref):
    r = own_ref.shape[0]
    b = (lax.axis_index("dp") >> bit) & 1

    def some(i, size):
        at = pl.ds(i, size)
        mine = pl.ds(pl.multiple_of(b * r + i, 16), size)
        other = pl.ds(pl.multiple_of((1 - b) * r + i, 16), size)
        out_ref[mine, :] = own_ref[at, :].astype(out_ref.dtype)
        out_ref[other, :] = rcv_ref[at, :].astype(out_ref.dtype)

    by_rows(r, some)


def join_both_kernel(bit, rcv_a, own_a, rcv_b, own_b, qkv_ref, out_ref):
    r = own_a.shape[0]
    b = (lax.axis_index("dp") >> bit) & 1

    def some(i, size):
        at = pl.ds(i, size)
        qkv_ref[pl.ds(pl.multiple_of(b * r + i, 16), size), :] = own_a[at, :].astype(F32)
        qkv_ref[pl.ds(pl.multiple_of((1 - b) * r + i, 16), size), :] = rcv_a[at, :].astype(F32)
        own = own_b[at, :].astype(F32)
        rcv = rcv_b[at, :].astype(F32)
        qkv_ref[pl.ds(pl.multiple_of(2 * r + i, 16), size), :] = jnp.where(b == 0, own, rcv)
        out_ref[at, :] = jnp.where(b == 0, rcv, own)

    by_rows(r, some)


def stats_kernel(count, *refs):
    lst2 = refs[:count]
    fsums = refs[count : 3 * count]
    q_ref, lst1_ref, own_ref, send_ref = refs[3 * count :]
    c = lax.axis_index("tensor") & 1
    common = lst1_ref[...]
    for r in lst2:
        common = common + r[...]
    f = fsums[0][...]
    for r in fsums[1:]:
        f = f + r[...]
    q = q_ref[...]
    wide = own_ref.shape[1]
    hc = q.shape[1] // 2
    qpad = jnp.zeros((1, wide - 2 * hc), F32)
    low = jnp.concatenate([q[0:1, :hc], q[1:2, :hc], qpad], axis=1)
    high = jnp.concatenate([q[0:1, hc:], q[1:2, hc:], qpad], axis=1)
    own_ref[...] = common
    send_ref[...] = common
    own_ref[6:7] = jnp.where(c == 0, low, high)
    send_ref[6:7] = jnp.where(c == 0, high, low)
    own_ref[7:8] = f[0:1]
    send_ref[7:8] = f[1:2]


def spread_kernel(rcv_ref, own_ref, fb_ref, qb_ref, *outs):
    at = lax.broadcasted_iota(jnp.int32, own_ref.shape, 0)
    total = own_ref[...] + jnp.where(at < 6, rcv_ref[...], 0.0)
    for i, o_ref in enumerate(outs):
        o_ref[...] = total[i : i + 1].reshape(o_ref.shape)
    hc = qb_ref.shape[1]
    qb_ref[0:1, :] = total[6:7, :hc]
    qb_ref[1:2, :] = total[6:7, hc : 2 * hc]
    fb_ref[...] = total[7:8, : fb_ref.shape[0]].reshape(fb_ref.shape)


def body(
    tokens, qkv_weight, qv_bias, out_weight, out_bias, ln1_gain, ln1_shift, fc_weight, fc_bias,
    proj_weight, proj_bias, ln2_gain, ln2_shift, seq_lengths, out_grad,
):
    batches, rows, width = tokens.shape
    hc = out_weight.shape[0]
    wide = 2 * hc
    units = fc_weight.shape[1]
    tsize = lax.axis_size("tensor")
    dsize = lax.axis_size("dp")
    bits = dsize.bit_length() - 1
    cpairs = [(i, i ^ 1) for i in range(tsize)]
    ypairs = [(i, i ^ 2) for i in range(tsize)]
    mb = range(batches)
    line = Line()

    def core(v):
        return lax.ppermute(v, "tensor", cpairs)

    def across(v):
        return lax.ppermute(v, "tensor", ypairs)

    def swap(v, b):
        return lax.ppermute(v, "dp", [(i, i ^ (1 << b)) for i in range(dsize)])

    def after(v, *deps):
        return lax.optimization_barrier((v,) + deps)[0]

    def kernel_of(f, *static):
        def kernel(*refs):
            f(*static, *refs)

        return kernel

    def halve(own, rcv, b, name, **kw):
        size = own.shape[0] // 2
        if size % 16:
            both = own.astype(F32) + rcv.astype(F32)
            both = both.reshape((2, size) + own.shape[1:])
            bit = (lax.axis_index("dp") >> b) & 1
            keep = lax.dynamic_index_in_dim(both, bit, 0, keepdims=False)
            return keep, lax.dynamic_index_in_dim(both, 1 - bit, 0, keepdims=False).astype(BF)
        shape = (size,) + own.shape[1:]
        return line(kernel_of(halve_kernel, b), "halve_" + name, [rcv, own], [sds(shape, F32), sds(shape, BF)], **kw)

    def join(piece, rcv, b, dtype, name, kind="join_"):
        size = piece.shape[0]
        if size % 16:
            low = ((lax.axis_index("dp") >> b) & 1) == 0
            return jnp.concatenate([jnp.where(low, piece, rcv), jnp.where(low, rcv, piece)], axis=0).astype(dtype)
        shape = (2 * size,) + piece.shape[1:]
        return line(kernel_of(join_kernel, b), kind + name, [rcv, piece], [sds(shape, dtype)])[0]

    class Sum:
        def __init__(self, own, rcv, name, turn=0):
            self.own, self.rcv, self.name, self.at = own, rcv, name, 0
            self.order = [(b + turn) % bits for b in range(bits)]

        def go(self, **kw):
            k = self.at
            self.at += 1
            if k > 2 * bits:
                return
            if k < bits:
                self.own, send = halve(self.own, self.rcv, self.order[k], self.name, **kw)
            elif k == bits:
                send = line(add_kernel, "last_" + self.name, [self.rcv, self.own], [sds(self.own.shape, BF)], **kw)[0]
                self.own = send
            else:
                b = self.order[2 * bits - k]
                final = k == 2 * bits
                kind = "final_" if final and self.name == "f" else "join_"
                send = join(self.own, self.rcv, b, F32 if final else BF, self.name, kind)
                self.own = send
            if k < 2 * bits:
                self.rcv = swap(send, self.order[k if k < bits else 2 * bits - 1 - k])

        def finish(self):
            while self.at <= 2 * bits:
                self.go()
            return self.own

    wq_o = jnp.transpose(qkv_weight, (1, 2, 0))
    wq_x = core(wq_o)
    wo_x = core(out_weight)

    packed = (8, max(units, width))
    *normed, small, vec = line(
        ln1_kernel, "ln1",
        [out_bias, ln1_gain, ln1_shift, proj_bias, ln2_gain, ln2_shift, fc_bias, qv_bias, tokens],
        [sds((rows, width), BF)] * batches + [sds(packed, F32), sds((8, width), F32)], far=9,
    )
    normed_p = [across(v) for v in normed]
    qb, fb, wo, wq = line(
        weights_kernel, "weights", [out_weight, wq_o, small, core(small), wo_x, wq_x],
        [sds((3, wide), F32), sds((2, units), F32), sds((wide, width), BF), sds((3, wide, width), BF)], far=2,
    )

    q = [[None, None] for _ in mb]
    kv = [[None, None] for _ in mb]

    def qkv(m, **kw):
        q[m][0], q[m][1], kv[m][0] = line(
            qkv_kernel, "qkv", [qb, wq, normed[m], normed_p[m]],
            [sds((rows, wide), BF)] * 2 + [sds((2 * rows, 2 * wide), BF)], **kw,
        )
        kv[m][1] = core(kv[m][0])

    mixed = [[None, None] for _ in mb]
    lse = [[None, None] for _ in mb]
    own = [None for _ in mb]
    rcv = [None for _ in mb]
    lse_rows = 8 * (wide // LANES)

    def attend(m, part, **kw):
        mixed[m][part], lse[m][part], term = line(
            kernel_of(attend_kernel, m, part), "attend", [seq_lengths] + kv[m] + [wo, q[m][part]],
            [sds((rows, wide), BF), sds((lse_rows, rows), F32), sds((rows, width), BF if part else F32)],
            n_smem=1, **kw,
        )
        if part:
            rcv[m] = across(term)
        else:
            own[m] = term

    hid = [None for _ in mb]
    n2 = [[None, None] for _ in mb]

    def mid(m, **kw):
        hid[m], n2[m][0] = line(
            kernel_of(mid_kernel, m), "mid", [own[m], rcv[m], vec, tokens],
            [sds((rows, width), F32), sds((rows, width), BF)], **kw,
        )
        n2[m][1] = across(n2[m][0])

    acts = [[None, None] for _ in mb]
    gates = [[None, None] for _ in mb]
    fsum = [[None, None] for _ in mb]
    nown = [None for _ in mb]
    nrcv = [None for _ in mb]

    def mlp(m, part, **kw):
        a_o, a_x, g_o, g_x, fsum[m][part], term = line(
            kernel_of(mlp_kernel, m), "mlp",
            [grads_p if part else out_grad, fc_weight, fc_x, fb, proj_weight, pj_x, n2[m][part]],
            [sds((rows, units), BF)] * 4 + [sds((2, units), F32), sds((rows, width), BF if part else F32)], **kw,
        )
        acts[m][part] = (a_o, a_x)
        gates[m][part] = (g_o, g_x)
        if part:
            nrcv[m] = across(term)
        else:
            nown[m] = term

    flat = [(m, part) for m in mb for part in range(2)]

    def mlp_weights(k, dtype, name, **kw):
        return line(
            kernel_of(mlp_weights_kernel, batches), name,
            [acts[m][i][k] for m, i in flat] + [gates[m][i][k] for m, i in flat] + [n2[m][i] for m, i in flat]
            + [out_grad, grads_p],
            [sds((units, width), dtype), sds((width, units), dtype)], **kw,
        )

    hg = [None for _ in mb]
    st2 = [None for _ in mb]
    br = [[None, None] for _ in mb]

    def ln2_back(m, **kw):
        hg[m], st2[m], br[m][0] = line(
            kernel_of(ln2_back_kernel, m), "ln2b", [hid[m], nown[m], nrcv[m], vec, out_grad],
            [sds((rows, width), F32), sds((8, width), F32), sds((rows, width), BF)], **kw,
        )
        br[m][1] = across(br[m][0])

    def proj(part, **kw):
        return line(
            kernel_of(proj_kernel, batches), "proj",
            [proj_weight, pj_x] + [acts[m][part][k] for m in mb for k in range(2)],
            [sds((batches, rows, width), BF if part else F32)], **kw,
        )[0]

    dq = [[None, None] for _ in mb]
    acc = [None for _ in mb]
    dkvo = [None for _ in mb]
    dkvr = [None for _ in mb]
    dkvs = [None for _ in mb]

    def attend_back(m, part, **kw):
        args = [seq_lengths] + kv[m] + [wo, mixed[m][part], lse[m][part], br[m][part]]
        scratch = [pltpu.VMEM((rows, wide), BF)]
        if part:
            dq[m][1], dkvo[m], send = line(
                kernel_of(attend_back_kernel, m, 1), "attendb", args + [acc[m], q[m][1]],
                [sds((rows, wide), BF), sds((2 * rows, 2 * wide), F32), sds((2 * rows, 2 * wide), BF)],
                n_smem=1, scratch=scratch, **kw,
            )
            dkvs[m] = send
        else:
            dq[m][0], acc[m] = line(
                kernel_of(attend_back_kernel, m, 0), "attendb", args + [q[m][0]],
                [sds((rows, wide), BF), sds((4 * rows, 2 * wide), F32)],
                n_smem=1, scratch=scratch, **kw,
            )

    def qkv_back(**kw):
        args = [wq]
        for m in mb:
            args += [dq[m][0], dq[m][1], dkvo[m], dkvr[m]]
        *res, qsum, rem = line(
            kernel_of(qkv_back_kernel, batches), "qkvb", args,
            [sds((2 * rows, 2 * wide), BF), sds((rows, width), F32)] * batches
            + [sds((2, wide), F32), sds((batches, rows, width), BF)], **kw,
        )
        return res[0::2], res[1::2], qsum, rem

    last = batches - 1
    qkv(0)
    fc_x = core(after(fc_weight, q[0][0]))
    pj_x = core(after(proj_weight, q[0][0]))
    grads_p = across(after(out_grad, q[0][0]))
    for m in mb[1:]:
        qkv(m)
    attend(0, 1)
    attend(1, 1)
    attend(0, 0, needs=[grads_p])
    attend(1, 0)
    mid(0)
    mid(1)
    mlp(0, 0)
    mlp(1, 0)
    mlp(0, 1)
    mlp(1, 1)
    pj_send, fc_send = mlp_weights(1, BF, "mlpwx")
    pj_own, fc_own = mlp_weights(0, F32, "mlpwo")
    ln2_back(0)
    ln2_back(1)
    pj_back = core(pj_send)
    fc_back = core(fc_send)
    p_sum = Sum(pj_own, pj_back, "p")
    f_sum = Sum(fc_own, fc_back, "f")
    p_sum.go()
    pown = proj(0)
    psend = proj(1)
    attend_back(0, 0)
    attend_back(1, 0)
    f_sum.go(needs=[br[m][1] for m in mb])
    p_sum.go()
    prcv = across(after(psend, p_sum.own))
    attend_back(0, 1)
    p_sum.go()
    attend_back(1, 1)
    p_sum.go(needs=[prcv])
    f_sum.go()
    for m in mb:
        dkvr[m] = core(after(dkvs[m], f_sum.own))
    dkv, ngo, qsum, ngs = qkv_back()

    both = [normed, normed_p]
    a1_own, a1_send, a2_own, a2_send = line(
        kernel_of(attend_weights_kernel, batches), "attw",
        [dq[m][i] for m, i in flat] + [both[i][m] for m, i in flat] + [mixed[m][i] for m, i in flat]
        + [br[m][i] for m, i in flat] + dkv,
        [sds((2 * hc, width), F32), sds((2 * hc, width), BF)] * 2,
        limit=32,
    )
    ngr = across(after(ngs, a2_send))
    a_sum = Sum(a1_own, core(a1_send), "a")
    b_sum = Sum(a2_own, core(a2_send), "b")
    p_sum.go()
    f_sum.go()
    a_sum.go()
    b_sum.go()
    layer_out = line(
        kernel_of(out_kernel, batches), "out", [vec] + hid + [pown, prcv], [sds((batches, rows, width), BF)],
    )[0]
    p_sum.go()
    f_sum.go()
    a_sum.go()
    b_sum.go()
    a_sum.go()
    f_sum.go()
    ig, st1 = line(
        kernel_of(ln1_back_kernel, batches), "ln1b", [tokens, vec] + hg + ngo + [ngr],
        [sds((batches, rows, width), F32), sds((8, width), F32)],
    )
    b_sum.go()
    s_own, s_send = line(
        kernel_of(stats_kernel, batches), "stats",
        st2 + [fsum[m][i] for m, i in flat] + [qsum, st1],
        [sds((8, width), F32), sds((8, width), F32)],
    )
    s_rcv = core(s_send)
    a_sum.go()

    def stat():
        return line(add_kernel, "stat", [s_rcv, stats], [sds((8, width), F32)])[0]

    stats = s_own
    stats = stat()
    s_rcv = swap(stats, 0)
    f_sum.go()
    p_sum.finish()
    b_sum.go()
    a_sum.go()
    for b in range(1, bits):
        stats = stat()
        s_rcv = swap(stats, b)
        for chain in (b_sum, a_sum):
            if chain.at < 2 * bits:
                chain.go()
    stats = stat()
    s_rcv = across(stats)
    for chain in (a_sum, b_sum):
        while chain.at < 2 * bits:
            chain.go()
    f_sum.finish()
    vector = sds((width,), F32)
    fb_grad, qb_grad, *vectors = line(
        spread_kernel, "spread", [s_rcv, stats],
        [sds((units,), F32), sds((2, hc), F32)] + [vector] * 6,
    )
    qkv_grad, out_grad_w = line(
        kernel_of(join_both_kernel, a_sum.order[0]), "join_ab", [a_sum.rcv, a_sum.own, b_sum.rcv, b_sum.own],
        [sds((3 * hc, width), F32), sds((hc, width), F32)],
    )
    fc_grad = f_sum.own
    pj_grad = p_sum.own

    return (
        layer_out,
        ig,
        jnp.transpose(qkv_grad.reshape(3, hc, width), (2, 0, 1)),
        qb_grad,
        out_grad_w,
        vectors[4],
        vectors[0],
        vectors[1],
        fc_grad,
        fb_grad,
        pj_grad,
        vectors[5],
        vectors[2],
        vectors[3],
    )


def solution(mesh):
    placed = (
        P(None, ("dp", "tensor"), None),
        P(None, None, "tensor"),
        P(None, "tensor"),
        P("tensor", None),
        P(),
        P(),
        P(),
        P(None, "tensor"),
        P("tensor"),
        P("tensor", None),
        P(),
        P(),
        P(),
        P(None, "dp"),
        P(None, ("dp", "tensor"), None),
    )
    return jax.shard_map(
        body,
        mesh=mesh,
        in_specs=placed,
        out_specs=(
            P(None, ("dp", "tensor"), None),
            P(None, ("dp", "tensor"), None),
            P(None, None, "tensor"),
            P(None, "tensor"),
            P("tensor", None),
            P(),
            P(),
            P(),
            P(None, "tensor"),
            P("tensor"),
            P("tensor", None),
            P(),
            P(),
            P(),
        ),
        check_vma=False,
    )
```

```python
import math

import jax
import jax.numpy as jnp
from jax import lax
from jax.experimental import pallas as pl
from jax.experimental.pallas import tpu as pltpu
from jax.sharding import PartitionSpec as P

HD = 64
LANES = 128
LOG2E = 1.4426950408889634
NEG = -1e30
EPS = 1e-05
BF = jnp.bfloat16
F32 = jnp.float32
VM = pl.BlockSpec(memory_space=pltpu.VMEM)
SM = pl.BlockSpec(memory_space=pltpu.SMEM)
HB = pl.BlockSpec(memory_space=pltpu.HBM)


def dg(a, b, ca, cb):
    return lax.dot_general(a, b, (((ca,), (cb,)), ((), ())), preferred_element_type=F32)


def sds(shape, dtype):
    return jax.ShapeDtypeStruct(tuple(shape), dtype)


TIMES = dict(
    ln1=2.0, weights=1.4, qkv=2.3, attend=5.2, mid=0.4, mlp=4.0, mlpw0=4.0, mlpwx=2.2, mlpwo=2.2, ln2b=27.0, proj=1.4,
    attendb=7.0, qkvb=2.8, attw=2.7, ln1b=2.4, out=1.1, halve=10.0, last=10.0, join=10.0,
)
SCALE = 0.3


class Line:
    def __init__(self):
        self.last = None

    def __call__(self, kernel, name, args, outs, n_smem=0, scratch=(), limit=24, far=0, needs=()):
        args = list(args)
        after = list(needs)
        if self.last is not None:
            after.append(self.last)
        if after:
            args[-1] = lax.optimization_barrier(tuple([args[-1]] + after))[0]
        for i in range(n_smem, n_smem + far):
            args[i] = pltpu.with_memory_space_constraint(args[i], pltpu.HBM)
        fetched = args[n_smem : n_smem + far]
        total = len(args)

        def run(*refs):
            if not far:
                return kernel(*refs)
            body_refs = refs[: len(refs) - far - 1]
            bufs = refs[len(refs) - far - 1 : -1]
            sems = refs[-1]
            copies = [
                pltpu.make_async_copy(refs[n_smem + i], bufs[i], sems.at[i]) for i in range(far)
            ]
            for cp in copies:
                cp.start()
            for cp in copies:
                cp.wait()
            return kernel(*body_refs[:n_smem], *bufs, *body_refs[n_smem + far :])

        extra = []
        if far:
            extra = [pltpu.VMEM(v.shape, v.dtype) for v in fetched] + [pltpu.SemaphoreType.DMA((far,))]
        res = pl.pallas_call(
            run,
            in_specs=[SM] * n_smem + [HB] * far + [VM] * (total - n_smem - far),
            out_specs=[VM] * len(outs),
            out_shape=outs,
            scratch_shapes=list(scratch) + extra,
            compiler_params=pltpu.CompilerParams(vmem_limit_bytes=limit << 20),
            cost_estimate=pl.CostEstimate(
                flops=int(SCALE * 1.1e9 * TIMES.get(name.split("_")[0], 0.2)), transcendentals=0, bytes_accessed=1
            ),
            name=name,
        )(*args)
        self.last = res[-1]
        return res


def normalize(x):
    d = x.shape[-1]
    xc = x - jnp.sum(x, axis=-1, keepdims=True) * (1.0 / d)
    var = jnp.sum(xc * xc, axis=-1, keepdims=True) * (1.0 / d)
    r = lax.rsqrt(var + EPS)
    return xc * r, r


def norm_back(grad, z, r, gain):
    d = z.shape[-1]
    e = grad * gain
    me = jnp.sum(e, axis=-1, keepdims=True) * (1.0 / d)
    mez = jnp.sum(e * z, axis=-1, keepdims=True) * (1.0 / d)
    return (e - me - z * mez) * r


def chunked(total, size, body, carry=None):
    if total % size:
        return body(pl.ds(0, total), carry)
    return lax.fori_loop(0, total // size, lambda i, c: body(pl.ds(pl.multiple_of(i * size, size), size), c), carry)


def col_sum(x):
    return jnp.sum(x.astype(F32), axis=0, keepdims=True)


def ln1_kernel(*refs):
    vecs = refs[:6]
    fb_ref, qb_ref, tok_ref = refs[6:9]
    outs = refs[9:-2]
    small_ref, vec_ref = refs[-2:]
    vec_ref[...] = jnp.zeros(vec_ref.shape, F32)
    for i, v in enumerate(vecs):
        vec_ref[i : i + 1, :] = v[...].astype(F32).reshape(1, -1)
    for m, o_ref in enumerate(outs):
        z, _ = normalize(tok_ref[m].astype(F32))
        o_ref[...] = (z * vec_ref[1:2] + vec_ref[2:3]).astype(BF)
    small_ref[...] = jnp.zeros(small_ref.shape, F32)
    small_ref[0:1, : fb_ref.shape[0]] = fb_ref[...].astype(F32).reshape(1, -1)
    small_ref[1:3, : qb_ref.shape[1]] = qb_ref[...].astype(F32)


def weights_kernel(woo_ref, wqo_ref, so_ref, sx_ref, wox_ref, wqx_ref, qb_ref, fb_ref, wo_ref, wq_ref):
    c = lax.axis_index("tensor") & 1
    hc = woo_ref.shape[0]
    units = fb_ref.shape[1]
    fb_ref[0:1, :] = so_ref[0:1, :units]
    fb_ref[1:2, :] = sx_ref[0:1, :units]
    qb_ref[...] = jnp.zeros(qb_ref.shape, F32)

    def place(at_o, at_x):
        for at, b, o, q in ((at_o, so_ref, woo_ref, wqo_ref), (at_x, sx_ref, wox_ref, wqx_ref)):
            qb_ref[0:1, at : at + hc] = b[1:2, :hc]
            qb_ref[2:3, at : at + hc] = b[2:3, :hc]
            wo_ref[at : at + hc, :] = o[...]
            wq_ref[:, at : at + hc, :] = q[...]

    @pl.when(c == 0)
    def _():
        place(0, hc)

    @pl.when(c != 0)
    def _():
        place(hc, 0)


def qkv_kernel(b_ref, w_ref, no_ref, np_ref, qo_ref, qp_ref, kv_ref):
    rows, wide = qo_ref.shape
    for i, (n_ref, q_ref) in enumerate(((no_ref, qo_ref), (np_ref, qp_ref))):
        n = n_ref[...]
        for s in range(3):
            v = (dg(n, w_ref[s], 1, 1) + b_ref[s : s + 1]).astype(BF)
            if s == 0:
                q_ref[...] = v
            else:
                kv_ref[i * rows : (i + 1) * rows, wide * (s - 1) : wide * s] = v


def row_starts(rows):
    t = lax.axis_index("tensor")
    return [rows * t, rows * (t ^ 2), rows * (t ^ 1), rows * (t ^ 3)]


def key_bias(starts, length, rows):
    out = []
    for b in range(4):
        at = lax.broadcasted_iota(jnp.int32, (rows, LANES), 0) + starts[b]
        out.append(jnp.where(at < length, 0.0, NEG).astype(BF))
    return jnp.concatenate(out, axis=0)


def attend_kernel(m, part, len_ref, ka_ref, kb_ref, w_ref, q_ref, mixed_ref, lse_ref, term_ref):
    rows, wide = q_ref.shape
    length = len_ref[m, 0]
    starts = row_starts(rows)
    c = LOG2E / math.sqrt(HD)
    bias = key_bias(starts, length, rows)
    lane = lax.broadcasted_iota(jnp.int32, (4 * rows, LANES), 1)
    laneq = lax.broadcasted_iota(jnp.int32, (rows, LANES), 1)
    valid = lax.broadcasted_iota(jnp.int32, (rows, LANES), 0) + starts[part] < length
    kvs = (ka_ref, kb_ref)

    def head(at, carry):
        p = at >> 1
        h = at & 1
        cs = pl.ds(pl.multiple_of(LANES * p, LANES), LANES)
        vs = pl.ds(pl.multiple_of(wide + LANES * p, LANES), LANES)
        kp = jnp.concatenate([r[:, cs] for r in kvs], axis=0)
        vp = jnp.concatenate([r[:, vs] for r in kvs], axis=0)
        inh = (laneq // HD) == h
        mark = HD * (1 - h)
        one = jnp.where(laneq == mark, 1.0, 0.0).astype(BF)
        s = dg(jnp.where(inh, q_ref[:, cs], one), jnp.where(lane == mark, bias, kp), 1, 1)
        top = jnp.max(s, axis=1, keepdims=True)
        e = jnp.exp2((s - top) * c)
        l = jnp.sum(e, axis=1, keepdims=True)
        o = dg(e.astype(BF), vp, 1, 0) * (1.0 / l)
        lt = jnp.broadcast_to(top * c + jnp.log2(l), o.shape).T
        lse_ref[pl.ds(8 * p + h, 1), :] = lt[0:1]
        mixed_ref[:, cs] = jnp.where(inh, jnp.where(valid, o, 0.0).astype(BF), mixed_ref[:, cs])
        return carry

    lax.fori_loop(0, wide // HD, head, 0)
    term_ref[...] = dg(mixed_ref[...], w_ref[...], 1, 0).astype(term_ref.dtype)


def mid_kernel(m, own_ref, rcv_ref, vec_ref, tok_ref, hid_ref, n_ref):
    h = tok_ref[m].astype(F32) + (own_ref[...] + rcv_ref[...].astype(F32)) + vec_ref[0:1]
    hid_ref[...] = h
    z, _ = normalize(h)
    n_ref[...] = (z * vec_ref[4:5] + vec_ref[5:6]).astype(BF)


def mlp_kernel(m, g_ref, fo_ref, fx_ref, bias_ref, po_ref, px_ref, n_ref, ao_ref, ax_ref, ggo_ref, ggx_ref, sum_ref, term_ref):
    n = n_ref[...]
    g = g_ref[m]
    back = None
    for j, (f_ref, p_ref, a_ref, gg_ref) in enumerate(
        ((fo_ref, po_ref, ao_ref, ggo_ref), (fx_ref, px_ref, ax_ref, ggx_ref))
    ):
        f = f_ref[...]
        gate = dg(n, f, 1, 0) + bias_ref[j : j + 1]
        q = 0.5 * jnp.tanh(0.851 * gate) + 0.5
        a_ref[...] = (gate * q).astype(BF)
        slope = q + 1.702 * gate * q * (1.0 - q)
        gg = (dg(g, p_ref[...], 1, 1) * slope).astype(BF)
        gg_ref[...] = gg
        term = dg(gg, f, 1, 1)
        back = term if back is None else back + term
        sum_ref[j : j + 1] = col_sum(gg)
    term_ref[...] = back.astype(term_ref.dtype)


def proj_kernel(count, po_ref, px_ref, *refs):
    out_ref = refs[-1]
    for m in range(count):
        out_ref[m] = (dg(refs[2 * m][...], po_ref[...], 1, 0) + dg(refs[2 * m + 1][...], px_ref[...], 1, 0)).astype(
            out_ref.dtype
        )


def ln2_back_kernel(m, hid_ref, own_ref, rcv_ref, vec_ref, grad_ref, hg_ref, st_ref, br_ref):
    st_ref[...] = jnp.zeros(st_ref.shape, F32)

    def some(at, carry):
        z, r = normalize(hid_ref[at, :])
        ng = own_ref[at, :] + rcv_ref[at, :].astype(F32)
        g = grad_ref[m, at, :].astype(F32)
        hg = g + norm_back(ng, z, r, vec_ref[4:5])
        hg_ref[at, :] = hg
        br = hg.astype(BF)
        br_ref[at, :] = br
        for i, v in enumerate((ng * z, ng, br, g)):
            st_ref[2 + i : 3 + i] = st_ref[2 + i : 3 + i] + col_sum(v)
        return carry

    chunked(br_ref.shape[0], 128, some, 0)


def attend_back_kernel(m, part, *refs):
    len_ref, ka_ref, kb_ref, w_ref, mixed_ref, lse_ref, b_ref = refs[:7]
    refs = refs[7:]
    if part:
        (acc_in, q_ref, dq_ref, out_ref, send_ref, do_ref) = refs
    else:
        (q_ref, dq_ref, acc_ref, do_ref) = refs
    rows, wide = q_ref.shape
    length = len_ref[m, 0]
    starts = row_starts(rows)
    c = LOG2E / math.sqrt(HD)
    sc = 1.0 / math.sqrt(HD)
    at = lax.broadcasted_iota(jnp.int32, (rows, wide), 0) + starts[part]
    do_ref[...] = jnp.where(at < length, dg(b_ref[...], w_ref[...], 1, 1), 0.0).astype(BF)
    bias = key_bias(starts, length, rows)
    laneq = lax.broadcasted_iota(jnp.int32, (rows, LANES), 1)
    zero = jnp.zeros((), BF)
    kvs = (ka_ref, kb_ref)
    blocks = 2 if part else 1
    size = 4 * rows // blocks
    lane = lax.broadcasted_iota(jnp.int32, (size, LANES), 1)

    def pair(p, carry):
        cs = pl.ds(pl.multiple_of(LANES * p, LANES), LANES)
        vs = pl.ds(pl.multiple_of(wide + LANES * p, LANES), LANES)
        qp = q_ref[:, cs]
        dop = do_ref[:, cs]
        prod = (dop.astype(F32) * mixed_ref[:, cs].astype(F32)).T
        dqt = [None, None]
        for j in range(blocks):
            mine = kvs if blocks == 1 else kvs[j : j + 1]
            kp = jnp.concatenate([r[:, cs] for r in mine], axis=0)
            vp = jnp.concatenate([r[:, vs] for r in mine], axis=0)
            bj = bias[size * j : size * (j + 1)]
            kt = kp.T
            dk = None
            dv = None
            for h in range(2):
                inh = (laneq < HD) if h == 0 else (laneq >= HD)
                mark = HD * (1 - h)
                qz = jnp.where(inh, qp, zero)
                qh = jnp.where(laneq == mark, jnp.ones((), BF), qz)
                doh = jnp.where(inh, dop, zero)
                st = dg(jnp.where(lane == mark, bj, kp), qh, 1, 1)
                pt = jnp.exp2(st * c - lse_ref[pl.ds(8 * p + h, 1), :])
                dpt = dg(vp, doh, 1, 1)
                row = jnp.sum(prod[HD * h : HD * (h + 1)], axis=0, keepdims=True)
                ds = (pt * (dpt - row)).astype(BF)
                dvh = dg(pt.astype(BF), doh, 1, 0)
                dkh = dg(ds, qz, 1, 0)
                t = dg(kt[HD * h : HD * (h + 1)], ds, 1, 0)
                dqt[h] = t if dqt[h] is None else dqt[h] + t
                dv = dvh if dv is None else dv + dvh
                dk = dkh if dk is None else dk + dkh
            dk = dk * sc
            if part:
                at = slice(size * j, size * (j + 1))
                dk = dk + acc_in[at, cs]
                dv = dv + acc_in[at, vs]
                o_ref = send_ref if j else out_ref
                o_ref[:, cs] = dk.astype(o_ref.dtype)
                o_ref[:, vs] = dv.astype(o_ref.dtype)
            else:
                acc_ref[:, cs] = dk
                acc_ref[:, vs] = dv
        dq_ref[:, cs] = (jnp.concatenate(dqt, axis=0).T * sc).astype(BF)
        return carry

    lax.fori_loop(0, wide // LANES, pair, 0)


def qkv_back_kernel(count, *refs):
    w_ref = refs[0]
    ins = refs[1 : 1 + 4 * count]
    outs = refs[1 + 4 * count :]
    ngr_ref = outs[-1]
    sum_ref = outs[-2]
    rows = ngr_ref.shape[1]
    sq = None
    sv = None
    for m in range(count):
        dqo_ref, dqp_ref, own_ref, rcv_ref = ins[4 * m : 4 * m + 4]
        dkv_ref, ngo_ref = outs[2 * m : 2 * m + 2]
        wide = dqo_ref.shape[1]
        for i, dq_ref in ((1, dqp_ref), (0, dqo_ref)):
            at = slice(i * rows, (i + 1) * rows)
            dkv = (own_ref[at, :] + rcv_ref[at, :].astype(F32)).astype(BF)
            dkv_ref[at, :] = dkv
            dq = dq_ref[...]
            ng = dg(dq, w_ref[0], 1, 0) + dg(dkv[:, :wide], w_ref[1], 1, 0) + dg(dkv[:, wide:], w_ref[2], 1, 0)
            if i:
                ngr_ref[m] = ng.astype(BF)
            else:
                ngo_ref[...] = ng
            cq = col_sum(dq)
            cv = col_sum(dkv[:, wide:])
            sq = cq if sq is None else sq + cq
            sv = cv if sv is None else sv + cv
    sum_ref[0:1] = sq
    sum_ref[1:2] = sv


def ln1_back_kernel(count, *refs):
    tok_ref = refs[0]
    vec_ref = refs[1]
    hgs = refs[2 : 2 + count]
    owns = refs[2 + count : 2 + 2 * count]
    rcv_ref, ig_ref, st_ref = refs[2 + 2 * count :]
    st_ref[...] = jnp.zeros(st_ref.shape, F32)
    for m in range(count):

        def some(at, carry, m=m):
            z, r = normalize(tok_ref[m, at, :].astype(F32))
            ng = owns[m][at, :] + rcv_ref[m, at, :].astype(F32)
            ig_ref[m, at, :] = hgs[m][at, :] + norm_back(ng, z, r, vec_ref[1:2])
            for i, v in enumerate((ng * z, ng)):
                st_ref[i : i + 1] = st_ref[i : i + 1] + col_sum(v)
            return carry

        chunked(tok_ref.shape[1], 128, some, 0)


def out_kernel(count, vec_ref, *refs):
    hids = refs[:count]
    own_ref, rcv_ref, o_ref = refs[count:]
    for m in range(count):

        def some(i, size, m=m):
            at = pl.ds(i, size)
            o_ref[m, at, :] = (
                hids[m][at, :] + (own_ref[m, at, :] + rcv_ref[m, at, :].astype(F32)) + vec_ref[3:4]
            ).astype(BF)

        by_rows(o_ref.shape[1], some)


def rows_product(pairs):
    acc = None
    for a, b in pairs:
        t = dg(a, b, 0, 0)
        acc = t if acc is None else acc + t
    return acc


def mlp_weights_kernel(m, halves, *refs):
    acts = refs[: 2 * halves]
    gates = refs[2 * halves : 4 * halves]
    refs = refs[4 * halves :]
    norms = refs[:2]
    go_ref, gp_ref = refs[2:4]
    refs = refs[4:]
    outs = refs[-2 * halves :]
    before = refs[: -2 * halves]
    gs = [go_ref[m], gp_ref[m]]
    for k in range(halves):
        pj = rows_product([(a[...], g) for a, g in zip(acts[2 * k : 2 * k + 2], gs)])
        fc = rows_product([(a[...], b[...]) for a, b in zip(norms, gates[2 * k : 2 * k + 2])])
        for o_ref, v, prev in zip(outs[2 * k : 2 * k + 2], (pj, fc), before[2 * k : 2 * k + 2] or (None, None)):
            o_ref[...] = (v if prev is None else v + prev[...]).astype(o_ref.dtype)


def attend_weights_kernel(count, *refs):
    n = 2 * count
    dqs = refs[:n]
    norms = refs[n : 2 * n]
    mixes = refs[2 * n : 3 * n]
    brs = refs[3 * n : 4 * n]
    dkvs = refs[4 * n : 4 * n + count]
    outs = refs[4 * n + count :]
    c = lax.axis_index("tensor") & 1
    rows, wide = dqs[0].shape
    hc = wide // 2
    ns = [r[...] for r in norms]
    full = [jnp.concatenate(ns[2 * m : 2 * m + 2], axis=0) for m in range(count)]
    pieces = [
        rows_product([(a[...], b) for a, b in zip(dqs, ns)]),
        rows_product([(a[:, :wide], b) for a, b in zip(dkvs, full)]),
        rows_product([(a[:, wide:], b) for a, b in zip(dkvs, full)]),
        rows_product([(a[...], b[...]) for a, b in zip(mixes, brs)]),
    ]
    for i, p in enumerate(pieces):
        own_ref, send_ref = outs[2 * (i // 2) : 2 * (i // 2) + 2]
        at = slice((i % 2) * hc, (i % 2 + 1) * hc)
        low = p[:hc]
        high = p[hc:]
        own_ref[at, :] = jnp.where(c == 0, low, high)
        send_ref[at, :] = jnp.where(c == 0, high, low).astype(BF)


def by_rows(total, body):
    size = 48 if total % 48 == 0 else 64 if total % 64 == 0 else total
    if size == total:
        body(0, total)
        return

    def some(i, carry):
        body(pl.multiple_of(i * size, 16), size)
        return carry

    lax.fori_loop(0, total // size, some, 0)


def add_kernel(rcv_ref, own_ref, out_ref):
    def some(i, size):
        at = pl.ds(i, size)
        out_ref[at, :] = (own_ref[at, :].astype(F32) + rcv_ref[at, :].astype(F32)).astype(out_ref.dtype)

    by_rows(out_ref.shape[0], some)


def halve_kernel(bit, rcv_ref, own_ref, keep_ref, send_ref):
    r = keep_ref.shape[0]
    b = (lax.axis_index("dp") >> bit) & 1

    def some(i, size):
        at = pl.ds(i, size)
        mine = pl.ds(pl.multiple_of(b * r + i, 16), size)
        other = pl.ds(pl.multiple_of((1 - b) * r + i, 16), size)
        send_ref[at, :] = (own_ref[other, :].astype(F32) + rcv_ref[other, :].astype(F32)).astype(BF)
        keep_ref[at, :] = own_ref[mine, :].astype(F32) + rcv_ref[mine, :].astype(F32)

    by_rows(r, some)


def join_kernel(bit, rcv_ref, own_ref, out_ref):
    r = own_ref.shape[0]
    b = (lax.axis_index("dp") >> bit) & 1

    def some(i, size):
        at = pl.ds(i, size)
        mine = pl.ds(pl.multiple_of(b * r + i, 16), size)
        other = pl.ds(pl.multiple_of((1 - b) * r + i, 16), size)
        out_ref[mine, :] = own_ref[at, :].astype(out_ref.dtype)
        out_ref[other, :] = rcv_ref[at, :].astype(out_ref.dtype)

    by_rows(r, some)


def join_both_kernel(bit, rcv_a, own_a, rcv_b, own_b, qkv_ref, out_ref):
    r = own_a.shape[0]
    b = (lax.axis_index("dp") >> bit) & 1

    def some(i, size):
        at = pl.ds(i, size)
        qkv_ref[pl.ds(pl.multiple_of(b * r + i, 16), size), :] = own_a[at, :].astype(F32)
        qkv_ref[pl.ds(pl.multiple_of((1 - b) * r + i, 16), size), :] = rcv_a[at, :].astype(F32)
        own = own_b[at, :].astype(F32)
        rcv = rcv_b[at, :].astype(F32)
        qkv_ref[pl.ds(pl.multiple_of(2 * r + i, 16), size), :] = jnp.where(b == 0, own, rcv)
        out_ref[at, :] = jnp.where(b == 0, rcv, own)

    by_rows(r, some)


def stats_kernel(count, *refs):
    lst2 = refs[:count]
    fsums = refs[count : 3 * count]
    q_ref, lst1_ref, own_ref, send_ref = refs[3 * count :]
    c = lax.axis_index("tensor") & 1
    common = lst1_ref[...]
    for r in lst2:
        common = common + r[...]
    f = fsums[0][...]
    for r in fsums[1:]:
        f = f + r[...]
    q = q_ref[...]
    wide = own_ref.shape[1]
    hc = q.shape[1] // 2
    qpad = jnp.zeros((1, wide - 2 * hc), F32)
    low = jnp.concatenate([q[0:1, :hc], q[1:2, :hc], qpad], axis=1)
    high = jnp.concatenate([q[0:1, hc:], q[1:2, hc:], qpad], axis=1)
    own_ref[...] = common
    send_ref[...] = common
    own_ref[6:7] = jnp.where(c == 0, low, high)
    send_ref[6:7] = jnp.where(c == 0, high, low)
    own_ref[7:8] = f[0:1]
    send_ref[7:8] = f[1:2]


def spread_kernel(rcv_ref, own_ref, fb_ref, qb_ref, *outs):
    at = lax.broadcasted_iota(jnp.int32, own_ref.shape, 0)
    total = own_ref[...] + jnp.where(at < 6, rcv_ref[...], 0.0)
    for i, o_ref in enumerate(outs):
        o_ref[...] = total[i : i + 1].reshape(o_ref.shape)
    hc = qb_ref.shape[1]
    qb_ref[0:1, :] = total[6:7, :hc]
    qb_ref[1:2, :] = total[6:7, hc : 2 * hc]
    fb_ref[...] = total[7:8, : fb_ref.shape[0]].reshape(fb_ref.shape)


def body(
    tokens, qkv_weight, qv_bias, out_weight, out_bias, ln1_gain, ln1_shift, fc_weight, fc_bias,
    proj_weight, proj_bias, ln2_gain, ln2_shift, seq_lengths, out_grad,
):
    batches, rows, width = tokens.shape
    hc = out_weight.shape[0]
    wide = 2 * hc
    units = fc_weight.shape[1]
    tsize = lax.axis_size("tensor")
    dsize = lax.axis_size("dp")
    bits = dsize.bit_length() - 1
    cpairs = [(i, i ^ 1) for i in range(tsize)]
    ypairs = [(i, i ^ 2) for i in range(tsize)]
    mb = range(batches)
    line = Line()

    def core(v):
        return lax.ppermute(v, "tensor", cpairs)

    def across(v):
        return lax.ppermute(v, "tensor", ypairs)

    def swap(v, b):
        return lax.ppermute(v, "dp", [(i, i ^ (1 << b)) for i in range(dsize)])

    def after(v, *deps):
        return lax.optimization_barrier((v,) + deps)[0]

    def kernel_of(f, *static):
        def kernel(*refs):
            f(*static, *refs)

        return kernel

    def halve(own, rcv, b, name, **kw):
        size = own.shape[0] // 2
        if size % 16:
            both = own.astype(F32) + rcv.astype(F32)
            both = both.reshape((2, size) + own.shape[1:])
            bit = (lax.axis_index("dp") >> b) & 1
            keep = lax.dynamic_index_in_dim(both, bit, 0, keepdims=False)
            return keep, lax.dynamic_index_in_dim(both, 1 - bit, 0, keepdims=False).astype(BF)
        shape = (size,) + own.shape[1:]
        return line(kernel_of(halve_kernel, b), "halve_" + name, [rcv, own], [sds(shape, F32), sds(shape, BF)], **kw)

    def join(piece, rcv, b, dtype, name, kind="join_"):
        size = piece.shape[0]
        if size % 16:
            low = ((lax.axis_index("dp") >> b) & 1) == 0
            return jnp.concatenate([jnp.where(low, piece, rcv), jnp.where(low, rcv, piece)], axis=0).astype(dtype)
        shape = (2 * size,) + piece.shape[1:]
        return line(kernel_of(join_kernel, b), kind + name, [rcv, piece], [sds(shape, dtype)])[0]

    class Sum:
        def __init__(self, own, rcv, name, turn=0):
            self.own, self.rcv, self.name, self.at = own, rcv, name, 0
            self.order = [(b + turn) % bits for b in range(bits)]

        def go(self, **kw):
            k = self.at
            self.at += 1
            if k > 2 * bits:
                return
            if k < bits:
                self.own, send = halve(self.own, self.rcv, self.order[k], self.name, **kw)
            elif k == bits:
                send = line(add_kernel, "last_" + self.name, [self.rcv, self.own], [sds(self.own.shape, BF)], **kw)[0]
                self.own = send
            else:
                b = self.order[2 * bits - k]
                final = k == 2 * bits
                kind = "final_" if final and self.name == "f" else "join_"
                send = join(self.own, self.rcv, b, F32 if final else BF, self.name, kind)
                self.own = send
            if k < 2 * bits:
                self.rcv = swap(send, self.order[k if k < bits else 2 * bits - 1 - k])

        def finish(self):
            while self.at <= 2 * bits:
                self.go()
            return self.own

    wq_o = jnp.transpose(qkv_weight, (1, 2, 0))
    wq_x = core(wq_o)
    wo_x = core(out_weight)

    packed = (8, max(units, width))
    *normed, small, vec = line(
        ln1_kernel, "ln1",
        [out_bias, ln1_gain, ln1_shift, proj_bias, ln2_gain, ln2_shift, fc_bias, qv_bias, tokens],
        [sds((rows, width), BF)] * batches + [sds(packed, F32), sds((8, width), F32)], far=9,
    )
    normed_p = [across(v) for v in normed]
    qb, fb, wo, wq = line(
        weights_kernel, "weights", [out_weight, wq_o, small, core(small), wo_x, wq_x],
        [sds((3, wide), F32), sds((2, units), F32), sds((wide, width), BF), sds((3, wide, width), BF)], far=2,
    )

    q = [[None, None] for _ in mb]
    kv = [[None, None] for _ in mb]

    def qkv(m, **kw):
        q[m][0], q[m][1], kv[m][0] = line(
            qkv_kernel, "qkv", [qb, wq, normed[m], normed_p[m]],
            [sds((rows, wide), BF)] * 2 + [sds((2 * rows, 2 * wide), BF)], **kw,
        )
        kv[m][1] = core(kv[m][0])

    mixed = [[None, None] for _ in mb]
    lse = [[None, None] for _ in mb]
    own = [None for _ in mb]
    rcv = [None for _ in mb]
    lse_rows = 8 * (wide // LANES)

    def attend(m, part, **kw):
        mixed[m][part], lse[m][part], term = line(
            kernel_of(attend_kernel, m, part), "attend", [seq_lengths] + kv[m] + [wo, q[m][part]],
            [sds((rows, wide), BF), sds((lse_rows, rows), F32), sds((rows, width), BF if part else F32)],
            n_smem=1, **kw,
        )
        if part:
            rcv[m] = across(term)
        else:
            own[m] = term

    hid = [None for _ in mb]
    n2 = [[None, None] for _ in mb]

    def mid(m, **kw):
        hid[m], n2[m][0] = line(
            kernel_of(mid_kernel, m), "mid", [own[m], rcv[m], vec, tokens],
            [sds((rows, width), F32), sds((rows, width), BF)], **kw,
        )
        n2[m][1] = across(n2[m][0])

    acts = [[None, None] for _ in mb]
    gates = [[None, None] for _ in mb]
    fsum = [[None, None] for _ in mb]
    nown = [None for _ in mb]
    nrcv = [None for _ in mb]

    def mlp(m, part, **kw):
        a_o, a_x, g_o, g_x, fsum[m][part], term = line(
            kernel_of(mlp_kernel, m), "mlp",
            [grads_p if part else out_grad, fc_weight, fc_x, fb, proj_weight, pj_x, n2[m][part]],
            [sds((rows, units), BF)] * 4 + [sds((2, units), F32), sds((rows, width), BF if part else F32)], **kw,
        )
        acts[m][part] = (a_o, a_x)
        gates[m][part] = (g_o, g_x)
        if part:
            nrcv[m] = across(term)
        else:
            nown[m] = term

    flat = [(m, part) for m in mb for part in range(2)]

    def mlp_weights(m, ks, before, dtype, name, **kw):
        args = [acts[m][i][k] for k in ks for i in range(2)] + [gates[m][i][k] for k in ks for i in range(2)]
        return line(
            kernel_of(mlp_weights_kernel, m, len(ks)), name, args + [n2[m][i] for i in range(2)] + [out_grad, grads_p] + before,
            [sds((units, width), dtype), sds((width, units), dtype)] * len(ks), **kw,
        )

    hg = [None for _ in mb]
    st2 = [None for _ in mb]
    br = [[None, None] for _ in mb]

    def ln2_back(m, **kw):
        hg[m], st2[m], br[m][0] = line(
            kernel_of(ln2_back_kernel, m), "ln2b", [hid[m], nown[m], nrcv[m], vec, out_grad],
            [sds((rows, width), F32), sds((8, width), F32), sds((rows, width), BF)], **kw,
        )
        br[m][1] = across(br[m][0])

    def proj(part, **kw):
        return line(
            kernel_of(proj_kernel, batches), "proj",
            [proj_weight, pj_x] + [acts[m][part][k] for m in mb for k in range(2)],
            [sds((batches, rows, width), BF if part else F32)], **kw,
        )[0]

    dq = [[None, None] for _ in mb]
    acc = [None for _ in mb]
    dkvo = [None for _ in mb]
    dkvr = [None for _ in mb]
    dkvs = [None for _ in mb]

    def attend_back(m, part, **kw):
        args = [seq_lengths] + kv[m] + [wo, mixed[m][part], lse[m][part], br[m][part]]
        scratch = [pltpu.VMEM((rows, wide), BF)]
        if part:
            dq[m][1], dkvo[m], send = line(
                kernel_of(attend_back_kernel, m, 1), "attendb", args + [acc[m], q[m][1]],
                [sds((rows, wide), BF), sds((2 * rows, 2 * wide), F32), sds((2 * rows, 2 * wide), BF)],
                n_smem=1, scratch=scratch, **kw,
            )
            dkvs[m] = send
        else:
            dq[m][0], acc[m] = line(
                kernel_of(attend_back_kernel, m, 0), "attendb", args + [q[m][0]],
                [sds((rows, wide), BF), sds((4 * rows, 2 * wide), F32)],
                n_smem=1, scratch=scratch, **kw,
            )

    def qkv_back(**kw):
        args = [wq]
        for m in mb:
            args += [dq[m][0], dq[m][1], dkvo[m], dkvr[m]]
        *res, qsum, rem = line(
            kernel_of(qkv_back_kernel, batches), "qkvb", args,
            [sds((2 * rows, 2 * wide), BF), sds((rows, width), F32)] * batches
            + [sds((2, wide), F32), sds((batches, rows, width), BF)], **kw,
        )
        return res[0::2], res[1::2], qsum, rem

    last = batches - 1
    qkv(0)
    fc_x = core(after(fc_weight, q[0][0]))
    pj_x = core(after(proj_weight, q[0][0]))
    grads_p = across(after(out_grad, q[0][0]))
    for m in mb[1:]:
        qkv(m)
    attend(0, 1)
    attend(1, 1)
    attend(0, 0, needs=[grads_p])
    attend(1, 0)
    mid(0)
    mlp(0, 0)
    mid(1)
    mlp(1, 0)
    mlp(0, 1)
    o_pj, o_fc, x_pj, x_fc = mlp_weights(0, (0, 1), [], F32, "mlpw0")
    mlp(1, 1)
    pj_send, fc_send = mlp_weights(1, (1,), [x_pj, x_fc], BF, "mlpwx")
    pj_own, fc_own = mlp_weights(1, (0,), [o_pj, o_fc], F32, "mlpwo")
    ln2_back(0)
    pown = proj(0)
    psend = proj(1)
    ln2_back(1)
    pj_back = core(pj_send)
    fc_back = core(fc_send)
    p_sum = Sum(pj_own, pj_back, "p")
    f_sum = Sum(fc_own, fc_back, "f")
    p_sum.go()
    attend_back(0, 0)
    attend_back(1, 0)
    f_sum.go(needs=[br[m][1] for m in mb])
    p_sum.go()
    prcv = across(after(psend, p_sum.own))
    attend_back(0, 1)
    p_sum.go()
    attend_back(1, 1)
    p_sum.go(needs=[prcv])
    f_sum.go()
    for m in mb:
        dkvr[m] = core(after(dkvs[m], f_sum.own))
    dkv, ngo, qsum, ngs = qkv_back()

    both = [normed, normed_p]
    a1_own, a1_send, a2_own, a2_send = line(
        kernel_of(attend_weights_kernel, batches), "attw",
        [dq[m][i] for m, i in flat] + [both[i][m] for m, i in flat] + [mixed[m][i] for m, i in flat]
        + [br[m][i] for m, i in flat] + dkv,
        [sds((2 * hc, width), F32), sds((2 * hc, width), BF)] * 2,
        limit=32,
    )
    ngr = across(after(ngs, a2_send))
    a_sum = Sum(a1_own, core(a1_send), "a")
    b_sum = Sum(a2_own, core(a2_send), "b")
    p_sum.go()
    f_sum.go()
    a_sum.go()
    b_sum.go()
    layer_out = line(
        kernel_of(out_kernel, batches), "out", [vec] + hid + [pown, prcv], [sds((batches, rows, width), BF)],
    )[0]
    p_sum.go()
    f_sum.go()
    a_sum.go()
    b_sum.go()
    a_sum.go()
    f_sum.go()
    ig, st1 = line(
        kernel_of(ln1_back_kernel, batches), "ln1b", [tokens, vec] + hg + ngo + [ngr],
        [sds((batches, rows, width), F32), sds((8, width), F32)],
    )
    b_sum.go()
    s_own, s_send = line(
        kernel_of(stats_kernel, batches), "stats",
        st2 + [fsum[m][i] for m, i in flat] + [qsum, st1],
        [sds((8, width), F32), sds((8, width), F32)],
    )
    s_rcv = core(s_send)
    a_sum.go()

    def stat():
        return line(add_kernel, "stat", [s_rcv, stats], [sds((8, width), F32)])[0]

    stats = s_own
    stats = stat()
    s_rcv = swap(stats, 0)
    f_sum.go()
    p_sum.finish()
    b_sum.go()
    a_sum.go()
    for b in range(1, bits):
        stats = stat()
        s_rcv = swap(stats, b)
        for chain in (b_sum, a_sum):
            if chain.at < 2 * bits:
                chain.go()
    stats = stat()
    s_rcv = across(stats)
    for chain in (a_sum, b_sum):
        while chain.at < 2 * bits:
            chain.go()
    f_sum.finish()
    vector = sds((width,), F32)
    fb_grad, qb_grad, *vectors = line(
        spread_kernel, "spread", [s_rcv, stats],
        [sds((units,), F32), sds((2, hc), F32)] + [vector] * 6,
    )
    qkv_grad, out_grad_w = line(
        kernel_of(join_both_kernel, a_sum.order[0]), "join_ab", [a_sum.rcv, a_sum.own, b_sum.rcv, b_sum.own],
        [sds((3 * hc, width), F32), sds((hc, width), F32)],
    )
    fc_grad = f_sum.own
    pj_grad = p_sum.own

    return (
        layer_out,
        ig,
        jnp.transpose(qkv_grad.reshape(3, hc, width), (2, 0, 1)),
        qb_grad,
        out_grad_w,
        vectors[4],
        vectors[0],
        vectors[1],
        fc_grad,
        fb_grad,
        pj_grad,
        vectors[5],
        vectors[2],
        vectors[3],
    )


def solution(mesh):
    placed = (
        P(None, ("dp", "tensor"), None),
        P(None, None, "tensor"),
        P(None, "tensor"),
        P("tensor", None),
        P(),
        P(),
        P(),
        P(None, "tensor"),
        P("tensor"),
        P("tensor", None),
        P(),
        P(),
        P(),
        P(None, "dp"),
        P(None, ("dp", "tensor"), None),
    )
    return jax.shard_map(
        body,
        mesh=mesh,
        in_specs=placed,
        out_specs=(
            P(None, ("dp", "tensor"), None),
            P(None, ("dp", "tensor"), None),
            P(None, None, "tensor"),
            P(None, "tensor"),
            P("tensor", None),
            P(),
            P(),
            P(),
            P(None, "tensor"),
            P("tensor"),
            P("tensor", None),
            P(),
            P(),
            P(),
        ),
        check_vma=False,
    )
```

```python
import math

import jax
import jax.numpy as jnp
from jax import lax
from jax.experimental import pallas as pl
from jax.experimental.pallas import tpu as pltpu
from jax.sharding import PartitionSpec as P

HD = 64
LANES = 128
LOG2E = 1.4426950408889634
NEG = -1e30
EPS = 1e-05
BF = jnp.bfloat16
F32 = jnp.float32
VM = pl.BlockSpec(memory_space=pltpu.VMEM)
SM = pl.BlockSpec(memory_space=pltpu.SMEM)
HB = pl.BlockSpec(memory_space=pltpu.HBM)


def dg(a, b, ca, cb):
    return lax.dot_general(a, b, (((ca,), (cb,)), ((), ())), preferred_element_type=F32)


def sds(shape, dtype):
    return jax.ShapeDtypeStruct(tuple(shape), dtype)


TIMES = dict(
    ln1=2.0, weights=1.4, qkv=2.3, attend=5.2, mid=0.4, mlp=4.0, mlpw0=4.0, mlpwx=2.2, mlpwo=2.2, ln2b=27.0, proj=1.4,
    attendb=7.0, qkvb=2.8, attw=2.7, ln1b=2.4, out=1.1, halve=10.0, last=10.0, join=10.0,
)
SCALE = 0.3


class Line:
    def __init__(self):
        self.last = None

    def __call__(self, kernel, name, args, outs, n_smem=0, scratch=(), limit=24, far=0, needs=()):
        args = list(args)
        after = list(needs)
        if self.last is not None:
            after.append(self.last)
        if after:
            args[-1] = lax.optimization_barrier(tuple([args[-1]] + after))[0]
        for i in range(n_smem, n_smem + far):
            args[i] = pltpu.with_memory_space_constraint(args[i], pltpu.HBM)
        fetched = args[n_smem : n_smem + far]
        total = len(args)

        def run(*refs):
            if not far:
                return kernel(*refs)
            body_refs = refs[: len(refs) - far - 1]
            bufs = refs[len(refs) - far - 1 : -1]
            sems = refs[-1]
            copies = [
                pltpu.make_async_copy(refs[n_smem + i], bufs[i], sems.at[i]) for i in range(far)
            ]
            for cp in copies:
                cp.start()
            for cp in copies:
                cp.wait()
            return kernel(*body_refs[:n_smem], *bufs, *body_refs[n_smem + far :])

        extra = []
        if far:
            extra = [pltpu.VMEM(v.shape, v.dtype) for v in fetched] + [pltpu.SemaphoreType.DMA((far,))]
        res = pl.pallas_call(
            run,
            in_specs=[SM] * n_smem + [HB] * far + [VM] * (total - n_smem - far),
            out_specs=[VM] * len(outs),
            out_shape=outs,
            scratch_shapes=list(scratch) + extra,
            compiler_params=pltpu.CompilerParams(vmem_limit_bytes=limit << 20),
            cost_estimate=pl.CostEstimate(
                flops=int(SCALE * 1.1e9 * TIMES.get(name.split("_")[0], 0.2)), transcendentals=0, bytes_accessed=1
            ),
            name=name,
        )(*args)
        self.last = res[-1]
        return res


def normalize(x):
    d = x.shape[-1]
    xc = x - jnp.sum(x, axis=-1, keepdims=True) * (1.0 / d)
    var = jnp.sum(xc * xc, axis=-1, keepdims=True) * (1.0 / d)
    r = lax.rsqrt(var + EPS)
    return xc * r, r


def norm_back(grad, z, r, gain):
    d = z.shape[-1]
    e = grad * gain
    me = jnp.sum(e, axis=-1, keepdims=True) * (1.0 / d)
    mez = jnp.sum(e * z, axis=-1, keepdims=True) * (1.0 / d)
    return (e - me - z * mez) * r


def chunked(total, size, body, carry=None):
    if total % size:
        return body(pl.ds(0, total), carry)
    return lax.fori_loop(0, total // size, lambda i, c: body(pl.ds(pl.multiple_of(i * size, size), size), c), carry)


def col_sum(x):
    return jnp.sum(x.astype(F32), axis=0, keepdims=True)


def ln1_kernel(*refs):
    vecs = refs[:6]
    fb_ref, qb_ref, tok_ref = refs[6:9]
    outs = refs[9:-2]
    small_ref, vec_ref = refs[-2:]
    vec_ref[...] = jnp.zeros(vec_ref.shape, F32)
    for i, v in enumerate(vecs):
        vec_ref[i : i + 1, :] = v[...].astype(F32).reshape(1, -1)
    for m, o_ref in enumerate(outs):
        z, _ = normalize(tok_ref[m].astype(F32))
        o_ref[...] = (z * vec_ref[1:2] + vec_ref[2:3]).astype(BF)
    small_ref[...] = jnp.zeros(small_ref.shape, F32)
    small_ref[0:1, : fb_ref.shape[0]] = fb_ref[...].astype(F32).reshape(1, -1)
    small_ref[1:3, : qb_ref.shape[1]] = qb_ref[...].astype(F32)


def weights_kernel(woo_ref, wqo_ref, so_ref, sx_ref, wox_ref, wqx_ref, qb_ref, fb_ref, wo_ref, wq_ref):
    c = lax.axis_index("tensor") & 1
    hc = woo_ref.shape[0]
    units = fb_ref.shape[1]
    fb_ref[0:1, :] = so_ref[0:1, :units]
    fb_ref[1:2, :] = sx_ref[0:1, :units]
    qb_ref[...] = jnp.zeros(qb_ref.shape, F32)

    def place(at_o, at_x):
        for at, b, o, q in ((at_o, so_ref, woo_ref, wqo_ref), (at_x, sx_ref, wox_ref, wqx_ref)):
            qb_ref[0:1, at : at + hc] = b[1:2, :hc]
            qb_ref[2:3, at : at + hc] = b[2:3, :hc]
            wo_ref[at : at + hc, :] = o[...]
            wq_ref[:, at : at + hc, :] = q[...]

    @pl.when(c == 0)
    def _():
        place(0, hc)

    @pl.when(c != 0)
    def _():
        place(hc, 0)


def qkv_kernel(b_ref, w_ref, no_ref, np_ref, qo_ref, qp_ref, kv_ref):
    rows, wide = qo_ref.shape
    for i, (n_ref, q_ref) in enumerate(((no_ref, qo_ref), (np_ref, qp_ref))):
        n = n_ref[...]
        for s in range(3):
            v = (dg(n, w_ref[s], 1, 1) + b_ref[s : s + 1]).astype(BF)
            if s == 0:
                q_ref[...] = v
            else:
                kv_ref[i * rows : (i + 1) * rows, wide * (s - 1) : wide * s] = v


def row_starts(rows):
    t = lax.axis_index("tensor")
    return [rows * t, rows * (t ^ 2), rows * (t ^ 1), rows * (t ^ 3)]


def key_bias(starts, length, rows):
    out = []
    for b in range(4):
        at = lax.broadcasted_iota(jnp.int32, (rows, LANES), 0) + starts[b]
        out.append(jnp.where(at < length, 0.0, NEG).astype(BF))
    return jnp.concatenate(out, axis=0)


def attend_kernel(m, part, len_ref, ka_ref, kb_ref, w_ref, q_ref, mixed_ref, lse_ref, term_ref):
    rows, wide = q_ref.shape
    length = len_ref[m, 0]
    starts = row_starts(rows)
    c = LOG2E / math.sqrt(HD)
    bias = key_bias(starts, length, rows)
    lane = lax.broadcasted_iota(jnp.int32, (4 * rows, LANES), 1)
    laneq = lax.broadcasted_iota(jnp.int32, (rows, LANES), 1)
    valid = lax.broadcasted_iota(jnp.int32, (rows, LANES), 0) + starts[part] < length
    kvs = (ka_ref, kb_ref)

    def head(at, carry):
        p = at >> 1
        h = at & 1
        cs = pl.ds(pl.multiple_of(LANES * p, LANES), LANES)
        vs = pl.ds(pl.multiple_of(wide + LANES * p, LANES), LANES)
        kp = jnp.concatenate([r[:, cs] for r in kvs], axis=0)
        vp = jnp.concatenate([r[:, vs] for r in kvs], axis=0)
        inh = (laneq // HD) == h
        mark = HD * (1 - h)
        one = jnp.where(laneq == mark, 1.0, 0.0).astype(BF)
        s = dg(jnp.where(inh, q_ref[:, cs], one), jnp.where(lane == mark, bias, kp), 1, 1)
        top = jnp.max(s, axis=1, keepdims=True)
        e = jnp.exp2((s - top) * c)
        l = jnp.sum(e, axis=1, keepdims=True)
        o = dg(e.astype(BF), vp, 1, 0) * (1.0 / l)
        lt = jnp.broadcast_to(top * c + jnp.log2(l), o.shape).T
        lse_ref[pl.ds(8 * p + h, 1), :] = lt[0:1]
        mixed_ref[:, cs] = jnp.where(inh, jnp.where(valid, o, 0.0).astype(BF), mixed_ref[:, cs])
        return carry

    lax.fori_loop(0, wide // HD, head, 0)
    term_ref[...] = dg(mixed_ref[...], w_ref[...], 1, 0).astype(term_ref.dtype)


def mid_kernel(m, own_ref, rcv_ref, vec_ref, tok_ref, hid_ref, n_ref):
    h = tok_ref[m].astype(F32) + (own_ref[...] + rcv_ref[...].astype(F32)) + vec_ref[0:1]
    hid_ref[...] = h
    z, _ = normalize(h)
    n_ref[...] = (z * vec_ref[4:5] + vec_ref[5:6]).astype(BF)


def mlp_kernel(m, g_ref, fo_ref, fx_ref, bias_ref, po_ref, px_ref, n_ref, ao_ref, ax_ref, ggo_ref, ggx_ref, sum_ref, term_ref):
    n = n_ref[...]
    g = g_ref[m]
    back = None
    for j, (f_ref, p_ref, a_ref, gg_ref) in enumerate(
        ((fo_ref, po_ref, ao_ref, ggo_ref), (fx_ref, px_ref, ax_ref, ggx_ref))
    ):
        f = f_ref[...]
        gate = dg(n, f, 1, 0) + bias_ref[j : j + 1]
        q = 0.5 * jnp.tanh(0.851 * gate) + 0.5
        a_ref[...] = (gate * q).astype(BF)
        slope = q + 1.702 * gate * q * (1.0 - q)
        gg = (dg(g, p_ref[...], 1, 1) * slope).astype(BF)
        gg_ref[...] = gg
        term = dg(gg, f, 1, 1)
        back = term if back is None else back + term
        sum_ref[j : j + 1] = col_sum(gg)
    term_ref[...] = back.astype(term_ref.dtype)


def proj_kernel(count, po_ref, px_ref, *refs):
    out_ref = refs[-1]
    for m in range(count):
        out_ref[m] = (dg(refs[2 * m][...], po_ref[...], 1, 0) + dg(refs[2 * m + 1][...], px_ref[...], 1, 0)).astype(
            out_ref.dtype
        )


def ln2_back_kernel(m, hid_ref, own_ref, rcv_ref, vec_ref, grad_ref, hg_ref, st_ref, br_ref):
    st_ref[...] = jnp.zeros(st_ref.shape, F32)

    def some(at, carry):
        z, r = normalize(hid_ref[at, :])
        ng = own_ref[at, :] + rcv_ref[at, :].astype(F32)
        g = grad_ref[m, at, :].astype(F32)
        hg = g + norm_back(ng, z, r, vec_ref[4:5])
        hg_ref[at, :] = hg
        br = hg.astype(BF)
        br_ref[at, :] = br
        for i, v in enumerate((ng * z, ng, br, g)):
            st_ref[2 + i : 3 + i] = st_ref[2 + i : 3 + i] + col_sum(v)
        return carry

    chunked(br_ref.shape[0], 128, some, 0)


def attend_back_kernel(m, part, *refs):
    len_ref, ka_ref, kb_ref, w_ref, mixed_ref, lse_ref, b_ref = refs[:7]
    refs = refs[7:]
    if part:
        (acc_in, q_ref, dq_ref, out_ref, send_ref, do_ref) = refs
    else:
        (q_ref, dq_ref, acc_ref, do_ref) = refs
    rows, wide = q_ref.shape
    length = len_ref[m, 0]
    starts = row_starts(rows)
    c = LOG2E / math.sqrt(HD)
    sc = 1.0 / math.sqrt(HD)
    at = lax.broadcasted_iota(jnp.int32, (rows, wide), 0) + starts[part]
    do_ref[...] = jnp.where(at < length, dg(b_ref[...], w_ref[...], 1, 1), 0.0).astype(BF)
    bias = key_bias(starts, length, rows)
    laneq = lax.broadcasted_iota(jnp.int32, (rows, LANES), 1)
    zero = jnp.zeros((), BF)
    kvs = (ka_ref, kb_ref)
    blocks = 2 if part else 1
    size = 4 * rows // blocks
    lane = lax.broadcasted_iota(jnp.int32, (size, LANES), 1)

    def pair(p, carry):
        cs = pl.ds(pl.multiple_of(LANES * p, LANES), LANES)
        vs = pl.ds(pl.multiple_of(wide + LANES * p, LANES), LANES)
        qp = q_ref[:, cs]
        dop = do_ref[:, cs]
        prod = (dop.astype(F32) * mixed_ref[:, cs].astype(F32)).T
        dqt = [None, None]
        for j in range(blocks):
            mine = kvs if blocks == 1 else kvs[j : j + 1]
            kp = jnp.concatenate([r[:, cs] for r in mine], axis=0)
            vp = jnp.concatenate([r[:, vs] for r in mine], axis=0)
            bj = bias[size * j : size * (j + 1)]
            kt = kp.T
            dk = None
            dv = None
            for h in range(2):
                inh = (laneq < HD) if h == 0 else (laneq >= HD)
                mark = HD * (1 - h)
                qz = jnp.where(inh, qp, zero)
                qh = jnp.where(laneq == mark, jnp.ones((), BF), qz)
                doh = jnp.where(inh, dop, zero)
                st = dg(jnp.where(lane == mark, bj, kp), qh, 1, 1)
                pt = jnp.exp2(st * c - lse_ref[pl.ds(8 * p + h, 1), :])
                dpt = dg(vp, doh, 1, 1)
                row = jnp.sum(prod[HD * h : HD * (h + 1)], axis=0, keepdims=True)
                ds = (pt * (dpt - row)).astype(BF)
                dvh = dg(pt.astype(BF), doh, 1, 0)
                dkh = dg(ds, qz * jnp.asarray(sc, BF), 1, 0)
                t = dg(kt[HD * h : HD * (h + 1)], ds, 1, 0)
                dqt[h] = t if dqt[h] is None else dqt[h] + t
                dv = dvh if dv is None else dv + dvh
                dk = dkh if dk is None else dk + dkh
            if part:
                at = slice(size * j, size * (j + 1))
                dk = dk + acc_in[at, cs]
                dv = dv + acc_in[at, vs]
                o_ref = send_ref if j else out_ref
                o_ref[:, cs] = dk.astype(o_ref.dtype)
                o_ref[:, vs] = dv.astype(o_ref.dtype)
            else:
                acc_ref[:, cs] = dk
                acc_ref[:, vs] = dv
        dq_ref[:, cs] = (jnp.concatenate(dqt, axis=0).T * sc).astype(BF)
        return carry

    lax.fori_loop(0, wide // LANES, pair, 0)


def qkv_back_kernel(count, *refs):
    w_ref = refs[0]
    ins = refs[1 : 1 + 4 * count]
    outs = refs[1 + 4 * count :]
    ngr_ref = outs[-1]
    sum_ref = outs[-2]
    rows = ngr_ref.shape[1]
    sq = None
    sv = None
    for m in range(count):
        dqo_ref, dqp_ref, own_ref, rcv_ref = ins[4 * m : 4 * m + 4]
        dkv_ref, ngo_ref = outs[2 * m : 2 * m + 2]
        wide = dqo_ref.shape[1]
        for i, dq_ref in ((1, dqp_ref), (0, dqo_ref)):
            at = slice(i * rows, (i + 1) * rows)
            dkv = (own_ref[at, :] + rcv_ref[at, :].astype(F32)).astype(BF)
            dkv_ref[at, :] = dkv
            dq = dq_ref[...]
            ng = dg(dq, w_ref[0], 1, 0) + dg(dkv[:, :wide], w_ref[1], 1, 0) + dg(dkv[:, wide:], w_ref[2], 1, 0)
            if i:
                ngr_ref[m] = ng.astype(BF)
            else:
                ngo_ref[...] = ng
            cq = col_sum(dq)
            cv = col_sum(dkv[:, wide:])
            sq = cq if sq is None else sq + cq
            sv = cv if sv is None else sv + cv
    sum_ref[0:1] = sq
    sum_ref[1:2] = sv


def ln1_back_kernel(count, *refs):
    tok_ref = refs[0]
    vec_ref = refs[1]
    hgs = refs[2 : 2 + count]
    owns = refs[2 + count : 2 + 2 * count]
    rcv_ref, ig_ref, st_ref = refs[2 + 2 * count :]
    st_ref[...] = jnp.zeros(st_ref.shape, F32)
    for m in range(count):

        def some(at, carry, m=m):
            z, r = normalize(tok_ref[m, at, :].astype(F32))
            ng = owns[m][at, :] + rcv_ref[m, at, :].astype(F32)
            ig_ref[m, at, :] = hgs[m][at, :] + norm_back(ng, z, r, vec_ref[1:2])
            for i, v in enumerate((ng * z, ng)):
                st_ref[i : i + 1] = st_ref[i : i + 1] + col_sum(v)
            return carry

        chunked(tok_ref.shape[1], 128, some, 0)


def out_kernel(count, vec_ref, *refs):
    hids = refs[:count]
    own_ref, rcv_ref, o_ref = refs[count:]
    for m in range(count):

        def some(i, size, m=m):
            at = pl.ds(i, size)
            o_ref[m, at, :] = (
                hids[m][at, :] + (own_ref[m, at, :] + rcv_ref[m, at, :].astype(F32)) + vec_ref[3:4]
            ).astype(BF)

        by_rows(o_ref.shape[1], some)


def rows_product(pairs):
    acc = None
    for a, b in pairs:
        t = dg(a, b, 0, 0)
        acc = t if acc is None else acc + t
    return acc


def mlp_weights_kernel(m, halves, *refs):
    acts = refs[: 2 * halves]
    gates = refs[2 * halves : 4 * halves]
    refs = refs[4 * halves :]
    norms = refs[:2]
    go_ref, gp_ref = refs[2:4]
    refs = refs[4:]
    outs = refs[-2 * halves :]
    before = refs[: -2 * halves]
    gs = [go_ref[m], gp_ref[m]]
    for k in range(halves):
        pj = rows_product([(a[...], g) for a, g in zip(acts[2 * k : 2 * k + 2], gs)])
        fc = rows_product([(a[...], b[...]) for a, b in zip(norms, gates[2 * k : 2 * k + 2])])
        for o_ref, v, prev in zip(outs[2 * k : 2 * k + 2], (pj, fc), before[2 * k : 2 * k + 2] or (None, None)):
            o_ref[...] = (v if prev is None else v + prev[...]).astype(o_ref.dtype)


def attend_weights_kernel(count, *refs):
    n = 2 * count
    dqs = refs[:n]
    norms = refs[n : 2 * n]
    mixes = refs[2 * n : 3 * n]
    brs = refs[3 * n : 4 * n]
    dkvs = refs[4 * n : 4 * n + count]
    outs = refs[4 * n + count :]
    c = lax.axis_index("tensor") & 1
    rows, wide = dqs[0].shape
    hc = wide // 2
    ns = [r[...] for r in norms]
    full = [jnp.concatenate(ns[2 * m : 2 * m + 2], axis=0) for m in range(count)]
    pieces = [
        rows_product([(a[...], b) for a, b in zip(dqs, ns)]),
        rows_product([(a[:, :wide], b) for a, b in zip(dkvs, full)]),
        rows_product([(a[:, wide:], b) for a, b in zip(dkvs, full)]),
        rows_product([(a[...], b[...]) for a, b in zip(mixes, brs)]),
    ]
    for i, p in enumerate(pieces):
        own_ref, send_ref = outs[2 * (i // 2) : 2 * (i // 2) + 2]
        at = slice((i % 2) * hc, (i % 2 + 1) * hc)
        low = p[:hc]
        high = p[hc:]
        own_ref[at, :] = jnp.where(c == 0, low, high)
        send_ref[at, :] = jnp.where(c == 0, high, low).astype(BF)


def by_rows(total, body):
    size = 48 if total % 48 == 0 else 64 if total % 64 == 0 else total
    if size == total:
        body(0, total)
        return

    def some(i, carry):
        body(pl.multiple_of(i * size, 16), size)
        return carry

    lax.fori_loop(0, total // size, some, 0)


def add_kernel(rcv_ref, own_ref, out_ref):
    def some(i, size):
        at = pl.ds(i, size)
        out_ref[at, :] = (own_ref[at, :].astype(F32) + rcv_ref[at, :].astype(F32)).astype(out_ref.dtype)

    by_rows(out_ref.shape[0], some)


def halve_kernel(bit, rcv_ref, own_ref, keep_ref, send_ref):
    r = keep_ref.shape[0]
    b = (lax.axis_index("dp") >> bit) & 1

    def some(i, size):
        at = pl.ds(i, size)
        mine = pl.ds(pl.multiple_of(b * r + i, 16), size)
        other = pl.ds(pl.multiple_of((1 - b) * r + i, 16), size)
        send_ref[at, :] = (own_ref[other, :].astype(F32) + rcv_ref[other, :].astype(F32)).astype(BF)
        keep_ref[at, :] = own_ref[mine, :].astype(F32) + rcv_ref[mine, :].astype(F32)

    by_rows(r, some)


def join_kernel(bit, rcv_ref, own_ref, out_ref):
    r = own_ref.shape[0]
    b = (lax.axis_index("dp") >> bit) & 1

    def some(i, size):
        at = pl.ds(i, size)
        mine = pl.ds(pl.multiple_of(b * r + i, 16), size)
        other = pl.ds(pl.multiple_of((1 - b) * r + i, 16), size)
        out_ref[mine, :] = own_ref[at, :].astype(out_ref.dtype)
        out_ref[other, :] = rcv_ref[at, :].astype(out_ref.dtype)

    by_rows(r, some)


def join_both_kernel(bit, rcv_a, own_a, rcv_b, own_b, qkv_ref, out_ref):
    r = own_a.shape[0]
    b = (lax.axis_index("dp") >> bit) & 1

    def some(i, size):
        at = pl.ds(i, size)
        qkv_ref[pl.ds(pl.multiple_of(b * r + i, 16), size), :] = own_a[at, :].astype(F32)
        qkv_ref[pl.ds(pl.multiple_of((1 - b) * r + i, 16), size), :] = rcv_a[at, :].astype(F32)
        own = own_b[at, :].astype(F32)
        rcv = rcv_b[at, :].astype(F32)
        qkv_ref[pl.ds(pl.multiple_of(2 * r + i, 16), size), :] = jnp.where(b == 0, own, rcv)
        out_ref[at, :] = jnp.where(b == 0, rcv, own)

    by_rows(r, some)


def stats_kernel(count, *refs):
    lst2 = refs[:count]
    fsums = refs[count : 3 * count]
    q_ref, lst1_ref, own_ref, send_ref = refs[3 * count :]
    c = lax.axis_index("tensor") & 1
    common = lst1_ref[...]
    for r in lst2:
        common = common + r[...]
    f = fsums[0][...]
    for r in fsums[1:]:
        f = f + r[...]
    q = q_ref[...]
    wide = own_ref.shape[1]
    hc = q.shape[1] // 2
    qpad = jnp.zeros((1, wide - 2 * hc), F32)
    low = jnp.concatenate([q[0:1, :hc], q[1:2, :hc], qpad], axis=1)
    high = jnp.concatenate([q[0:1, hc:], q[1:2, hc:], qpad], axis=1)
    own_ref[...] = common
    send_ref[...] = common
    own_ref[6:7] = jnp.where(c == 0, low, high)
    send_ref[6:7] = jnp.where(c == 0, high, low)
    own_ref[7:8] = f[0:1]
    send_ref[7:8] = f[1:2]


def spread_kernel(rcv_ref, own_ref, fb_ref, qb_ref, *outs):
    at = lax.broadcasted_iota(jnp.int32, own_ref.shape, 0)
    total = own_ref[...] + jnp.where(at < 6, rcv_ref[...], 0.0)
    for i, o_ref in enumerate(outs):
        o_ref[...] = total[i : i + 1].reshape(o_ref.shape)
    hc = qb_ref.shape[1]
    qb_ref[0:1, :] = total[6:7, :hc]
    qb_ref[1:2, :] = total[6:7, hc : 2 * hc]
    fb_ref[...] = total[7:8, : fb_ref.shape[0]].reshape(fb_ref.shape)


def body(
    tokens, qkv_weight, qv_bias, out_weight, out_bias, ln1_gain, ln1_shift, fc_weight, fc_bias,
    proj_weight, proj_bias, ln2_gain, ln2_shift, seq_lengths, out_grad,
):
    batches, rows, width = tokens.shape
    hc = out_weight.shape[0]
    wide = 2 * hc
    units = fc_weight.shape[1]
    tsize = lax.axis_size("tensor")
    dsize = lax.axis_size("dp")
    bits = dsize.bit_length() - 1
    cpairs = [(i, i ^ 1) for i in range(tsize)]
    ypairs = [(i, i ^ 2) for i in range(tsize)]
    mb = range(batches)
    line = Line()

    def core(v):
        return lax.ppermute(v, "tensor", cpairs)

    def across(v):
        return lax.ppermute(v, "tensor", ypairs)

    def swap(v, b):
        return lax.ppermute(v, "dp", [(i, i ^ (1 << b)) for i in range(dsize)])

    def after(v, *deps):
        return lax.optimization_barrier((v,) + deps)[0]

    def kernel_of(f, *static):
        def kernel(*refs):
            f(*static, *refs)

        return kernel

    def halve(own, rcv, b, name, **kw):
        size = own.shape[0] // 2
        if size % 16:
            both = own.astype(F32) + rcv.astype(F32)
            both = both.reshape((2, size) + own.shape[1:])
            bit = (lax.axis_index("dp") >> b) & 1
            keep = lax.dynamic_index_in_dim(both, bit, 0, keepdims=False)
            return keep, lax.dynamic_index_in_dim(both, 1 - bit, 0, keepdims=False).astype(BF)
        shape = (size,) + own.shape[1:]
        return line(kernel_of(halve_kernel, b), "halve_" + name, [rcv, own], [sds(shape, F32), sds(shape, BF)], **kw)

    def join(piece, rcv, b, dtype, name, kind="join_"):
        size = piece.shape[0]
        if size % 16:
            low = ((lax.axis_index("dp") >> b) & 1) == 0
            return jnp.concatenate([jnp.where(low, piece, rcv), jnp.where(low, rcv, piece)], axis=0).astype(dtype)
        shape = (2 * size,) + piece.shape[1:]
        return line(kernel_of(join_kernel, b), kind + name, [rcv, piece], [sds(shape, dtype)])[0]

    class Sum:
        def __init__(self, own, rcv, name, turn=0):
            self.own, self.rcv, self.name, self.at = own, rcv, name, 0
            self.order = [(b + turn) % bits for b in range(bits)]

        def go(self, **kw):
            k = self.at
            self.at += 1
            if k > 2 * bits:
                return
            if k < bits:
                self.own, send = halve(self.own, self.rcv, self.order[k], self.name, **kw)
            elif k == bits:
                send = line(add_kernel, "last_" + self.name, [self.rcv, self.own], [sds(self.own.shape, BF)], **kw)[0]
                self.own = send
            else:
                b = self.order[2 * bits - k]
                final = k == 2 * bits
                kind = "final_" if final and self.name == "f" else "join_"
                send = join(self.own, self.rcv, b, F32 if final else BF, self.name, kind)
                self.own = send
            if k < 2 * bits:
                self.rcv = swap(send, self.order[k if k < bits else 2 * bits - 1 - k])

        def finish(self):
            while self.at <= 2 * bits:
                self.go()
            return self.own

    wq_o = jnp.transpose(qkv_weight, (1, 2, 0))
    wq_x = core(wq_o)
    wo_x = core(out_weight)

    packed = (8, max(units, width))
    *normed, small, vec = line(
        ln1_kernel, "ln1",
        [out_bias, ln1_gain, ln1_shift, proj_bias, ln2_gain, ln2_shift, fc_bias, qv_bias, tokens],
        [sds((rows, width), BF)] * batches + [sds(packed, F32), sds((8, width), F32)], far=9,
    )
    normed_p = [across(v) for v in normed]
    qb, fb, wo, wq = line(
        weights_kernel, "weights", [out_weight, wq_o, small, core(small), wo_x, wq_x],
        [sds((3, wide), F32), sds((2, units), F32), sds((wide, width), BF), sds((3, wide, width), BF)], far=2,
    )

    q = [[None, None] for _ in mb]
    kv = [[None, None] for _ in mb]

    def qkv(m, **kw):
        q[m][0], q[m][1], kv[m][0] = line(
            qkv_kernel, "qkv", [qb, wq, normed[m], normed_p[m]],
            [sds((rows, wide), BF)] * 2 + [sds((2 * rows, 2 * wide), BF)], **kw,
        )
        kv[m][1] = core(kv[m][0])

    mixed = [[None, None] for _ in mb]
    lse = [[None, None] for _ in mb]
    own = [None for _ in mb]
    rcv = [None for _ in mb]
    lse_rows = 8 * (wide // LANES)

    def attend(m, part, **kw):
        mixed[m][part], lse[m][part], term = line(
            kernel_of(attend_kernel, m, part), "attend", [seq_lengths] + kv[m] + [wo, q[m][part]],
            [sds((rows, wide), BF), sds((lse_rows, rows), F32), sds((rows, width), BF if part else F32)],
            n_smem=1, **kw,
        )
        if part:
            rcv[m] = across(term)
        else:
            own[m] = term

    hid = [None for _ in mb]
    n2 = [[None, None] for _ in mb]

    def mid(m, **kw):
        hid[m], n2[m][0] = line(
            kernel_of(mid_kernel, m), "mid", [own[m], rcv[m], vec, tokens],
            [sds((rows, width), F32), sds((rows, width), BF)], **kw,
        )
        n2[m][1] = across(n2[m][0])

    acts = [[None, None] for _ in mb]
    gates = [[None, None] for _ in mb]
    fsum = [[None, None] for _ in mb]
    nown = [None for _ in mb]
    nrcv = [None for _ in mb]

    def mlp(m, part, **kw):
        a_o, a_x, g_o, g_x, fsum[m][part], term = line(
            kernel_of(mlp_kernel, m), "mlp",
            [grads_p if part else out_grad, fc_weight, fc_x, fb, proj_weight, pj_x, n2[m][part]],
            [sds((rows, units), BF)] * 4 + [sds((2, units), F32), sds((rows, width), BF if part else F32)], **kw,
        )
        acts[m][part] = (a_o, a_x)
        gates[m][part] = (g_o, g_x)
        if part:
            nrcv[m] = across(term)
        else:
            nown[m] = term

    flat = [(m, part) for m in mb for part in range(2)]

    def mlp_weights(m, ks, before, dtype, name, **kw):
        args = [acts[m][i][k] for k in ks for i in range(2)] + [gates[m][i][k] for k in ks for i in range(2)]
        return line(
            kernel_of(mlp_weights_kernel, m, len(ks)), name, args + [n2[m][i] for i in range(2)] + [out_grad, grads_p] + before,
            [sds((units, width), dtype), sds((width, units), dtype)] * len(ks), **kw,
        )

    hg = [None for _ in mb]
    st2 = [None for _ in mb]
    br = [[None, None] for _ in mb]

    def ln2_back(m, **kw):
        hg[m], st2[m], br[m][0] = line(
            kernel_of(ln2_back_kernel, m), "ln2b", [hid[m], nown[m], nrcv[m], vec, out_grad],
            [sds((rows, width), F32), sds((8, width), F32), sds((rows, width), BF)], **kw,
        )
        br[m][1] = across(br[m][0])

    def proj(part, **kw):
        return line(
            kernel_of(proj_kernel, batches), "proj",
            [proj_weight, pj_x] + [acts[m][part][k] for m in mb for k in range(2)],
            [sds((batches, rows, width), BF if part else F32)], **kw,
        )[0]

    dq = [[None, None] for _ in mb]
    acc = [None for _ in mb]
    dkvo = [None for _ in mb]
    dkvr = [None for _ in mb]
    dkvs = [None for _ in mb]

    def attend_back(m, part, **kw):
        args = [seq_lengths] + kv[m] + [wo, mixed[m][part], lse[m][part], br[m][part]]
        scratch = [pltpu.VMEM((rows, wide), BF)]
        if part:
            dq[m][1], dkvo[m], send = line(
                kernel_of(attend_back_kernel, m, 1), "attendb", args + [acc[m], q[m][1]],
                [sds((rows, wide), BF), sds((2 * rows, 2 * wide), F32), sds((2 * rows, 2 * wide), BF)],
                n_smem=1, scratch=scratch, **kw,
            )
            dkvs[m] = send
        else:
            dq[m][0], acc[m] = line(
                kernel_of(attend_back_kernel, m, 0), "attendb", args + [q[m][0]],
                [sds((rows, wide), BF), sds((4 * rows, 2 * wide), F32)],
                n_smem=1, scratch=scratch, **kw,
            )

    def qkv_back(**kw):
        args = [wq]
        for m in mb:
            args += [dq[m][0], dq[m][1], dkvo[m], dkvr[m]]
        *res, qsum, rem = line(
            kernel_of(qkv_back_kernel, batches), "qkvb", args,
            [sds((2 * rows, 2 * wide), BF), sds((rows, width), F32)] * batches
            + [sds((2, wide), F32), sds((batches, rows, width), BF)], **kw,
        )
        return res[0::2], res[1::2], qsum, rem

    last = batches - 1
    qkv(0)
    fc_x = core(after(fc_weight, q[0][0]))
    pj_x = core(after(proj_weight, q[0][0]))
    grads_p = across(after(out_grad, q[0][0]))
    for m in mb[1:]:
        qkv(m)
    attend(0, 1)
    attend(1, 1)
    attend(0, 0, needs=[grads_p])
    attend(1, 0)
    mid(0)
    mlp(0, 0)
    mid(1)
    mlp(1, 0)
    mlp(0, 1)
    o_pj, o_fc, x_pj, x_fc = mlp_weights(0, (0, 1), [], F32, "mlpw0")
    mlp(1, 1)
    pj_send, fc_send = mlp_weights(1, (1,), [x_pj, x_fc], BF, "mlpwx")
    pj_own, fc_own = mlp_weights(1, (0,), [o_pj, o_fc], F32, "mlpwo")
    ln2_back(0)
    pown = proj(0)
    psend = proj(1)
    ln2_back(1)
    pj_back = core(pj_send)
    fc_back = core(fc_send)
    p_sum = Sum(pj_own, pj_back, "p")
    f_sum = Sum(fc_own, fc_back, "f")
    p_sum.go()
    attend_back(0, 0)
    attend_back(1, 0)
    f_sum.go(needs=[br[m][1] for m in mb])
    p_sum.go()
    prcv = across(after(psend, p_sum.own))
    attend_back(0, 1)
    p_sum.go()
    attend_back(1, 1)
    p_sum.go(needs=[prcv])
    f_sum.go()
    for m in mb:
        dkvr[m] = core(after(dkvs[m], f_sum.own))
    dkv, ngo, qsum, ngs = qkv_back()

    both = [normed, normed_p]
    a1_own, a1_send, a2_own, a2_send = line(
        kernel_of(attend_weights_kernel, batches), "attw",
        [dq[m][i] for m, i in flat] + [both[i][m] for m, i in flat] + [mixed[m][i] for m, i in flat]
        + [br[m][i] for m, i in flat] + dkv,
        [sds((2 * hc, width), F32), sds((2 * hc, width), BF)] * 2,
        limit=32,
    )
    ngr = across(after(ngs, a2_send))
    a_sum = Sum(a1_own, core(a1_send), "a")
    b_sum = Sum(a2_own, core(a2_send), "b")
    p_sum.go()
    f_sum.go()
    a_sum.go()
    b_sum.go()
    layer_out = line(
        kernel_of(out_kernel, batches), "out", [vec] + hid + [pown, prcv], [sds((batches, rows, width), BF)],
    )[0]
    p_sum.go()
    f_sum.go()
    a_sum.go()
    b_sum.go()
    a_sum.go()
    f_sum.go()
    ig, st1 = line(
        kernel_of(ln1_back_kernel, batches), "ln1b", [tokens, vec] + hg + ngo + [ngr],
        [sds((batches, rows, width), F32), sds((8, width), F32)],
    )
    b_sum.go()
    s_own, s_send = line(
        kernel_of(stats_kernel, batches), "stats",
        st2 + [fsum[m][i] for m, i in flat] + [qsum, st1],
        [sds((8, width), F32), sds((8, width), F32)],
    )
    s_rcv = core(s_send)
    a_sum.go()

    def stat():
        return line(add_kernel, "stat", [s_rcv, stats], [sds((8, width), F32)])[0]

    stats = s_own
    stats = stat()
    s_rcv = swap(stats, 0)
    f_sum.go()
    p_sum.finish()
    b_sum.go()
    a_sum.go()
    for b in range(1, bits):
        stats = stat()
        s_rcv = swap(stats, b)
        for chain in (b_sum, a_sum):
            if chain.at < 2 * bits:
                chain.go()
    stats = stat()
    s_rcv = across(stats)
    for chain in (a_sum, b_sum):
        while chain.at < 2 * bits:
            chain.go()
    f_sum.finish()
    vector = sds((width,), F32)
    fb_grad, qb_grad, *vectors = line(
        spread_kernel, "spread", [s_rcv, stats],
        [sds((units,), F32), sds((2, hc), F32)] + [vector] * 6,
    )
    qkv_grad, out_grad_w = line(
        kernel_of(join_both_kernel, a_sum.order[0]), "join_ab", [a_sum.rcv, a_sum.own, b_sum.rcv, b_sum.own],
        [sds((3 * hc, width), F32), sds((hc, width), F32)],
    )
    fc_grad = f_sum.own
    pj_grad = p_sum.own

    return (
        layer_out,
        ig,
        jnp.transpose(qkv_grad.reshape(3, hc, width), (2, 0, 1)),
        qb_grad,
        out_grad_w,
        vectors[4],
        vectors[0],
        vectors[1],
        fc_grad,
        fb_grad,
        pj_grad,
        vectors[5],
        vectors[2],
        vectors[3],
    )


def solution(mesh):
    placed = (
        P(None, ("dp", "tensor"), None),
        P(None, None, "tensor"),
        P(None, "tensor"),
        P("tensor", None),
        P(),
        P(),
        P(),
        P(None, "tensor"),
        P("tensor"),
        P("tensor", None),
        P(),
        P(),
        P(),
        P(None, "dp"),
        P(None, ("dp", "tensor"), None),
    )
    return jax.shard_map(
        body,
        mesh=mesh,
        in_specs=placed,
        out_specs=(
            P(None, ("dp", "tensor"), None),
            P(None, ("dp", "tensor"), None),
            P(None, None, "tensor"),
            P(None, "tensor"),
            P("tensor", None),
            P(),
            P(),
            P(),
            P(None, "tensor"),
            P("tensor"),
            P("tensor", None),
            P(),
            P(),
            P(),
        ),
        check_vma=False,
    )
```
